32 devices in a mesh: ctx: 8 (over y, x, core), tp: 4 (over z).
Axes of the slice: x: 2, y: 2, z: 4, core: 2. Of those that a mesh axis runs over, the one named last changes fastest.
Arguments:
- query_rows: bfloat16 [4096, 4096], P('ctx', 'tp'), may hold values from -6 to 6
- key_rows: bfloat16 [4096, 4096], P('ctx', 'tp'), may hold values from -6 to 6
- value_rows: bfloat16 [4096, 4096], P('ctx', 'tp'), may hold values from -6 to 6
- short_weight: float32 [3, 3, 4096], P(None, None, 'tp'), may hold values from -3 to 3
- skip_gain: float32 [4096], P('tp'), may hold values from 0.5 to 1.5
- filter_taps: bfloat16 [4096, 4096], P('tp', 'ctx'), may hold values from 0 to 0.4
- out_weight: bfloat16 [4096, 4096], P('tp'), may hold values from -0.09375 to 0.09375
Outputs:
- layer_out: bfloat16 [4096, 4096], P('ctx', 'tp')
The draws below stay inside these ranges and needn't reach their ends.
All inputs are finite; a program needn't handle non-finite values.
Results may differ from the reference program's by a relative error of at most 0.017.
Values may be sent and summed in bfloat16 or wider, within the bound.
No kernel may reach another device: no remote copies, remote signals or barrier semaphores. Data moves between devices by JAX's collectives and lax.ppermute only.
A program may use at most 192 MiB of HBM per device.

```python
import jax
import jax.numpy as jnp
from jax import lax

MODEL_WIDTH = 4096
SEQUENCE_TOKENS = 4096
N_TP = 4


def draw_filter_taps(key, part):
    keys = jax.random.split(key, 6)
    share = 0.5
    slow = jax.random.uniform(keys[0], (MODEL_WIDTH, 1)) < share
    fast_tau = jnp.exp(jax.random.uniform(keys[1], (MODEL_WIDTH, 1), jnp.float32, jnp.log(30.0), jnp.log(50.0)))
    slow_tau = SEQUENCE_TOKENS * jnp.exp(jax.random.uniform(keys[2], (MODEL_WIDTH, 1), jnp.float32, jnp.log(2.0), jnp.log(8.0)))
    decay_length = jnp.where(slow, slow_tau, fast_tau)
    filter_amplitude = jnp.sqrt(2.0 / jnp.minimum(decay_length, 1.0 * SEQUENCE_TOKENS))
    time_position = jnp.arange(SEQUENCE_TOKENS).astype(jnp.float32)[None, :]
    position_grid = jax.random.randint(keys[3], (3, MODEL_WIDTH, 1), 1, SEQUENCE_TOKENS)
    error_terms = jnp.log(jax.random.uniform(keys[4], (3, MODEL_WIDTH, 1), jnp.float32, 0.6, 0.8))
    pulse_train = jnp.zeros((MODEL_WIDTH, SEQUENCE_TOKENS), jnp.float32)
    for token_index in range(3):
        pulse_train = pulse_train + jnp.where(time_position >= position_grid[token_index].astype(jnp.float32), error_terms[token_index], 0.0)
    noisy_signal = 0.5 + jax.random.uniform(keys[5], (MODEL_WIDTH, SEQUENCE_TOKENS), jnp.float32)
    value_entries = filter_amplitude * jnp.exp(-time_position / decay_length + pulse_train) * noisy_signal
    return value_entries.astype(jnp.bfloat16)


def shard_levels(rng, extent, cuts, smallest, high):
    def one(position, blocks):
        heights = jax.random.uniform(jax.random.fold_in(jax.random.fold_in(rng, 6), position), (blocks,), jnp.float32, smallest / len(cuts), high / len(cuts))
        return jnp.repeat(jnp.exp(heights), extent[position] // blocks).reshape((-1,) + (1,) * (len(extent) - position - 1))

    loudness = one(*cuts[0])
    for cut in cuts[1:]:
        loudness = loudness * one(*cut)
    return loudness


def bell_draw(own_key, extent, deviation, reach, cuts=(), kind=jnp.bfloat16):
    loudness = shard_levels(own_key, extent, cuts, -0.22, 0.18) if cuts else 1.0
    array = jax.random.normal(own_key, extent, jnp.float32) * deviation * loudness
    return jnp.minimum(jnp.maximum(array, -reach), reach).astype(kind)


def setup_inputs(seed: int = 0) -> dict:
    key_list = jax.random.split(jax.random.key(seed), 8)
    return {
        "query_rows": bell_draw(key_list[0], (SEQUENCE_TOKENS, MODEL_WIDTH), 1.0, 6.0, ((0, 8), (1, 4))),
        "key_rows": bell_draw(key_list[1], (SEQUENCE_TOKENS, MODEL_WIDTH), 1.0, 6.0, ((0, 8), (1, 4))),
        "value_rows": bell_draw(key_list[2], (SEQUENCE_TOKENS, MODEL_WIDTH), 1.0, 6.0, ((0, 8), (1, 4))),
        "short_weight": bell_draw(key_list[3], (3, 3, MODEL_WIDTH), 0.6, 3.0, ((2, 4),), jnp.float32),
        "skip_gain": jnp.clip(0.5 + 1.0 * jax.random.uniform(key_list[4], (MODEL_WIDTH,), jnp.float32) ** shard_levels(key_list[4], (MODEL_WIDTH,), ((0, 4),), -0.2, 0.2), 0.5, 1.5),
        "filter_taps": draw_filter_taps(jax.random.fold_in(key_list[7], 71), 0),
        "out_weight": bell_draw(key_list[6], (MODEL_WIDTH, MODEL_WIDTH), MODEL_WIDTH ** -0.5, 0.09375, ((0, 4),)),
    }


def short_mix(stream, taps):
    series = stream.astype(jnp.float32)
    first = jnp.pad(series, ((1, 0), (0, 0)))[:-1]
    second = jnp.pad(series, ((2, 0), (0, 0)))[:-2]
    return taps[0] * series + taps[1] * first + taps[2] * second


def reference(query_rows, key_rows, value_rows, short_weight, skip_gain, filter_taps, out_weight):
    mixed_q = short_mix(query_rows, short_weight[:, 0, :])
    mixed_k = short_mix(key_rows, short_weight[:, 1, :])
    mixed_v = short_mix(value_rows, short_weight[:, 2, :])
    gated_in = (mixed_k * mixed_v).astype(jnp.bfloat16)
    length = gated_in.shape[0]
    width = gated_in.shape[1]
    group = width // N_TP
    inputs_t = gated_in.astype(jnp.float32).T.reshape(N_TP, group, length)
    filters_t = filter_taps.astype(jnp.float32).reshape(N_TP, group, length)

    def convolve(pair):
        signal, taps = pair
        spectrum = jnp.fft.rfft(signal, n=2 * length, axis=1) * jnp.fft.rfft(taps, n=2 * length, axis=1)
        return jnp.fft.irfft(spectrum, n=2 * length, axis=1)[:, :length].astype(jnp.float32)

    long_part = lax.map(convolve, (inputs_t, filters_t)).reshape(width, length).T
    conv = (long_part + skip_gain[None, :] * gated_in.astype(jnp.float32)).astype(jnp.bfloat16)
    gated_out = (mixed_q * conv.astype(jnp.float32)).astype(jnp.bfloat16)
    gated_groups = jnp.transpose(gated_out.reshape(length, N_TP, group), (1, 0, 2))
    weight_groups = out_weight.reshape(N_TP, group, width)

    def accumulate(total, pair):
        rows, weights = pair
        partial_value = jnp.dot(rows, weights, preferred_element_type=jnp.float32).astype(jnp.bfloat16)
        return total + partial_value.astype(jnp.float32), None

    total, unused = lax.scan(accumulate, jnp.zeros((length, width), jnp.float32), (gated_groups, weight_groups))
    return total.astype(jnp.bfloat16)
```

```python
from functools import partial
import math

import jax
import jax.numpy as jnp
import numpy as np
from jax import lax
from jax.experimental import pallas as pl
from jax.experimental.pallas import tpu as pltpu
from jax.sharding import PartitionSpec as P

TRIPLE = lax.Precision.HIGH


def passed_along(block, axis, distance):
    devices = range(lax.axis_size(axis))
    route = [(i - distance, i) for i in devices if i - distance in devices]
    return lax.ppermute(block, axis, route)


def angle_table(left, right, offset, period):
    rows = lax.broadcasted_iota(jnp.int32, (left, right), 0)
    cols = lax.broadcasted_iota(jnp.int32, (left, right), 1) + offset
    turns = rows * cols % period
    return turns.astype(jnp.float32) * (2.0 * math.pi / period)


def inner_spectrum(rows, table_high, table_low):
    upper = jnp.dot(rows, table_high, preferred_element_type=jnp.float32)
    lower = jnp.dot(rows, table_low, preferred_element_type=jnp.float32)
    return upper + lower


def block_mix(real_component, imaginary_component, cosine_lookup, sine_lookup, sign):
    multiplier = partial(jnp.einsum, precision=TRIPLE, preferred_element_type=jnp.float32)
    cosine_real = multiplier("id,rdy->riy", cosine_lookup, real_component)
    cosine_imaginary = multiplier("id,rdy->riy", cosine_lookup, imaginary_component)
    sine_real = multiplier("id,rdy->riy", sine_lookup, real_component)
    sine_imaginary = multiplier("id,rdy->riy", sine_lookup, imaginary_component)
    return (cosine_real + sign * sine_imaginary, cosine_imaginary - sign * sine_real)


def general_per_device(query_rows, key_rows, value_rows, short_weight, skip_gain, filter_taps, out_weight):
    span = query_rows.shape[0]
    chans = query_rows.shape[1]
    blocks = lax.axis_size("ctx")
    group = chans // blocks
    period = 2 * span
    padded = 2 * blocks
    forward = angle_table(span, period, 0, period)
    forward = jnp.concatenate([jnp.cos(forward), -jnp.sin(forward)], axis=1)
    table_high = forward.astype(jnp.bfloat16)
    table_low = (forward - table_high.astype(jnp.float32)).astype(jnp.bfloat16)
    parity = 1.0 - 2.0 * (jnp.arange(period) % 2).astype(jnp.float32)
    parity = jnp.concatenate([parity, parity])
    stacked = jnp.stack([query_rows, key_rows, value_rows])
    rims = passed_along(stacked[:, -2:, :], "ctx", 1)
    extended = jnp.concatenate([rims, stacked], axis=1).astype(jnp.float32)
    mixed = (
        short_weight[0][:, None, :] * extended[:, 2:]
        + short_weight[1][:, None, :] * extended[:, 1:-1]
        + short_weight[2][:, None, :] * extended[:, :span]
    )
    gated_in = (mixed[1] * mixed[2]).astype(jnp.bfloat16)
    gated_t = gated_in.T
    inputs_local, taps_local = (
        lax.all_to_all(gated_t, "ctx", split_axis=0, concat_axis=1, tiled=True),
        lax.all_to_all(filter_taps, "ctx", split_axis=0, concat_axis=1, tiled=True),
    )
    spectra = inner_spectrum(
        taps_local.reshape(group * blocks, span), table_high, table_low
    ).reshape(group, blocks, 2 * period)
    earlier = jnp.concatenate(
        [jnp.zeros((group, 1, 2 * period), jnp.float32), spectra[:, :-1]], axis=1
    )
    kernel_spec = earlier + parity * spectra
    input_spec = inner_spectrum(
        inputs_local.reshape(group * blocks, span), table_high, table_low
    ).reshape(group, blocks, 2 * period)
    block_angle = angle_table(padded, blocks, 0, padded)
    cos_fwd = jnp.cos(block_angle)
    sin_fwd = jnp.sin(block_angle)
    input_re, input_im = block_mix(
        input_spec[..., :period], input_spec[..., period:], cos_fwd, sin_fwd, 1.0
    )
    kernel_re, kernel_im = block_mix(
        kernel_spec[..., :period], kernel_spec[..., period:], cos_fwd, sin_fwd, 1.0
    )
    product_re = input_re * kernel_re - input_im * kernel_im
    product_im = input_re * kernel_im + input_im * kernel_re
    back_angle = angle_table(blocks, padded, 0, padded)
    out_re, out_im = block_mix(
        product_re, product_im, jnp.cos(back_angle), jnp.sin(back_angle), -1.0
    )
    inverse = angle_table(period, span, span, period)
    inverse = jnp.concatenate([jnp.cos(inverse), -jnp.sin(inverse)], axis=0) * (
        1.0 / (period * padded)
    )
    joined = jnp.concatenate([out_re, out_im], axis=2).reshape(group * blocks, 2 * period)
    long_local = jnp.dot(
        joined, inverse, precision=TRIPLE, preferred_element_type=jnp.float32
    ).reshape(group, blocks * span)
    long_t = lax.all_to_all(
        long_local.astype(jnp.bfloat16), "ctx", split_axis=1, concat_axis=0, tiled=True
    ).astype(long_local.dtype)
    conv_t = (long_t + skip_gain[:, None] * gated_t.astype(jnp.float32)).astype(jnp.bfloat16)
    gated_out = (mixed[0].T * conv_t.astype(jnp.float32)).astype(jnp.bfloat16)
    term = lax.dot_general(
        gated_out, out_weight, (((0,), (0,)), ((), ())), preferred_element_type=jnp.float32
    )
    return lax.psum_scatter(term.astype(jnp.bfloat16), "tp", scatter_dimension=1, tiled=True)


SUB = 128
F32 = jnp.float32
BF16 = jnp.bfloat16


def split_table(matrix):
    high = matrix.astype(jnp.bfloat16)
    low = (matrix - high.astype(np.float32)).astype(jnp.bfloat16)
    return np.concatenate([high, high, low], axis=1)


def dft_tables(period):
    index = np.arange(SUB)
    turns = np.outer(index, index) % SUB * (2.0 * np.pi / SUB)
    cos, sin = np.cos(turns), np.sin(turns)
    forward = np.block([[cos, sin], [-sin, cos]]).astype(np.float32)
    inverse = (np.block([[cos, -sin], [sin, cos]]) / period).astype(np.float32)
    return split_table(forward), split_table(inverse)


def twiddle_table(radix):
    half = radix // 2
    turns = np.outer(np.arange(SUB), np.arange(half + 1)) * (2.0 * np.pi / (radix * SUB))
    return np.concatenate([np.cos(turns), -np.sin(turns)], axis=1).astype(np.float32)


def times(value, factor):
    return None if value is None else value * factor


def plus(left, right):
    if left is None:
        return right
    return left if right is None else left + right


def minus(left, right):
    if right is None:
        return left
    return -right if left is None else left - right


def rotate(value, turn):
    real, imag = value
    cos, sin = math.cos(2 * math.pi * turn), math.sin(2 * math.pi * turn)
    if abs(cos - sin) < 1e-12 and imag is not None:
        return (real + imag) * cos, (imag - real) * cos
    return plus(times(real, cos), times(imag, sin)), minus(times(imag, cos), times(real, sin))


def real_forward(values):
    points = 2 * len(values)
    if points == 2:
        return [(values[0], None), (values[0], None)]
    even, odd = real_forward(values[0::2]), real_forward(values[1::2])
    bins = [None] * (points // 2 + 1)
    bins[0] = (even[0][0] + odd[0][0], None)
    bins[points // 2] = (even[0][0] - odd[0][0], None)
    quarter = points // 4
    for k in range(1, quarter):
        turned = rotate(odd[k], k / points)
        bins[k] = (even[k][0] + turned[0], even[k][1] + turned[1])
        bins[points // 2 - k] = (even[k][0] - turned[0], turned[1] - even[k][1])
    bins[quarter] = (even[quarter][0], -odd[quarter][0])
    return bins


def real_inverse(bins):
    half = len(bins) - 1
    points = 2 * half
    if points == 2:
        return [bins[0][0] + bins[1][0]]
    even, odd = [], []
    for k in range(half // 2 + 1):
        ahead, back = bins[k], bins[half - k]
        if k == 0:
            even.append((ahead[0] + back[0], None))
            odd.append((ahead[0] - back[0], None))
        elif k == half // 2:
            even.append((ahead[0] * 2.0, None))
            odd.append((ahead[1] * -2.0, None))
        else:
            even.append((ahead[0] + back[0], ahead[1] - back[1]))
            difference = (ahead[0] - back[0], ahead[1] + back[1])
            odd.append(rotate(difference, -k / points))
    even, odd = real_inverse(even), real_inverse(odd)
    return [value for pair in zip(even, odd) for value in pair]


def split_dot(table, data):
    high = data.astype(BF16)
    low = (data - high.astype(F32)).astype(BF16)
    return jnp.dot(
        table[...], jnp.concatenate([high, low, high], axis=0), preferred_element_type=F32
    )


def first_stage(series, spectra, twiddle):
    half = series.shape[0] // SUB
    lanes = series.shape[1]

    def slab(step, carry):
        row = pl.multiple_of(step * 8, 8)
        values = [series[pl.ds(SUB * n + row, 8), :] for n in range(half)]
        factors = twiddle[pl.ds(row, 8), :]
        for k, (real, imag) in enumerate(real_forward(values)):
            if k == 0:
                spectra[0, pl.ds(row, 8), :] = real
                spectra[0, pl.ds(SUB + row, 8), :] = jnp.zeros_like(real)
                continue
            cos = jnp.broadcast_to(factors[:, k : k + 1], (8, lanes))
            sin = jnp.broadcast_to(factors[:, half + 1 + k : half + 2 + k], (8, lanes))
            if imag is None:
                spectra[k, pl.ds(row, 8), :] = real * cos
                spectra[k, pl.ds(SUB + row, 8), :] = real * sin
            else:
                spectra[k, pl.ds(row, 8), :] = real * cos - imag * sin
                spectra[k, pl.ds(SUB + row, 8), :] = real * sin + imag * cos
        return carry

    lax.fori_loop(0, SUB // 8, slab, 0)
    for k in range(half + 1, spectra.shape[0]):
        spectra[k] = jnp.zeros(spectra.shape[1:], F32)


def last_stage(spectra, series):
    half = series.shape[0] // SUB

    def slab(step, carry):
        row = pl.multiple_of(step * 8, 8)
        bins = []
        for k in range(half + 1):
            real = spectra[k, pl.ds(row, 8), :]
            imag = None if k in (0, half) else spectra[k, pl.ds(SUB + row, 8), :]
            bins.append((real, imag))
        for n, value in enumerate(real_inverse(bins)):
            series[pl.ds(SUB * n + row, 8), :] = value
        return carry

    lax.fori_loop(0, SUB // 8, slab, 0)


def taps_kernel(blocks, me_ref, *refs):
    pieces, (twiddle, forward, spectra_out, series, spectra) = refs[:blocks], refs[blocks:]
    span = pieces[0].shape[1]
    for m in range(blocks):
        start = pl.multiple_of((me_ref[0] ^ m) * span, span)
        series[pl.ds(start, span), :] = pieces[m][...].astype(F32).T
    first_stage(series, spectra, twiddle)

    def pair(p, carry):
        data = jnp.concatenate([spectra[2 * p], spectra[2 * p + 1]], axis=1)
        spectra_out[p] = split_dot(forward, data)
        return carry

    lax.fori_loop(0, spectra_out.shape[0], pair, 0)


def conv_kernel(blocks, me_ref, *refs):
    pieces = refs[:blocks]
    taps_spectra, twiddle, forward, inverse, skip = refs[blocks : blocks + 5]
    outs = refs[blocks + 5 : 2 * blocks + 5]
    series, spectra, result = refs[2 * blocks + 5 :]
    span, lanes = pieces[0].shape
    half = series.shape[0] // SUB
    for m in range(blocks):
        start = pl.multiple_of((me_ref[0] ^ m) * span, span)
        series[pl.ds(start, span), :] = pieces[m][...].astype(F32)
    first_stage(series, spectra, twiddle)

    def pair(p, carry):
        data = jnp.concatenate([spectra[2 * p], spectra[2 * p + 1]], axis=1)
        signal = split_dot(forward, data)
        signal_re, signal_im = signal[:SUB], signal[SUB:]
        taps_re, taps_im = taps_spectra[p, :SUB, :], taps_spectra[p, SUB:, :]
        product = jnp.concatenate(
            [
                signal_re * taps_re - signal_im * taps_im,
                signal_re * taps_im + signal_im * taps_re,
            ],
            axis=0,
        )
        back = split_dot(inverse, product)
        spectra[2 * p] = back[:, :lanes]
        spectra[2 * p + 1] = back[:, lanes:]
        return carry

    lax.fori_loop(0, taps_spectra.shape[0], pair, 0)
    for k in range(1, half + 1):
        real, imag = spectra[k, :SUB, :], spectra[k, SUB:, :]
        cos = jnp.broadcast_to(twiddle[:, k : k + 1], (SUB, lanes))
        sin = jnp.broadcast_to(twiddle[:, half + 1 + k : half + 2 + k], (SUB, lanes))
        spectra[k, :SUB, :] = real * cos + imag * sin
        if k < half:
            spectra[k, SUB:, :] = imag * cos - real * sin
    last_stage(spectra, result)
    for m in range(blocks):
        start = pl.multiple_of((me_ref[0] ^ m) * span, span)
        window = pl.ds(start, span)
        outs[m][...] = (result[window, :] + skip[...] * series[window, :]).astype(BF16)


VMEM = pl.BlockSpec(memory_space=pltpu.VMEM)
SMEM = pl.BlockSpec(memory_space=pltpu.SMEM)
GRANT = pltpu.CompilerParams(vmem_limit_bytes=40 * 2**20)


def taps_spectra_of(me, pieces, twiddle, forward):
    blocks = len(pieces)
    lanes, span = pieces[0].shape
    half = blocks * span // SUB
    pairs = (half + 2) // 2
    return pl.pallas_call(
        partial(taps_kernel, blocks),
        out_shape=jax.ShapeDtypeStruct((pairs, 2 * SUB, 2 * lanes), F32),
        in_specs=[SMEM] + [VMEM] * (blocks + 2),
        out_specs=VMEM,
        scratch_shapes=[
            pltpu.VMEM((blocks * span, lanes), F32),
            pltpu.VMEM((2 * pairs, 2 * SUB, lanes), F32),
        ],
        compiler_params=GRANT,
        name="taps_spectra",
    )(me, *pieces, twiddle, forward)


def long_conv(me, pieces, taps_spectra, twiddle, forward, inverse, skip):
    blocks = len(pieces)
    span, lanes = pieces[0].shape
    pairs = taps_spectra.shape[0]
    return pl.pallas_call(
        partial(conv_kernel, blocks),
        out_shape=[jax.ShapeDtypeStruct((span, lanes), BF16)] * blocks,
        in_specs=[SMEM] + [VMEM] * (blocks + 5),
        out_specs=[VMEM] * blocks,
        scratch_shapes=[
            pltpu.VMEM((blocks * span, lanes), F32),
            pltpu.VMEM((2 * pairs, 2 * SUB, lanes), F32),
            pltpu.VMEM((blocks * span, lanes), F32),
        ],
        compiler_params=GRANT,
        name="long_conv",
    )(me, *pieces, taps_spectra, twiddle, forward, inverse, skip)


def shifted_mix(stream, edge, weight):
    first = jnp.concatenate([edge[1:2], stream[:-1]], axis=0)
    second = jnp.concatenate([edge, stream[:-2]], axis=0)
    return weight[0:1] * stream + weight[1:2] * first + weight[2:3] * second


def gate_in_kernel(me_ref, key, value, edges, weight, *outs):
    mixed = [
        shifted_mix(ref[...].astype(F32), edges[2 * s : 2 * s + 2].astype(F32), weight[:, s, :])
        for s, ref in ((1, key), (2, value))
    ]
    gated = (mixed[0] * mixed[1]).astype(BF16)
    for m, out in enumerate(outs):

        @pl.when(pl.program_id(0) == m)
        def _(out=out):
            out[...] = gated


def gate_in(me, key_rows, value_rows, edges, short_weight, blocks):
    span, chans = key_rows.shape
    lanes = chans // blocks
    column = lambda m, me: (0, me[0] ^ m)
    return pl.pallas_call(
        gate_in_kernel,
        grid_spec=pltpu.PrefetchScalarGridSpec(
            num_scalar_prefetch=1,
            grid=(blocks,),
            in_specs=[
                pl.BlockSpec((span, lanes), column),
                pl.BlockSpec((span, lanes), column),
                pl.BlockSpec((6, lanes), column),
                pl.BlockSpec((3, 3, lanes), lambda m, me: (0, 0, me[0] ^ m)),
            ],
            out_specs=[pl.BlockSpec((span, lanes), lambda m, me: (0, 0))] * blocks,
        ),
        out_shape=[jax.ShapeDtypeStruct((span, lanes), BF16)] * blocks,
        name="gate_in",
    )(me, key_rows, value_rows, edges, short_weight)


def split_taps_kernel(me_ref, taps, *outs):
    for m, out in enumerate(outs):

        @pl.when(pl.program_id(0) == m)
        def _(out=out):
            out[...] = taps[...]


def split_taps(me, filter_taps, blocks):
    chans, span = filter_taps.shape
    lanes = chans // blocks
    return pl.pallas_call(
        split_taps_kernel,
        grid_spec=pltpu.PrefetchScalarGridSpec(
            num_scalar_prefetch=1,
            grid=(blocks,),
            in_specs=[pl.BlockSpec((lanes, span), lambda m, me: (me[0] ^ m, 0))],
            out_specs=[pl.BlockSpec((lanes, span), lambda m, me: (0, 0))] * blocks,
        ),
        out_shape=[jax.ShapeDtypeStruct((lanes, span), BF16)] * blocks,
        name="split_taps",
    )(me, filter_taps)


def mix_query_kernel(query, edges, weight, out):
    out[...] = shifted_mix(query[...].astype(F32), edges[0:2].astype(F32), weight[:, 0, :])


def mix_query(query_rows, edges, short_weight):
    span, chans = query_rows.shape
    lanes = chans // 4
    return pl.pallas_call(
        mix_query_kernel,
        grid=(4,),
        in_specs=[
            pl.BlockSpec((span, lanes), lambda g: (0, g)),
            pl.BlockSpec((6, lanes), lambda g: (0, g)),
            pl.BlockSpec((3, 3, lanes), lambda g: (0, 0, g)),
        ],
        out_specs=pl.BlockSpec((span, lanes), lambda g: (0, g)),
        out_shape=jax.ShapeDtypeStruct((span, chans), F32),
        name="mix_query",
    )(query_rows, edges, short_weight)


def exchange(pieces, axis):
    devices = range(lax.axis_size(axis))
    return [pieces[0]] + [
        lax.ppermute(piece, axis, [(i, i ^ m) for i in devices])
        for m, piece in enumerate(pieces)
        if m
    ]


def project(gated_out, out_weight):
    term = jnp.dot(gated_out, out_weight, preferred_element_type=F32)
    return lax.psum_scatter(term.astype(BF16), "tp", scatter_dimension=1, tiled=True)


def gate_out_kernel(blocks, me_ref, *refs):
    convs, (mixed, out) = refs[:blocks], refs[blocks:]
    lanes = convs[0].shape[1]
    for m in range(blocks):
        window = pl.ds(pl.multiple_of((me_ref[0] ^ m) * lanes, lanes), lanes)
        out[:, window] = (mixed[:, window] * convs[m][...].astype(F32)).astype(BF16)


def gate_out(me, convs, mixed):
    span, chans = mixed.shape
    return pl.pallas_call(
        partial(gate_out_kernel, len(convs)),
        out_shape=jax.ShapeDtypeStruct((span, chans), BF16),
        in_specs=[SMEM] + [VMEM] * (len(convs) + 1),
        out_specs=VMEM,
        compiler_params=GRANT,
        name="gate_out",
    )(me, *convs, mixed)


def fast_per_device(
    query_rows, key_rows, value_rows, short_weight, skip_gain, filter_taps, out_weight
):
    span, chans = query_rows.shape
    blocks = lax.axis_size("ctx")
    lanes = chans // blocks
    length = span * blocks
    radix = 2 * length // SUB
    place = lax.axis_index("ctx")
    me = place.astype(jnp.int32).reshape(1)
    forward, inverse = (jnp.asarray(t) for t in dft_tables(2 * length))
    twiddle = jnp.asarray(twiddle_table(radix))
    edges = jnp.concatenate([x[-2:] for x in (query_rows, key_rows, value_rows)])
    edges = passed_along(edges, "ctx", 1)
    taps = exchange(split_taps(me, filter_taps, blocks), "ctx")
    gated = exchange(gate_in(me, key_rows, value_rows, edges, short_weight, blocks), "ctx")
    mixed = mix_query(query_rows, edges, short_weight)
    skip = lax.dynamic_slice(skip_gain, (place * lanes,), (lanes,)).reshape(1, lanes)
    spectra = taps_spectra_of(me, taps, twiddle, forward)
    convs = long_conv(me, gated, spectra, twiddle, forward, inverse, skip)
    convs = exchange(convs, "ctx")
    gated_out = gate_out(me, convs, mixed)
    return project(gated_out, out_weight)


def per_device(*arrays):
    span, chans = arrays[0].shape
    blocks = lax.axis_size("ctx")
    suits = blocks == 8 and lax.axis_size("tp") == 4 and span == 512 and chans == 8 * SUB
    return (fast_per_device if suits else general_per_device)(*arrays)


def solution(mesh):
    placed = (
        P("ctx", "tp"),
        P("ctx", "tp"),
        P("ctx", "tp"),
        P(None, None, "tp"),
        P("tp"),
        P("tp", "ctx"),
        P("tp", None),
    )
    return jax.shard_map(
        per_device, mesh=mesh, in_specs=placed, out_specs=P("ctx", "tp"), check_vma=False
    )
```

```python
from functools import partial
import math

import jax
import jax.numpy as jnp
import numpy as np
from jax import lax
from jax.experimental import pallas as pl
from jax.experimental.pallas import tpu as pltpu
from jax.sharding import PartitionSpec as P

TRIPLE = lax.Precision.HIGH


def passed_along(block, axis, distance):
    devices = range(lax.axis_size(axis))
    route = [(i - distance, i) for i in devices if i - distance in devices]
    return lax.ppermute(block, axis, route)


def angle_table(left, right, offset, period):
    rows = lax.broadcasted_iota(jnp.int32, (left, right), 0)
    cols = lax.broadcasted_iota(jnp.int32, (left, right), 1) + offset
    turns = rows * cols % period
    return turns.astype(jnp.float32) * (2.0 * math.pi / period)


def inner_spectrum(rows, table_high, table_low):
    upper = jnp.dot(rows, table_high, preferred_element_type=jnp.float32)
    lower = jnp.dot(rows, table_low, preferred_element_type=jnp.float32)
    return upper + lower


def block_mix(real_component, imaginary_component, cosine_lookup, sine_lookup, sign):
    multiplier = partial(jnp.einsum, precision=TRIPLE, preferred_element_type=jnp.float32)
    cosine_real = multiplier("id,rdy->riy", cosine_lookup, real_component)
    cosine_imaginary = multiplier("id,rdy->riy", cosine_lookup, imaginary_component)
    sine_real = multiplier("id,rdy->riy", sine_lookup, real_component)
    sine_imaginary = multiplier("id,rdy->riy", sine_lookup, imaginary_component)
    return (cosine_real + sign * sine_imaginary, cosine_imaginary - sign * sine_real)


def general_per_device(query_rows, key_rows, value_rows, short_weight, skip_gain, filter_taps, out_weight):
    span = query_rows.shape[0]
    chans = query_rows.shape[1]
    blocks = lax.axis_size("ctx")
    group = chans // blocks
    period = 2 * span
    padded = 2 * blocks
    forward = angle_table(span, period, 0, period)
    forward = jnp.concatenate([jnp.cos(forward), -jnp.sin(forward)], axis=1)
    table_high = forward.astype(jnp.bfloat16)
    table_low = (forward - table_high.astype(jnp.float32)).astype(jnp.bfloat16)
    parity = 1.0 - 2.0 * (jnp.arange(period) % 2).astype(jnp.float32)
    parity = jnp.concatenate([parity, parity])
    stacked = jnp.stack([query_rows, key_rows, value_rows])
    rims = passed_along(stacked[:, -2:, :], "ctx", 1)
    extended = jnp.concatenate([rims, stacked], axis=1).astype(jnp.float32)
    mixed = (
        short_weight[0][:, None, :] * extended[:, 2:]
        + short_weight[1][:, None, :] * extended[:, 1:-1]
        + short_weight[2][:, None, :] * extended[:, :span]
    )
    gated_in = (mixed[1] * mixed[2]).astype(jnp.bfloat16)
    gated_t = gated_in.T
    inputs_local, taps_local = (
        lax.all_to_all(gated_t, "ctx", split_axis=0, concat_axis=1, tiled=True),
        lax.all_to_all(filter_taps, "ctx", split_axis=0, concat_axis=1, tiled=True),
    )
    spectra = inner_spectrum(
        taps_local.reshape(group * blocks, span), table_high, table_low
    ).reshape(group, blocks, 2 * period)
    earlier = jnp.concatenate(
        [jnp.zeros((group, 1, 2 * period), jnp.float32), spectra[:, :-1]], axis=1
    )
    kernel_spec = earlier + parity * spectra
    input_spec = inner_spectrum(
        inputs_local.reshape(group * blocks, span), table_high, table_low
    ).reshape(group, blocks, 2 * period)
    block_angle = angle_table(padded, blocks, 0, padded)
    cos_fwd = jnp.cos(block_angle)
    sin_fwd = jnp.sin(block_angle)
    input_re, input_im = block_mix(
        input_spec[..., :period], input_spec[..., period:], cos_fwd, sin_fwd, 1.0
    )
    kernel_re, kernel_im = block_mix(
        kernel_spec[..., :period], kernel_spec[..., period:], cos_fwd, sin_fwd, 1.0
    )
    product_re = input_re * kernel_re - input_im * kernel_im
    product_im = input_re * kernel_im + input_im * kernel_re
    back_angle = angle_table(blocks, padded, 0, padded)
    out_re, out_im = block_mix(
        product_re, product_im, jnp.cos(back_angle), jnp.sin(back_angle), -1.0
    )
    inverse = angle_table(period, span, span, period)
    inverse = jnp.concatenate([jnp.cos(inverse), -jnp.sin(inverse)], axis=0) * (
        1.0 / (period * padded)
    )
    joined = jnp.concatenate([out_re, out_im], axis=2).reshape(group * blocks, 2 * period)
    long_local = jnp.dot(
        joined, inverse, precision=TRIPLE, preferred_element_type=jnp.float32
    ).reshape(group, blocks * span)
    long_t = lax.all_to_all(
        long_local.astype(jnp.bfloat16), "ctx", split_axis=1, concat_axis=0, tiled=True
    ).astype(long_local.dtype)
    conv_t = (long_t + skip_gain[:, None] * gated_t.astype(jnp.float32)).astype(jnp.bfloat16)
    gated_out = (mixed[0].T * conv_t.astype(jnp.float32)).astype(jnp.bfloat16)
    term = lax.dot_general(
        gated_out, out_weight, (((0,), (0,)), ((), ())), preferred_element_type=jnp.float32
    )
    return lax.psum_scatter(term.astype(jnp.bfloat16), "tp", scatter_dimension=1, tiled=True)


SUB = 128
F32 = jnp.float32
BF16 = jnp.bfloat16


def split_table(matrix):
    high = matrix.astype(jnp.bfloat16)
    low = (matrix - high.astype(np.float32)).astype(jnp.bfloat16)
    return np.concatenate([high, high, low], axis=1)


def dft_tables(period):
    index = np.arange(SUB)
    turns = np.outer(index, index) % SUB * (2.0 * np.pi / SUB)
    cos, sin = np.cos(turns), np.sin(turns)
    forward = np.block([[cos, sin], [-sin, cos]]).astype(np.float32)
    inverse = (np.block([[cos, -sin], [sin, cos]]) / period).astype(np.float32)
    return split_table(forward), split_table(inverse)


def twiddle_table(radix):
    half = radix // 2
    turns = np.outer(np.arange(SUB), np.arange(half + 1)) * (2.0 * np.pi / (radix * SUB))
    return np.concatenate([np.cos(turns), -np.sin(turns)], axis=1).astype(np.float32)


def times(value, factor):
    return None if value is None else value * factor


def plus(left, right):
    if left is None:
        return right
    return left if right is None else left + right


def minus(left, right):
    if right is None:
        return left
    return -right if left is None else left - right


def rotate(value, turn):
    real, imag = value
    cos, sin = math.cos(2 * math.pi * turn), math.sin(2 * math.pi * turn)
    if abs(cos - sin) < 1e-12 and imag is not None:
        return (real + imag) * cos, (imag - real) * cos
    return plus(times(real, cos), times(imag, sin)), minus(times(imag, cos), times(real, sin))


def real_forward(values):
    points = 2 * len(values)
    if points == 2:
        return [(values[0], None), (values[0], None)]
    even, odd = real_forward(values[0::2]), real_forward(values[1::2])
    bins = [None] * (points // 2 + 1)
    bins[0] = (even[0][0] + odd[0][0], None)
    bins[points // 2] = (even[0][0] - odd[0][0], None)
    quarter = points // 4
    for k in range(1, quarter):
        turned = rotate(odd[k], k / points)
        bins[k] = (even[k][0] + turned[0], even[k][1] + turned[1])
        bins[points // 2 - k] = (even[k][0] - turned[0], turned[1] - even[k][1])
    bins[quarter] = (even[quarter][0], -odd[quarter][0])
    return bins


def real_inverse(bins):
    half = len(bins) - 1
    points = 2 * half
    if points == 2:
        return [bins[0][0] + bins[1][0]]
    even, odd = [], []
    for k in range(half // 2 + 1):
        ahead, back = bins[k], bins[half - k]
        if k == 0:
            even.append((ahead[0] + back[0], None))
            odd.append((ahead[0] - back[0], None))
        elif k == half // 2:
            even.append((ahead[0] * 2.0, None))
            odd.append((ahead[1] * -2.0, None))
        else:
            even.append((ahead[0] + back[0], ahead[1] - back[1]))
            difference = (ahead[0] - back[0], ahead[1] + back[1])
            odd.append(rotate(difference, -k / points))
    even, odd = real_inverse(even), real_inverse(odd)
    return [value for pair in zip(even, odd) for value in pair]


def split_dot(table, data):
    high = data.astype(BF16)
    low = (data - high.astype(F32)).astype(BF16)
    return jnp.dot(
        table[...], jnp.concatenate([high, low, high], axis=0), preferred_element_type=F32
    )


def first_stage(series, spectra, twiddle):
    half = series.shape[0] // SUB
    lanes = series.shape[1]

    def slab(step, carry):
        row = pl.multiple_of(step * 8, 8)
        values = [series[pl.ds(SUB * n + row, 8), :] for n in range(half)]
        factors = twiddle[pl.ds(row, 8), :]
        for k, (real, imag) in enumerate(real_forward(values)):
            if k == 0:
                spectra[0, pl.ds(row, 8), :] = real
                spectra[0, pl.ds(SUB + row, 8), :] = jnp.zeros_like(real)
                continue
            cos = jnp.broadcast_to(factors[:, k : k + 1], (8, lanes))
            sin = jnp.broadcast_to(factors[:, half + 1 + k : half + 2 + k], (8, lanes))
            if imag is None:
                spectra[k, pl.ds(row, 8), :] = real * cos
                spectra[k, pl.ds(SUB + row, 8), :] = real * sin
            else:
                spectra[k, pl.ds(row, 8), :] = real * cos - imag * sin
                spectra[k, pl.ds(SUB + row, 8), :] = real * sin + imag * cos
        return carry

    lax.fori_loop(0, SUB // 8, slab, 0)
    for k in range(half + 1, spectra.shape[0]):
        spectra[k] = jnp.zeros(spectra.shape[1:], F32)


def last_stage(spectra, series):
    half = series.shape[0] // SUB

    def slab(step, carry):
        row = pl.multiple_of(step * 8, 8)
        bins = []
        for k in range(half + 1):
            real = spectra[k, pl.ds(row, 8), :]
            imag = None if k in (0, half) else spectra[k, pl.ds(SUB + row, 8), :]
            bins.append((real, imag))
        for n, value in enumerate(real_inverse(bins)):
            series[pl.ds(SUB * n + row, 8), :] = value
        return carry

    lax.fori_loop(0, SUB // 8, slab, 0)


def taps_kernel(blocks, me_ref, *refs):
    pieces, (twiddle, forward, spectra_out, series, spectra) = refs[:blocks], refs[blocks:]
    span = pieces[0].shape[1]
    for m in range(blocks):
        start = pl.multiple_of((me_ref[0] ^ m) * span, span)
        series[pl.ds(start, span), :] = pieces[m][...].astype(F32).T
    first_stage(series, spectra, twiddle)

    def pair(p, carry):
        data = jnp.concatenate([spectra[2 * p], spectra[2 * p + 1]], axis=1)
        spectra_out[p] = split_dot(forward, data)
        return carry

    lax.fori_loop(0, spectra_out.shape[0], pair, 0)


def conv_kernel(blocks, me_ref, *refs):
    pieces = refs[:blocks]
    taps_spectra, twiddle, forward, inverse, skip = refs[blocks : blocks + 5]
    outs = refs[blocks + 5 : 2 * blocks + 5]
    series, spectra, result = refs[2 * blocks + 5 :]
    span, lanes = pieces[0].shape
    half = series.shape[0] // SUB
    for m in range(blocks):
        start = pl.multiple_of((me_ref[0] ^ m) * span, span)
        series[pl.ds(start, span), :] = pieces[m][...].astype(F32)
    first_stage(series, spectra, twiddle)

    def pair(p, carry):
        data = jnp.concatenate([spectra[2 * p], spectra[2 * p + 1]], axis=1)
        signal = split_dot(forward, data)
        signal_re, signal_im = signal[:SUB], signal[SUB:]
        taps_re, taps_im = taps_spectra[p, :SUB, :], taps_spectra[p, SUB:, :]
        product = jnp.concatenate(
            [
                signal_re * taps_re - signal_im * taps_im,
                signal_re * taps_im + signal_im * taps_re,
            ],
            axis=0,
        )
        back = split_dot(inverse, product)
        spectra[2 * p] = back[:, :lanes]
        spectra[2 * p + 1] = back[:, lanes:]
        return carry

    lax.fori_loop(0, taps_spectra.shape[0], pair, 0)
    for k in range(1, half + 1):
        real, imag = spectra[k, :SUB, :], spectra[k, SUB:, :]
        cos = jnp.broadcast_to(twiddle[:, k : k + 1], (SUB, lanes))
        sin = jnp.broadcast_to(twiddle[:, half + 1 + k : half + 2 + k], (SUB, lanes))
        spectra[k, :SUB, :] = real * cos + imag * sin
        if k < half:
            spectra[k, SUB:, :] = imag * cos - real * sin
    last_stage(spectra, result)
    for m in range(blocks):
        start = pl.multiple_of((me_ref[0] ^ m) * span, span)
        window = pl.ds(start, span)
        outs[m][...] = (result[window, :] + skip[...] * series[window, :]).astype(BF16)


VMEM = pl.BlockSpec(memory_space=pltpu.VMEM)
SMEM = pl.BlockSpec(memory_space=pltpu.SMEM)
GRANT = pltpu.CompilerParams(vmem_limit_bytes=40 * 2**20)


def taps_spectra_of(me, pieces, twiddle, forward):
    blocks = len(pieces)
    lanes, span = pieces[0].shape
    half = blocks * span // SUB
    pairs = (half + 2) // 2
    return pl.pallas_call(
        partial(taps_kernel, blocks),
        out_shape=jax.ShapeDtypeStruct((pairs, 2 * SUB, 2 * lanes), F32),
        in_specs=[SMEM] + [VMEM] * (blocks + 2),
        out_specs=VMEM,
        scratch_shapes=[
            pltpu.VMEM((blocks * span, lanes), F32),
            pltpu.VMEM((2 * pairs, 2 * SUB, lanes), F32),
        ],
        compiler_params=GRANT,
        name="taps_spectra",
    )(me, *pieces, twiddle, forward)


def long_conv(me, pieces, taps_spectra, twiddle, forward, inverse, skip):
    blocks = len(pieces)
    span, lanes = pieces[0].shape
    pairs = taps_spectra.shape[0]
    return pl.pallas_call(
        partial(conv_kernel, blocks),
        out_shape=[jax.ShapeDtypeStruct((span, lanes), BF16)] * blocks,
        in_specs=[SMEM] + [VMEM] * (blocks + 5),
        out_specs=[VMEM] * blocks,
        scratch_shapes=[
            pltpu.VMEM((blocks * span, lanes), F32),
            pltpu.VMEM((2 * pairs, 2 * SUB, lanes), F32),
            pltpu.VMEM((blocks * span, lanes), F32),
        ],
        compiler_params=GRANT,
        name="long_conv",
    )(me, *pieces, taps_spectra, twiddle, forward, inverse, skip)


def shifted_mix(stream, edge, weight):
    first = jnp.concatenate([edge[1:2], stream[:-1]], axis=0)
    second = jnp.concatenate([edge, stream[:-2]], axis=0)
    return weight[0:1] * stream + weight[1:2] * first + weight[2:3] * second


def gate_in_kernel(me_ref, key, value, edges, weight, *outs):
    mixed = [
        shifted_mix(ref[...].astype(F32), edges[2 * s : 2 * s + 2].astype(F32), weight[:, s, :])
        for s, ref in ((1, key), (2, value))
    ]
    gated = (mixed[0] * mixed[1]).astype(BF16)
    for m, out in enumerate(outs):

        @pl.when(pl.program_id(0) == m)
        def _(out=out):
            out[...] = gated


def gate_in(me, key_rows, value_rows, edges, short_weight, blocks):
    span, chans = key_rows.shape
    lanes = chans // blocks
    column = lambda m, me: (0, me[0] ^ m)
    return pl.pallas_call(
        gate_in_kernel,
        grid_spec=pltpu.PrefetchScalarGridSpec(
            num_scalar_prefetch=1,
            grid=(blocks,),
            in_specs=[
                pl.BlockSpec((span, lanes), column),
                pl.BlockSpec((span, lanes), column),
                pl.BlockSpec((6, lanes), column),
                pl.BlockSpec((3, 3, lanes), lambda m, me: (0, 0, me[0] ^ m)),
            ],
            out_specs=[pl.BlockSpec((span, lanes), lambda m, me: (0, 0))] * blocks,
        ),
        out_shape=[jax.ShapeDtypeStruct((span, lanes), BF16)] * blocks,
        name="gate_in",
    )(me, key_rows, value_rows, edges, short_weight)


def split_taps_kernel(me_ref, taps, *outs):
    for m, out in enumerate(outs):

        @pl.when(pl.program_id(0) == m)
        def _(out=out):
            out[...] = taps[...]


def split_taps(me, filter_taps, blocks):
    chans, span = filter_taps.shape
    lanes = chans // blocks
    return pl.pallas_call(
        split_taps_kernel,
        grid_spec=pltpu.PrefetchScalarGridSpec(
            num_scalar_prefetch=1,
            grid=(blocks,),
            in_specs=[pl.BlockSpec((lanes, span), lambda m, me: (me[0] ^ m, 0))],
            out_specs=[pl.BlockSpec((lanes, span), lambda m, me: (0, 0))] * blocks,
        ),
        out_shape=[jax.ShapeDtypeStruct((lanes, span), BF16)] * blocks,
        name="split_taps",
    )(me, filter_taps)


def mix_query_kernel(query, edges, weight, out):
    out[...] = shifted_mix(query[...].astype(F32), edges[0:2].astype(F32), weight[:, 0, :])


def mix_query(query_rows, edges, short_weight):
    span, chans = query_rows.shape
    lanes = chans // 4
    return pl.pallas_call(
        mix_query_kernel,
        grid=(4,),
        in_specs=[
            pl.BlockSpec((span, lanes), lambda g: (0, g)),
            pl.BlockSpec((6, lanes), lambda g: (0, g)),
            pl.BlockSpec((3, 3, lanes), lambda g: (0, 0, g)),
        ],
        out_specs=pl.BlockSpec((span, lanes), lambda g: (0, g)),
        out_shape=jax.ShapeDtypeStruct((span, chans), F32),
        name="mix_query",
    )(query_rows, edges, short_weight)


def exchange(pieces, axis):
    devices = range(lax.axis_size(axis))
    return [pieces[0]] + [
        lax.ppermute(piece, axis, [(i, i ^ m) for i in devices])
        for m, piece in enumerate(pieces)
        if m
    ]


def gate_out_kernel(blocks, place, *refs):
    convs, (mixed, far_weight, head, tail, right, left) = refs[:blocks], refs[blocks:]
    lanes = convs[0].shape[1]
    rows = head.shape[0]
    stage, last = place[1], place[2]
    for m in range(blocks):
        window = pl.ds(pl.multiple_of((place[0] ^ m) * lanes, lanes), lanes)
        gated = (mixed[:, window] * convs[m][...].astype(F32)).astype(BF16)
        head[:, window] = gated[:rows]
        tail[:, window] = gated[rows:]
    for index, out in ((0, right), (last, left)):

        @pl.when(stage == index)
        def _(out=out):
            term = jnp.dot(tail[...], far_weight[...], preferred_element_type=F32)
            out[...] = term.astype(BF16)

        @pl.when(stage != index)
        def _(out=out):
            out[...] = head[...]


def gate_out(place, convs, mixed, out_weight):
    span, chans = mixed.shape
    whole = lambda shape: pl.BlockSpec(shape, lambda g, place: (0,) * len(shape))
    return pl.pallas_call(
        partial(gate_out_kernel, len(convs)),
        grid_spec=pltpu.PrefetchScalarGridSpec(
            num_scalar_prefetch=1,
            grid=(1,),
            in_specs=[whole(x.shape) for x in (*convs, mixed)]
            + [pl.BlockSpec((chans, chans), lambda g, place: (0, place[3]))],
            out_specs=[whole((span // 2, chans))] * 4,
        ),
        out_shape=[jax.ShapeDtypeStruct((span // 2, chans), BF16)] * 4,
        compiler_params=GRANT,
        name="gate_out",
    )(place, *convs, mixed, out_weight)


def weight_rows(out_weight, stages):
    stage, place = lax.axis_index("tp"), lax.axis_index("ctx")
    chans = out_weight.shape[0]
    rows = chans // lax.axis_size("ctx")
    found = []
    for d in range(1, stages):
        column = (stage + d) % stages * chans
        part = lax.dynamic_slice(out_weight, (place * rows, column), (rows, chans))
        found.append(lax.ppermute(part, "tp", [(i, (i + d) % stages) for i in range(stages)]))
    return jnp.stack(found)


def gather_weight(part):
    devices = range(lax.axis_size("ctx"))
    near = [(i, i ^ (4 if i & 1 else 2)) for i in devices]
    other = [(i, i ^ (2 if i & 1 else 4)) for i in devices]
    two = jnp.stack([part, lax.ppermute(part, "ctx", near)])
    four = jnp.concatenate([two, lax.ppermute(two, "ctx", other)])
    return four, lax.ppermute(four, "ctx", [(i, i ^ 1) for i in devices])


def add_parts(order, data, weights, chosen):
    total = None
    for half, weight in enumerate(weights):
        count, _, lanes, columns = weight.shape
        picked = jnp.concatenate(
            [
                data[:, pl.ds(pl.multiple_of(order[4 * half + q] * lanes, lanes), lanes)]
                for q in range(count)
            ],
            axis=1,
        )
        block = weight[:, chosen].reshape(count * lanes, columns)
        term = jnp.dot(picked, block, preferred_element_type=F32)
        total = term if total is None else total + term
    return total


def early_kernel(order, own, first, second, own_weight, near_weight, far_weight, out):
    weights = (near_weight, far_weight)
    out[...] = jnp.dot(own[...], own_weight[...], preferred_element_type=F32)
    out[...] += add_parts(order, first, weights, order[8])
    out[...] += add_parts(order, second, weights, order[9])


def early_sum(order, own, first, second, out_weight, near_weight, far_weight):
    rows, chans = own.shape
    whole = lambda shape: pl.BlockSpec(shape, lambda g, order: (0,) * len(shape))
    return pl.pallas_call(
        early_kernel,
        grid_spec=pltpu.PrefetchScalarGridSpec(
            num_scalar_prefetch=1,
            grid=(1,),
            in_specs=[whole(own.shape)] * 3
            + [pl.BlockSpec((chans, chans), lambda g, order: (0, order[11]))]
            + [whole(near_weight.shape)] * 2,
            out_specs=whole((rows, chans)),
        ),
        out_shape=jax.ShapeDtypeStruct((rows, chans), F32),
        compiler_params=GRANT,
        name="early_sum",
    )(order, own, first, second, out_weight, near_weight, far_weight)


def final_kernel(order, *refs):
    thirds, (early, own, right2, right3, left2, left3) = refs[:4], refs[4:10]
    near_weight, far_weight, out, picked = refs[10:]
    rows = early.shape[0]
    stage, last = order[11], order[12]
    for k, third in enumerate(thirds):

        @pl.when(stage == k)
        def _(third=third):
            picked[...] = third[...]

    total = early[...] + add_parts(order, picked, (near_weight, far_weight), order[10])
    out[:rows] = total.astype(BF16)
    right = jnp.where(stage == last, right2[...].astype(F32), right3[...].astype(F32))
    left = jnp.where(stage == 0, left2[...].astype(F32), left3[...].astype(F32))
    out[rows:] = (own[...].astype(F32) + right + left).astype(BF16)


def final_sum(order, thirds, early, own, arrived, near_weight, far_weight):
    rows, chans = own.shape
    return pl.pallas_call(
        final_kernel,
        out_shape=jax.ShapeDtypeStruct((2 * rows, chans), BF16),
        in_specs=[SMEM] + [VMEM] * 12,
        out_specs=VMEM,
        scratch_shapes=[pltpu.VMEM((rows, chans), BF16)],
        compiler_params=GRANT,
        name="final_sum",
    )(order, *thirds, early, own, *arrived, near_weight, far_weight)


def weight_order():
    place, stage = lax.axis_index("ctx"), lax.axis_index("tp")
    a = jnp.where(place % 2 == 0, 2, 4)
    masks = [0 * a, a, 6 - a, 0 * a + 6]
    swapped = [0 * a + 1, (6 - a) ^ 1, a ^ 1, 0 * a + 7]
    parts = [place ^ mask for mask in masks + swapped]
    distances = [jnp.array(row)[stage] - 1 for row in ((3, 3, 1, 1), (2, 1, 3, 2), (1, 2, 2, 3))]
    last = lax.axis_size("tp") - 1
    return jnp.stack(parts + distances + [stage, last + 0 * stage]).astype(jnp.int32)


def project(place, convs, mixed, out_weight, weight_part):
    stages = lax.axis_size("tp")
    stage = lax.axis_index("tp")
    order = weight_order()
    head, tail, right0, left0 = gate_out(place, convs, mixed, out_weight)
    chans = head.shape[1]
    ahead = [(i, i + 1) for i in range(stages - 1)]
    astern = [(i + 1, i) for i in range(stages - 1)]
    to_right = lambda x: lax.ppermute(x, "tp", ahead)
    to_left = lambda x: lax.ppermute(x, "tp", astern)
    got_right0, got_left0 = to_right(right0), to_left(left0)
    terms = jnp.dot(tail, out_weight, preferred_element_type=F32).astype(BF16)

    def term(index):
        return lax.dynamic_slice(terms, (0, index * chans), (terms.shape[0], chans)).astype(F32)

    def add(index, arrived):
        return (term(index) + arrived.astype(F32)).astype(BF16)

    right1 = jnp.where(
        stage == 0, head, jnp.where(stage == 1, add(3, got_right0), got_right0)
    )
    left1 = jnp.where(stage == 3, head, jnp.where(stage == 2, add(0, got_left0), got_left0))
    got_right1, got_left1 = to_right(right1), to_left(left1)
    right2 = jnp.where(
        stage == 1, got_right1, add(jnp.where(stage == 0, 2, 3), got_right1)
    )
    left2 = jnp.where(stage == 2, got_left1, add(jnp.where(stage == 3, 1, 0), got_left1))
    got_right2, got_left2 = to_right(right2), to_left(left2)
    right3 = jnp.where(stage == 2, got_right2, add(jnp.minimum(stage + 1, 3), got_right2))
    left3 = jnp.where(stage == 1, got_left2, add(jnp.maximum(stage - 1, 0), got_left2))
    got_right3, got_left3 = to_right(right3), to_left(left3)

    near_weight, far_weight = gather_weight(weight_part)
    first = jnp.where(stage < 2, got_left0, got_right0)
    second = jnp.where(stage % 2 == 0, got_left1, got_right1)
    early = early_sum(order, head, first, second, out_weight, near_weight, far_weight)
    own = term(stage).astype(BF16)
    thirds = (got_left3, got_left2, got_right2, got_right3)
    arrived = (got_right2, got_right3, got_left2, got_left3)
    return final_sum(order, thirds, early, own, arrived, near_weight, far_weight)


def fast_per_device(
    query_rows, key_rows, value_rows, short_weight, skip_gain, filter_taps, out_weight
):
    span, chans = query_rows.shape
    blocks, stages = lax.axis_size("ctx"), lax.axis_size("tp")
    lanes = chans // blocks
    length = span * blocks
    radix = 2 * length // SUB
    place, stage = lax.axis_index("ctx"), lax.axis_index("tp")
    me = place.astype(jnp.int32).reshape(1)
    far = jnp.where(stage == 0, stages - 1, 0)
    spot = jnp.stack([place, stage, stages - 1 + 0 * stage, far]).astype(jnp.int32)
    forward, inverse = (jnp.asarray(t) for t in dft_tables(2 * length))
    twiddle = jnp.asarray(twiddle_table(radix))
    edges = jnp.concatenate([x[-2:] for x in (query_rows, key_rows, value_rows)])
    edges = passed_along(edges, "ctx", 1)
    taps = exchange(split_taps(me, filter_taps, blocks), "ctx")
    gated = exchange(gate_in(me, key_rows, value_rows, edges, short_weight, blocks), "ctx")
    weight_part = weight_rows(out_weight, stages)
    mixed = mix_query(query_rows, edges, short_weight)
    skip = lax.dynamic_slice(skip_gain, (place * lanes,), (lanes,)).reshape(1, lanes)
    spectra = taps_spectra_of(me, taps, twiddle, forward)
    convs = long_conv(me, gated, spectra, twiddle, forward, inverse, skip)
    convs = exchange(convs, "ctx")
    weight_part, *convs = lax.optimization_barrier((weight_part, *convs))
    return project(spot, convs, mixed, out_weight, weight_part)


def per_device(*arrays):
    span, chans = arrays[0].shape
    blocks = lax.axis_size("ctx")
    suits = blocks == 8 and lax.axis_size("tp") == 4 and span == 512 and chans == 8 * SUB
    return (fast_per_device if suits else general_per_device)(*arrays)


def solution(mesh):
    placed = (
        P("ctx", "tp"),
        P("ctx", "tp"),
        P("ctx", "tp"),
        P(None, None, "tp"),
        P("tp"),
        P("tp", "ctx"),
        P("tp", None),
    )
    return jax.shard_map(
        per_device, mesh=mesh, in_specs=placed, out_specs=P("ctx", "tp"), check_vma=False
    )
```

```python
from functools import partial
import math

import jax
import jax.numpy as jnp
import numpy as np
from jax import lax
from jax.experimental import pallas as pl
from jax.experimental.pallas import tpu as pltpu
from jax.sharding import PartitionSpec as P

TRIPLE = lax.Precision.HIGH


def passed_along(block, axis, distance):
    devices = range(lax.axis_size(axis))
    route = [(i - distance, i) for i in devices if i - distance in devices]
    return lax.ppermute(block, axis, route)


def angle_table(left, right, offset, period):
    rows = lax.broadcasted_iota(jnp.int32, (left, right), 0)
    cols = lax.broadcasted_iota(jnp.int32, (left, right), 1) + offset
    turns = rows * cols % period
    return turns.astype(jnp.float32) * (2.0 * math.pi / period)


def inner_spectrum(rows, table_high, table_low):
    upper = jnp.dot(rows, table_high, preferred_element_type=jnp.float32)
    lower = jnp.dot(rows, table_low, preferred_element_type=jnp.float32)
    return upper + lower


def block_mix(real_component, imaginary_component, cosine_lookup, sine_lookup, sign):
    multiplier = partial(jnp.einsum, precision=TRIPLE, preferred_element_type=jnp.float32)
    cosine_real = multiplier("id,rdy->riy", cosine_lookup, real_component)
    cosine_imaginary = multiplier("id,rdy->riy", cosine_lookup, imaginary_component)
    sine_real = multiplier("id,rdy->riy", sine_lookup, real_component)
    sine_imaginary = multiplier("id,rdy->riy", sine_lookup, imaginary_component)
    return (cosine_real + sign * sine_imaginary, cosine_imaginary - sign * sine_real)


def general_per_device(query_rows, key_rows, value_rows, short_weight, skip_gain, filter_taps, out_weight):
    span = query_rows.shape[0]
    chans = query_rows.shape[1]
    blocks = lax.axis_size("ctx")
    group = chans // blocks
    period = 2 * span
    padded = 2 * blocks
    forward = angle_table(span, period, 0, period)
    forward = jnp.concatenate([jnp.cos(forward), -jnp.sin(forward)], axis=1)
    table_high = forward.astype(jnp.bfloat16)
    table_low = (forward - table_high.astype(jnp.float32)).astype(jnp.bfloat16)
    parity = 1.0 - 2.0 * (jnp.arange(period) % 2).astype(jnp.float32)
    parity = jnp.concatenate([parity, parity])
    stacked = jnp.stack([query_rows, key_rows, value_rows])
    rims = passed_along(stacked[:, -2:, :], "ctx", 1)
    extended = jnp.concatenate([rims, stacked], axis=1).astype(jnp.float32)
    mixed = (
        short_weight[0][:, None, :] * extended[:, 2:]
        + short_weight[1][:, None, :] * extended[:, 1:-1]
        + short_weight[2][:, None, :] * extended[:, :span]
    )
    gated_in = (mixed[1] * mixed[2]).astype(jnp.bfloat16)
    gated_t = gated_in.T
    inputs_local, taps_local = (
        lax.all_to_all(gated_t, "ctx", split_axis=0, concat_axis=1, tiled=True),
        lax.all_to_all(filter_taps, "ctx", split_axis=0, concat_axis=1, tiled=True),
    )
    spectra = inner_spectrum(
        taps_local.reshape(group * blocks, span), table_high, table_low
    ).reshape(group, blocks, 2 * period)
    earlier = jnp.concatenate(
        [jnp.zeros((group, 1, 2 * period), jnp.float32), spectra[:, :-1]], axis=1
    )
    kernel_spec = earlier + parity * spectra
    input_spec = inner_spectrum(
        inputs_local.reshape(group * blocks, span), table_high, table_low
    ).reshape(group, blocks, 2 * period)
    block_angle = angle_table(padded, blocks, 0, padded)
    cos_fwd = jnp.cos(block_angle)
    sin_fwd = jnp.sin(block_angle)
    input_re, input_im = block_mix(
        input_spec[..., :period], input_spec[..., period:], cos_fwd, sin_fwd, 1.0
    )
    kernel_re, kernel_im = block_mix(
        kernel_spec[..., :period], kernel_spec[..., period:], cos_fwd, sin_fwd, 1.0
    )
    product_re = input_re * kernel_re - input_im * kernel_im
    product_im = input_re * kernel_im + input_im * kernel_re
    back_angle = angle_table(blocks, padded, 0, padded)
    out_re, out_im = block_mix(
        product_re, product_im, jnp.cos(back_angle), jnp.sin(back_angle), -1.0
    )
    inverse = angle_table(period, span, span, period)
    inverse = jnp.concatenate([jnp.cos(inverse), -jnp.sin(inverse)], axis=0) * (
        1.0 / (period * padded)
    )
    joined = jnp.concatenate([out_re, out_im], axis=2).reshape(group * blocks, 2 * period)
    long_local = jnp.dot(
        joined, inverse, precision=TRIPLE, preferred_element_type=jnp.float32
    ).reshape(group, blocks * span)
    long_t = lax.all_to_all(
        long_local.astype(jnp.bfloat16), "ctx", split_axis=1, concat_axis=0, tiled=True
    ).astype(long_local.dtype)
    conv_t = (long_t + skip_gain[:, None] * gated_t.astype(jnp.float32)).astype(jnp.bfloat16)
    gated_out = (mixed[0].T * conv_t.astype(jnp.float32)).astype(jnp.bfloat16)
    term = lax.dot_general(
        gated_out, out_weight, (((0,), (0,)), ((), ())), preferred_element_type=jnp.float32
    )
    return lax.psum_scatter(term.astype(jnp.bfloat16), "tp", scatter_dimension=1, tiled=True)


SUB = 128
F32 = jnp.float32
BF16 = jnp.bfloat16


def split_table(matrix):
    high = matrix.astype(jnp.bfloat16)
    low = (matrix - high.astype(np.float32)).astype(jnp.bfloat16)
    return np.concatenate([high, high, low], axis=1)


def dft_tables(period):
    index = np.arange(SUB)
    turns = np.outer(index, index) % SUB * (2.0 * np.pi / SUB)
    cos, sin = np.cos(turns), np.sin(turns)
    forward = np.block([[cos, sin], [-sin, cos]]).astype(np.float32)
    inverse = (np.block([[cos, -sin], [sin, cos]]) / period).astype(np.float32)
    return split_table(forward), split_table(inverse)


def twiddle_table(radix):
    half = radix // 2
    turns = np.outer(np.arange(SUB), np.arange(half + 1)) * (2.0 * np.pi / (radix * SUB))
    return np.concatenate([np.cos(turns), -np.sin(turns)], axis=1).astype(np.float32)


def times(value, factor):
    return None if value is None else value * factor


def plus(left, right):
    if left is None:
        return right
    return left if right is None else left + right


def minus(left, right):
    if right is None:
        return left
    return -right if left is None else left - right


def rotate(value, turn):
    real, imag = value
    cos, sin = math.cos(2 * math.pi * turn), math.sin(2 * math.pi * turn)
    if abs(cos - sin) < 1e-12 and imag is not None:
        return (real + imag) * cos, (imag - real) * cos
    return plus(times(real, cos), times(imag, sin)), minus(times(imag, cos), times(real, sin))


def real_forward(values):
    points = 2 * len(values)
    if points == 2:
        return [(values[0], None), (values[0], None)]
    even, odd = real_forward(values[0::2]), real_forward(values[1::2])
    bins = [None] * (points // 2 + 1)
    bins[0] = (even[0][0] + odd[0][0], None)
    bins[points // 2] = (even[0][0] - odd[0][0], None)
    quarter = points // 4
    for k in range(1, quarter):
        turned = rotate(odd[k], k / points)
        bins[k] = (even[k][0] + turned[0], even[k][1] + turned[1])
        bins[points // 2 - k] = (even[k][0] - turned[0], turned[1] - even[k][1])
    bins[quarter] = (even[quarter][0], -odd[quarter][0])
    return bins


def real_inverse(bins):
    half = len(bins) - 1
    points = 2 * half
    if points == 2:
        return [bins[0][0] + bins[1][0]]
    even, odd = [], []
    for k in range(half // 2 + 1):
        ahead, back = bins[k], bins[half - k]
        if k == 0:
            even.append((ahead[0] + back[0], None))
            odd.append((ahead[0] - back[0], None))
        elif k == half // 2:
            even.append((ahead[0] * 2.0, None))
            odd.append((ahead[1] * -2.0, None))
        else:
            even.append((ahead[0] + back[0], ahead[1] - back[1]))
            difference = (ahead[0] - back[0], ahead[1] + back[1])
            odd.append(rotate(difference, -k / points))
    even, odd = real_inverse(even), real_inverse(odd)
    return [value for pair in zip(even, odd) for value in pair]


def split_dot(table, data):
    high = data.astype(BF16)
    low = (data - high.astype(F32)).astype(BF16)
    return jnp.dot(
        table[...], jnp.concatenate([high, low, high], axis=0), preferred_element_type=F32
    )


def first_stage(series, spectra, twiddle):
    half = series.shape[0] // SUB
    lanes = series.shape[1]

    def slab(step, carry):
        row = pl.multiple_of(step * 8, 8)
        values = [series[pl.ds(SUB * n + row, 8), :] for n in range(half)]
        factors = twiddle[pl.ds(row, 8), :]
        for k, (real, imag) in enumerate(real_forward(values)):
            if k == 0:
                spectra[0, pl.ds(row, 8), :] = real
                spectra[0, pl.ds(SUB + row, 8), :] = jnp.zeros_like(real)
                continue
            cos = jnp.broadcast_to(factors[:, k : k + 1], (8, lanes))
            sin = jnp.broadcast_to(factors[:, half + 1 + k : half + 2 + k], (8, lanes))
            if imag is None:
                spectra[k, pl.ds(row, 8), :] = real * cos
                spectra[k, pl.ds(SUB + row, 8), :] = real * sin
            else:
                spectra[k, pl.ds(row, 8), :] = real * cos - imag * sin
                spectra[k, pl.ds(SUB + row, 8), :] = real * sin + imag * cos
        return carry

    lax.fori_loop(0, SUB // 8, slab, 0)
    for k in range(half + 1, spectra.shape[0]):
        spectra[k] = jnp.zeros(spectra.shape[1:], F32)


def last_stage(spectra, series):
    half = series.shape[0] // SUB

    def slab(step, carry):
        row = pl.multiple_of(step * 8, 8)
        bins = []
        for k in range(half + 1):
            real = spectra[k, pl.ds(row, 8), :]
            imag = None if k in (0, half) else spectra[k, pl.ds(SUB + row, 8), :]
            bins.append((real, imag))
        for n, value in enumerate(real_inverse(bins)):
            series[pl.ds(SUB * n + row, 8), :] = value
        return carry

    lax.fori_loop(0, SUB // 8, slab, 0)


def taps_kernel(chips, me_ref, *refs):
    pairs, (swapped, twiddle, forward, spectra_out, series, spectra) = refs[:chips], refs[chips:]
    _, lanes, span = swapped.shape
    mine = pl.ds(pl.multiple_of(me_ref[0] % 2 * lanes, lanes), lanes)
    for q in range(chips):
        for m, piece in ((2 * q, pairs[q][mine, :]), (2 * q + 1, swapped[q])):
            start = pl.multiple_of((me_ref[0] ^ m) * span, span)
            series[pl.ds(start, span), :] = piece.astype(F32).T
    first_stage(series, spectra, twiddle)

    def pair(p, carry):
        data = jnp.concatenate([spectra[2 * p], spectra[2 * p + 1]], axis=1)
        spectra_out[p] = split_dot(forward, data)
        return carry

    lax.fori_loop(0, spectra_out.shape[0], pair, 0)


def conv_kernel(blocks, me_ref, stay, swapped, *refs):
    others = refs[: blocks // 2 - 1]
    taps_spectra, twiddle, forward, inverse, skip = refs[blocks // 2 - 1 : blocks // 2 + 4]
    out, series, spectra = refs[blocks // 2 + 4 :]
    span, lanes = stay.shape
    half = series.shape[0] // SUB
    pieces = [stay, swapped.at[0]] + [ref.at[core] for ref in others for core in range(2)]
    for m in range(blocks):
        start = pl.multiple_of((me_ref[0] ^ m) * span, span)
        series[pl.ds(start, span), :] = pieces[m][...].astype(F32)
    first_stage(series, spectra, twiddle)

    def pair(p, carry):
        data = jnp.concatenate([spectra[2 * p], spectra[2 * p + 1]], axis=1)
        signal = split_dot(forward, data)
        signal_re, signal_im = signal[:SUB], signal[SUB:]
        taps_re, taps_im = taps_spectra[p, :SUB, :], taps_spectra[p, SUB:, :]
        product = jnp.concatenate(
            [
                signal_re * taps_re - signal_im * taps_im,
                signal_re * taps_im + signal_im * taps_re,
            ],
            axis=0,
        )
        back = split_dot(inverse, product)
        spectra[2 * p] = back[:, :lanes]
        spectra[2 * p + 1] = back[:, lanes:]
        return carry

    lax.fori_loop(0, taps_spectra.shape[0], pair, 0)
    for k in range(1, half + 1):
        real, imag = spectra[k, :SUB, :], spectra[k, SUB:, :]
        cos = jnp.broadcast_to(twiddle[:, k : k + 1], (SUB, lanes))
        sin = jnp.broadcast_to(twiddle[:, half + 1 + k : half + 2 + k], (SUB, lanes))
        spectra[k, :SUB, :] = real * cos + imag * sin
        if k < half:
            spectra[k, SUB:, :] = imag * cos - real * sin
    last_stage(spectra, out)
    for m in range(blocks):
        window = pl.ds(m * span, span)
        out[window, :] += skip[...] * series[window, :]


def spread_kernel(me_ref, conv, *outs):
    span = outs[0].shape[0]
    for m, out in enumerate(outs):
        start = pl.multiple_of((me_ref[0] ^ m) * span, span)
        out[...] = conv[pl.ds(start, span), :].astype(BF16)


VMEM = pl.BlockSpec(memory_space=pltpu.VMEM)
SMEM = pl.BlockSpec(memory_space=pltpu.SMEM)
HBM = pl.BlockSpec(memory_space=pltpu.HBM)


def grant(mebibytes):
    return pltpu.CompilerParams(vmem_limit_bytes=mebibytes * 2**20)


def cost(microseconds):
    return pl.CostEstimate(flops=microseconds * 10**9, bytes_accessed=0, transcendentals=0)


GRANT = grant(16)


def taps_spectra_of(me, pairs, swapped, twiddle, forward):
    chips, lanes, span = swapped.shape
    length = 2 * chips * span
    count = (length // SUB + 2) // 2
    return pl.pallas_call(
        partial(taps_kernel, chips),
        out_shape=jax.ShapeDtypeStruct((count, 2 * SUB, 2 * lanes), F32),
        in_specs=[SMEM] + [VMEM] * (chips + 3),
        out_specs=VMEM,
        scratch_shapes=[
            pltpu.VMEM((length, lanes), F32),
            pltpu.VMEM((2 * count, 2 * SUB, lanes), F32),
        ],
        compiler_params=GRANT,
        cost_estimate=cost(8),
        name="taps_spectra",
    )(me, *pairs, swapped, twiddle, forward)


def long_conv(me, stay, swapped, others, taps_spectra, twiddle, forward, inverse, skip):
    span, lanes = stay.shape
    blocks = 2 * len(others) + 2
    pairs = taps_spectra.shape[0]
    return pl.pallas_call(
        partial(conv_kernel, blocks),
        out_shape=jax.ShapeDtypeStruct((blocks * span, lanes), F32),
        in_specs=[SMEM] + [VMEM] * (len(others) + 7),
        out_specs=VMEM,
        scratch_shapes=[
            pltpu.VMEM((blocks * span, lanes), F32),
            pltpu.VMEM((2 * pairs, 2 * SUB, lanes), F32),
        ],
        compiler_params=grant(20),
        cost_estimate=cost(20),
        name="long_conv",
    )(me, stay, swapped, *others, taps_spectra, twiddle, forward, inverse, skip)


def spread(me, conv, blocks):
    rows, lanes = conv.shape
    return pl.pallas_call(
        spread_kernel,
        out_shape=[jax.ShapeDtypeStruct((rows // blocks, lanes), BF16)] * blocks,
        in_specs=[SMEM, VMEM],
        out_specs=[VMEM] * blocks,
        compiler_params=GRANT,
        name="spread",
    )(me, conv)


def shifted_mix(stream, edge, weight):
    row = lax.broadcasted_iota(jnp.int32, stream.shape, 0)
    first = jnp.where(row == 0, edge[1:2], pltpu.roll(stream, 1, 0))
    second = pltpu.roll(stream, 2, 0)
    second = jnp.where(row == 0, edge[0:1], jnp.where(row == 1, edge[1:2], second))
    return weight[0:1] * stream + weight[1:2] * first + weight[2:3] * second


def rims_kernel(query, key, value, out, held, sems):
    span = query.shape[0]
    copies = [
        pltpu.make_async_copy(ref.at[pl.ds(span - 16, 16), :], held.at[s], sems.at[s])
        for s, ref in enumerate((query, key, value))
    ]
    for copy in copies:
        copy.start()
    for s, copy in enumerate(copies):
        copy.wait()
        out[2 * s : 2 * s + 2, :] = held[s, 14:16, :]


def rims(*streams):
    chans = streams[0].shape[1]
    return pl.pallas_call(
        rims_kernel,
        in_specs=[HBM] * 3,
        out_specs=VMEM,
        out_shape=jax.ShapeDtypeStruct((6, chans), BF16),
        scratch_shapes=[pltpu.VMEM((3, 16, chans), BF16), pltpu.SemaphoreType.DMA((3,))],
        compiler_params=grant(56),
        name="rims",
    )(*streams)


def gate_in_kernel(me_ref, key, value, edges, weight, stay, same, swap, held, sems):
    lanes = stay.shape[1]
    chips = swap.shape[0]
    mine = me_ref[0] % 2
    copies = []
    for q in range(chips):
        start = pl.multiple_of(((me_ref[0] // 2) ^ q) * 2 * lanes, 2 * lanes)
        for s, ref in enumerate((key, value)):
            source = ref.at[:, pl.ds(start, 2 * lanes)]
            copies.append(pltpu.make_async_copy(source, held.at[q, s], sems.at[q, s]))
            copies[-1].start()
    for q in range(chips):
        start = ((me_ref[0] // 2) ^ q) * 2 * lanes
        for copy in copies[2 * q : 2 * q + 2]:
            copy.wait()
        for side in range(2):
            inner = pl.ds(pl.multiple_of((mine ^ side) * lanes, lanes), lanes)
            outer = pl.ds(pl.multiple_of(start + (mine ^ side) * lanes, lanes), lanes)
            mixed = [
                shifted_mix(
                    held[q, s, :, inner].astype(F32),
                    edges[2 * s + 2 : 2 * s + 4, outer].astype(F32),
                    weight[:, s + 1, outer],
                )
                for s in range(2)
            ]
            gated = (mixed[0] * mixed[1]).astype(BF16)
            if side:
                swap[q] = gated
            elif q:
                same[q - 1] = gated
            else:
                stay[...] = gated


def gate_in(me, key_rows, value_rows, edges, short_weight, blocks):
    span, chans = key_rows.shape
    lanes = chans // blocks
    chips = blocks // 2
    shapes = [(span, lanes), (chips - 1, span, lanes), (chips, span, lanes)]
    return pl.pallas_call(
        gate_in_kernel,
        in_specs=[SMEM, HBM, HBM, VMEM, VMEM],
        out_specs=[VMEM] * 3,
        out_shape=[jax.ShapeDtypeStruct(shape, BF16) for shape in shapes],
        scratch_shapes=[
            pltpu.VMEM((chips, 2, span, 2 * lanes), BF16),
            pltpu.SemaphoreType.DMA((chips, 2)),
        ],
        compiler_params=grant(56),
        name="gate_in",
    )(me, key_rows, value_rows, edges, short_weight)


def split_taps_kernel(me_ref, taps, *refs):
    outs, sems = refs[:-1], refs[-1]
    rows = outs[0].shape[0]
    copies = []
    for q, out in enumerate(outs):
        window = pl.ds(pl.multiple_of(((me_ref[0] // 2) ^ q) * rows, rows), rows)
        copies.append(pltpu.make_async_copy(taps.at[window, :], out, sems.at[q]))
        copies[-1].start()
    for copy in copies:
        copy.wait()


def split_taps(me, filter_taps, chips):
    chans, span = filter_taps.shape
    return pl.pallas_call(
        split_taps_kernel,
        in_specs=[SMEM, HBM],
        out_specs=[VMEM] * chips,
        out_shape=[jax.ShapeDtypeStruct((chans // chips, span), BF16)] * chips,
        scratch_shapes=[pltpu.SemaphoreType.DMA((chips,))],
        compiler_params=GRANT,
        name="split_taps",
    )(me, filter_taps)


def other_core_kernel(me_ref, *refs):
    pairs, out = refs[:-1], refs[-1]
    rows = out.shape[1]
    for q, pair in enumerate(pairs):
        window = pl.ds(pl.multiple_of((1 - me_ref[0] % 2) * rows, rows), rows)
        out[q] = pair[window, :]


def other_core(me, pairs):
    rows, span = pairs[0].shape
    return pl.pallas_call(
        other_core_kernel,
        in_specs=[SMEM] + [VMEM] * len(pairs),
        out_specs=VMEM,
        out_shape=jax.ShapeDtypeStruct((len(pairs), rows // 2, span), BF16),
        compiler_params=GRANT,
        name="other_core",
    )(me, *pairs)


def pair_kernel(same, swapped, *outs):
    for q, out in enumerate(outs):
        out[0] = same[q]
        out[1] = swapped[q + 1]


def pair_up(same, swapped):
    count, span, lanes = same.shape
    return pl.pallas_call(
        pair_kernel,
        out_shape=[jax.ShapeDtypeStruct((2, span, lanes), BF16)] * count,
        in_specs=[VMEM] * 2,
        out_specs=[VMEM] * count,
        compiler_params=GRANT,
        name="pair_up",
    )(same, swapped)


def mix_query_kernel(query, edges, weight, out):
    out[...] = shifted_mix(query[...].astype(F32), edges[0:2].astype(F32), weight[:, 0, :])


def mix_query(query_rows, edges, short_weight):
    span, chans = query_rows.shape
    lanes = chans // 4
    return pl.pallas_call(
        mix_query_kernel,
        grid=(4,),
        in_specs=[
            pl.BlockSpec((span, lanes), lambda g: (0, g)),
            pl.BlockSpec((6, lanes), lambda g: (0, g)),
            pl.BlockSpec((3, 3, lanes), lambda g: (0, 0, g)),
        ],
        out_specs=pl.BlockSpec((span, lanes), lambda g: (0, g)),
        out_shape=jax.ShapeDtypeStruct((span, chans), F32),
        compiler_params=GRANT,
        name="mix_query",
    )(query_rows, edges, short_weight)


def exchange(pieces, axis):
    devices = range(lax.axis_size(axis))
    return [pieces[0]] + [
        lax.ppermute(piece, axis, [(i, i ^ m) for i in devices])
        for m, piece in enumerate(pieces)
        if m
    ]


def after(values, others):
    return lax.optimization_barrier((values, others))[0]


HEAD, PASS, ADD = 0, 1, 2
SENT = np.array(
    [
        (HEAD, ADD, ADD, 2, 1),
        (ADD, PASS, ADD, 3, 2),
        (PASS, ADD, PASS, 3, 3),
        (PASS, PASS, PASS, 3, 3),
    ],
    np.int32,
)


def gate_out_kernel(blocks, spot, *refs):
    convs, (mixed, far_weight, gated, sent) = refs[:blocks], refs[blocks:]
    lanes = convs[0].shape[1]
    rows = gated.shape[1]
    for m in range(blocks):
        window = pl.ds(pl.multiple_of((spot[0] ^ m) * lanes, lanes), lanes)
        piece = (mixed[:, window] * convs[m][...].astype(F32)).astype(BF16)
        gated[0, :, window] = piece[:rows]
        gated[1, :, window] = piece[rows:]
    first_sent(spot, gated, far_weight, sent)


def first_sent(spot, gated, far_weight, sent):
    @pl.when(spot[1] == 0)
    def _():
        term = jnp.dot(gated[1], far_weight[...], preferred_element_type=F32)
        sent[...] = term.astype(BF16)

    @pl.when(spot[1] != 0)
    def _():
        sent[...] = gated[0]


def gate_out(spot, convs, mixed, far_weight):
    span, chans = mixed.shape
    return pl.pallas_call(
        partial(gate_out_kernel, len(convs)),
        in_specs=[SMEM] + [VMEM] * (len(convs) + 2),
        out_specs=[VMEM] * 2,
        out_shape=[
            jax.ShapeDtypeStruct((2, span // 2, chans), BF16),
            jax.ShapeDtypeStruct((span // 2, chans), BF16),
        ],
        compiler_params=GRANT,
        name="gate_out",
    )(spot, *convs, mixed, far_weight)


def partner_sent(spot, gated, far_weight):
    return pl.pallas_call(
        first_sent,
        in_specs=[SMEM, VMEM, VMEM],
        out_specs=VMEM,
        out_shape=jax.ShapeDtypeStruct(gated.shape[1:], BF16),
        compiler_params=GRANT,
        cost_estimate=cost(1),
        name="partner_sent",
    )(spot, gated, far_weight)


def step_kernel(step, plan, head, term, got, out):
    mode = plan[step - 1]

    @pl.when(mode == HEAD)
    def _():
        out[...] = head[...]

    @pl.when(mode == PASS)
    def _():
        out[...] = got[...]

    @pl.when(mode == ADD)
    def _():
        out[...] = (term[...].astype(F32) + got[...].astype(F32)).astype(BF16)


def next_step(plan, step, chain, gated, terms, got):
    rows, chans = got.shape
    whole = pl.BlockSpec((rows, chans), lambda g, plan: (0, 0))
    return pl.pallas_call(
        partial(step_kernel, step),
        grid_spec=pltpu.PrefetchScalarGridSpec(
            num_scalar_prefetch=1,
            grid=(1,),
            in_specs=[
                pl.BlockSpec((None, rows, chans), lambda g, plan: (0, 0, 0)),
                pl.BlockSpec(
                    (None, None, rows, chans), lambda g, plan: (chain, step // 3, 0, 0)
                ),
                whole,
            ],
            out_specs=whole,
        ),
        out_shape=jax.ShapeDtypeStruct((rows, chans), BF16),
        compiler_params=GRANT,
        cost_estimate=cost(1),
        name="next_step",
    )(plan, gated, terms, got)


def terms_kernel(plan, mine, partners, weight, out, held, sems):
    count, chans = held.shape[:2]
    copies = []
    for k in range(count):
        columns = pl.ds(pl.multiple_of(plan[3 + k] * chans, chans), chans)
        copies.append(pltpu.make_async_copy(weight.at[:, columns], held.at[k], sems.at[k]))
        copies[-1].start()
    for k, copy in enumerate(copies):
        copy.wait()
        for chain, gated in enumerate((mine, partners)):
            term = jnp.dot(gated[1], held[k], preferred_element_type=F32)
            out[chain, k] = term.astype(BF16)


def sent_terms(plan, mine, partners, out_weight):
    _, rows, chans = mine.shape
    return pl.pallas_call(
        terms_kernel,
        in_specs=[SMEM, VMEM, VMEM, HBM],
        out_specs=VMEM,
        out_shape=jax.ShapeDtypeStruct((2, 2, rows, chans), BF16),
        scratch_shapes=[pltpu.VMEM((2, chans, chans), BF16), pltpu.SemaphoreType.DMA((2,))],
        compiler_params=GRANT,
        cost_estimate=cost(4),
        name="sent_terms",
    )(plan, mine, partners, out_weight)


def spread_weight(out_weight, ready):
    stages, blocks = lax.axis_size("tp"), lax.axis_size("ctx")
    stage, place = lax.axis_index("tp"), lax.axis_index("ctx")
    chans = out_weight.shape[0]
    hops = jnp.where(place % 2 == 0, 1, stages - 1)
    found = []
    for rows, row, hop, static in (
        (2 * chans // blocks, place // 2, hops, (1, stages - 1)),
        (chans // blocks, place, 2 + 0 * place, (2, 2)),
    ):
        start = after((row * rows, (stage + hop) % stages * chans), ready)
        part = lax.dynamic_slice(out_weight, start, (rows, chans))
        route = [
            (c * stages + k, c * stages + (k + static[c % 2]) % stages)
            for c in range(blocks)
            for k in range(stages)
        ]
        found.append(lax.ppermute(part, ("ctx", "tp"), route))
    return found


def gather_weight(part):
    devices = range(lax.axis_size("ctx"))
    near = [(i, i ^ (4 if i & 1 else 2)) for i in devices]
    other = [(i, i ^ (2 if i & 1 else 4)) for i in devices]
    two = [part, lax.ppermute(part, "ctx", near)]
    return jnp.stack(two), jnp.stack([lax.ppermute(x, "ctx", other) for x in two])


def pairs_of(refs):
    return list(zip(refs[::2], refs[1::2]))


def spots(first, pair):
    return (first, pair[0]), (first + 2, pair[1])


def add_parts(order, data, *weights):
    total = None
    for first, weight in weights:
        count, lanes, columns = weight.shape
        picked = []
        for q in range(count):
            index = order[first + q]
            index = index // 2 if lanes == 2 * SUB else index
            picked.append(data[:, pl.ds(pl.multiple_of(index * lanes, lanes), lanes)])
        block = weight[...].reshape(count * lanes, columns)
        picked = jnp.concatenate(picked, axis=1)
        term = jnp.dot(picked, block, preferred_element_type=F32)
        total = term if total is None else total + term
    return total


def early_kernel(order, mine, got0, got1, partner0, partner1, weight, *refs):
    (near, near2, far2), (out, own, first, own_weight, sem) = pairs_of(refs[:6]), refs[6:]
    turn_count = order[8]
    rows, chans = got0.shape
    columns = pl.ds(pl.multiple_of(order[9] * chans, chans), chans)
    copy = pltpu.make_async_copy(weight.at[:, columns], own_weight, sem)
    copy.start()

    @pl.when(turn_count >= 2)
    def _():
        first[:rows, :] = got0[...]
        first[rows:, :] = partner0[...]

    @pl.when(turn_count < 2)
    def _():
        first[:rows, :] = got1[...]
        first[rows:, :] = partner1[...]

    @pl.when(turn_count >= 1)
    def _():
        out[...] = add_parts(order, first, *spots(0, near))

    @pl.when(turn_count < 1)
    def _():
        out[...] = jnp.zeros_like(out)

    @pl.when(turn_count == 3)
    def _():
        first[:rows, :] = got1[...]
        first[rows:, :] = partner1[...]
        out[...] += add_parts(order, first, *spots(0, near2), *spots(4, far2))

    copy.wait()
    out[:rows, :] += jnp.dot(mine[0], own_weight[...], preferred_element_type=F32)
    own[...] = jnp.dot(mine[1], own_weight[...], preferred_element_type=F32)


def early_sum(order, mine, arrivals, out_weight, weights):
    _, rows, chans = mine.shape
    whole = lambda shape: pl.BlockSpec(shape, lambda g, order: (0,) * len(shape))
    return pl.pallas_call(
        early_kernel,
        grid_spec=pltpu.PrefetchScalarGridSpec(
            num_scalar_prefetch=1,
            grid=(1,),
            in_specs=[whole(mine.shape)]
            + [whole((rows, chans))] * 4
            + [HBM]
            + [whole(x.shape) for x in weights],
            out_specs=[whole((2 * rows, chans)), whole((rows, chans))],
            scratch_shapes=[
                pltpu.VMEM((2 * rows, chans), BF16),
                pltpu.VMEM((chans, chans), BF16),
                pltpu.SemaphoreType.DMA,
            ],
        ),
        out_shape=[
            jax.ShapeDtypeStruct((2 * rows, chans), F32),
            jax.ShapeDtypeStruct((rows, chans), F32),
        ],
        compiler_params=grant(24),
        cost_estimate=cost(5),
        name="early_sum",
    )(order, mine, *arrivals, out_weight, *weights)


def late_sum(order, early, got2, got3, weights, total):
    behind = order[8]

    @pl.when(behind < 2)
    def _():
        total[...] = early[...]

    @pl.when(behind == 2)
    def _():
        total[...] = early[...] + add_parts(order, got2, *spots(0, weights[0]), *spots(4, weights[1]))

    @pl.when(behind == 3)
    def _():
        total[...] = early[...] + add_parts(order, got3, *spots(4, weights[2]))

    summed = jnp.where(behind == 3, got2[...].astype(F32), got3[...].astype(F32))
    return jnp.where(behind == 0, 0.0, summed)


def partner_kernel(order, early, got2, got3, *refs):
    weights, (out, total) = pairs_of(refs[:6]), refs[6:]
    out[1] = late_sum(order, early, got2, got3, weights, total).astype(BF16)
    out[0] = total[...].astype(BF16)


def partner_sum(order, early, arrivals, weights):
    rows, chans = arrivals[0].shape
    whole = lambda shape: pl.BlockSpec(shape, lambda g, order: (0,) * len(shape))
    return pl.pallas_call(
        partner_kernel,
        grid_spec=pltpu.PrefetchScalarGridSpec(
            num_scalar_prefetch=1,
            grid=(1,),
            in_specs=[pl.BlockSpec((rows, chans), lambda g, order: (1, 0))]
            + [whole((rows, chans))] * 2
            + [whole(x.shape) for x in weights],
            out_specs=whole((2, rows, chans)),
            scratch_shapes=[pltpu.VMEM((rows, chans), F32)],
        ),
        out_shape=jax.ShapeDtypeStruct((2, rows, chans), BF16),
        compiler_params=grant(24),
        cost_estimate=cost(2),
        name="partner_sum",
    )(order, early, *arrivals, *weights)


def mine_kernel(order, early, own, got2, got3, *refs):
    weights, (out, total) = pairs_of(refs[:6]), refs[6:]
    rows = early.shape[0]
    out[rows:, :] = late_sum(order, early, got2, got3, weights, total) + own[...]
    out[:rows, :] = total[...]


def mine_sum(order, early, own, arrivals, weights):
    rows, chans = arrivals[0].shape
    whole = lambda shape: pl.BlockSpec(shape, lambda g, order: (0,) * len(shape))
    return pl.pallas_call(
        mine_kernel,
        grid_spec=pltpu.PrefetchScalarGridSpec(
            num_scalar_prefetch=1,
            grid=(1,),
            in_specs=[pl.BlockSpec((rows, chans), lambda g, order: (0, 0))]
            + [whole((rows, chans))] * 3
            + [whole(x.shape) for x in weights],
            out_specs=whole((2 * rows, chans)),
            scratch_shapes=[pltpu.VMEM((rows, chans), F32)],
        ),
        out_shape=jax.ShapeDtypeStruct((2 * rows, chans), F32),
        compiler_params=grant(24),
        cost_estimate=cost(3),
        name="mine_sum",
    )(order, early, own, *arrivals, *weights)


def join_kernel(mine, partners, out):
    rows = partners.shape[1]
    for half in range(2):
        part = slice(half * rows, (half + 1) * rows)
        out[part, :] = (mine[part, :] + partners[half].astype(F32)).astype(BF16)


def join_sums(mine, partners):
    return pl.pallas_call(
        join_kernel,
        in_specs=[VMEM] * 2,
        out_specs=VMEM,
        out_shape=jax.ShapeDtypeStruct(mine.shape, BF16),
        compiler_params=GRANT,
        name="join_sums",
    )(mine, partners)


def weight_order():
    place, stage = lax.axis_index("ctx"), lax.axis_index("tp")
    up = place % 2 == 0
    last = lax.axis_size("tp") - 1
    a = jnp.where(up, 2, 4)
    masks = [0 * a, a, 6 - a, 0 * a + 6]
    swapped = [0 * a + 1, (6 - a) ^ 1, a ^ 1, 0 * a + 7]
    parts = [place ^ mask for mask in masks + swapped]
    return jnp.stack(parts + [jnp.where(up, stage, last - stage), stage]).astype(jnp.int32)


def project(spot, plan, order, convs, mixed, out_weight, weight_parts):
    stages, blocks = lax.axis_size("tp"), lax.axis_size("ctx")
    chans = out_weight.shape[0]
    far_weight = lax.dynamic_slice(out_weight, (0, spot[2] * chans), (chans, chans))
    mine, sent = gate_out(spot, convs, mixed, far_weight)
    route = []
    for c in range(blocks):
        for k in range(stages):
            to = k + (1 if c % 2 == 0 else -1)
            if 0 <= to < stages:
                route.append((c * stages + k, c * stages + to))
    onward = lambda x: lax.ppermute(x, ("ctx", "tp"), route)
    core_swap = lambda x: lax.ppermute(x, "ctx", [(i, i ^ 1) for i in range(blocks)])
    partners = core_swap(mine)
    partner_first = partner_sent(spot, partners, far_weight)
    got = [[onward(sent), onward(partner_first)]]
    terms = sent_terms(plan, mine, partners, out_weight)
    steps = []
    for step in range(1, stages):
        row = []
        for chain, gated in enumerate((mine, partners)):
            row.append(next_step(plan, step, chain, gated, terms, got[-1][chain]))
        steps.append(row)
        got.append([onward(x) for x in row])

    near, near2 = (gather_weight(part) for part in after(weight_parts, partner_first))
    far2, far = ([core_swap(x) for x in pair] for pair in (near2, near))
    arrivals = [got[0][0], got[1][0], got[0][1], got[1][1]]
    early, own = early_sum(order, mine, arrivals, out_weight, (*near, *near2, *far2))
    late = (*near2, *far2, *far)
    theirs = partner_sum(after(order, got[3][0]), early, [got[2][1], got[3][1]], late)
    ours = mine_sum(order, early, own, [got[2][0], got[3][0]], late)
    return join_sums(ours, core_swap(theirs))


def fast_per_device(
    query_rows, key_rows, value_rows, short_weight, skip_gain, filter_taps, out_weight
):
    span, chans = query_rows.shape
    blocks, stages = lax.axis_size("ctx"), lax.axis_size("tp")
    lanes = chans // blocks
    length = span * blocks
    radix = 2 * length // SUB
    place, stage = lax.axis_index("ctx"), lax.axis_index("tp")
    me = place.astype(jnp.int32).reshape(1)
    up = place % 2 == 0
    behind = jnp.where(up, stage, stages - 1 - stage)
    far = jnp.where(up, stages - 1, 0)
    spot = jnp.stack([place, behind, far]).astype(jnp.int32)
    plan = lax.dynamic_index_in_dim(jnp.asarray(SENT), behind, keepdims=False)
    plan = jnp.where(up | (jnp.arange(5) < 3), plan, stages - 1 - plan)
    me, spot, plan, order = lax.optimization_barrier((me, spot, plan, weight_order()))
    skip = lax.dynamic_slice(skip_gain, (place * lanes,), (lanes,)).reshape(1, lanes)
    forward, inverse = (jnp.asarray(t) for t in dft_tables(2 * length))
    twiddle = jnp.asarray(twiddle_table(radix))
    devices = range(blocks)
    core_swap = lambda x: lax.ppermute(x, "ctx", [(i, i ^ 1) for i in devices])
    to_chips = lambda xs: [
        lax.ppermute(x, "ctx", [(i, i ^ (2 * q + 2)) for i in devices])
        for q, x in enumerate(xs)
    ]
    edges = passed_along(rims(query_rows, key_rows, value_rows), "ctx", 1)
    pairs = split_taps(after(me, edges), filter_taps, blocks // 2)
    pairs = [pairs[0]] + to_chips(pairs[1:])
    stay, same, swap = gate_in(me, key_rows, value_rows, edges, short_weight, blocks)
    swapped = core_swap(swap)
    packed = pair_up(same, swapped)
    others = to_chips(packed)
    taps_swapped = core_swap(other_core(me, pairs))
    mixed = mix_query(query_rows, edges, short_weight)
    spectra = taps_spectra_of(me, pairs, taps_swapped, twiddle, forward)
    weight_parts = spread_weight(out_weight, taps_swapped)
    conv = long_conv(me, stay, swapped, others, spectra, twiddle, forward, inverse, skip)
    convs = exchange(spread(after(me, weight_parts), conv, blocks), "ctx")
    return project(spot, plan, order, convs, mixed, out_weight, weight_parts)


def per_device(*arrays):
    span, chans = arrays[0].shape
    blocks = lax.axis_size("ctx")
    suits = blocks == 8 and lax.axis_size("tp") == 4 and span == 512 and chans == 8 * SUB
    return (fast_per_device if suits else general_per_device)(*arrays)


def solution(mesh):
    placed = (
        P("ctx", "tp"),
        P("ctx", "tp"),
        P("ctx", "tp"),
        P(None, None, "tp"),
        P("tp"),
        P("tp", "ctx"),
        P("tp", None),
    )
    return jax.shard_map(
        per_device, mesh=mesh, in_specs=placed, out_specs=P("ctx", "tp"), check_vma=False
    )
```

```python
from functools import partial
import math

import jax
import jax.numpy as jnp
import numpy as np
from jax import lax
from jax.experimental import pallas as pl
from jax.experimental.pallas import tpu as pltpu
from jax.sharding import PartitionSpec as P

TRIPLE = lax.Precision.HIGH


def passed_along(block, axis, distance):
    devices = range(lax.axis_size(axis))
    route = [(i - distance, i) for i in devices if i - distance in devices]
    return lax.ppermute(block, axis, route)


def angle_table(left, right, offset, period):
    rows = lax.broadcasted_iota(jnp.int32, (left, right), 0)
    cols = lax.broadcasted_iota(jnp.int32, (left, right), 1) + offset
    turns = rows * cols % period
    return turns.astype(jnp.float32) * (2.0 * math.pi / period)


def inner_spectrum(rows, table_high, table_low):
    upper = jnp.dot(rows, table_high, preferred_element_type=jnp.float32)
    lower = jnp.dot(rows, table_low, preferred_element_type=jnp.float32)
    return upper + lower


def block_mix(real_component, imaginary_component, cosine_lookup, sine_lookup, sign):
    multiplier = partial(jnp.einsum, precision=TRIPLE, preferred_element_type=jnp.float32)
    cosine_real = multiplier("id,rdy->riy", cosine_lookup, real_component)
    cosine_imaginary = multiplier("id,rdy->riy", cosine_lookup, imaginary_component)
    sine_real = multiplier("id,rdy->riy", sine_lookup, real_component)
    sine_imaginary = multiplier("id,rdy->riy", sine_lookup, imaginary_component)
    return (cosine_real + sign * sine_imaginary, cosine_imaginary - sign * sine_real)


def general_per_device(query_rows, key_rows, value_rows, short_weight, skip_gain, filter_taps, out_weight):
    span = query_rows.shape[0]
    chans = query_rows.shape[1]
    blocks = lax.axis_size("ctx")
    group = chans // blocks
    period = 2 * span
    padded = 2 * blocks
    forward = angle_table(span, period, 0, period)
    forward = jnp.concatenate([jnp.cos(forward), -jnp.sin(forward)], axis=1)
    table_high = forward.astype(jnp.bfloat16)
    table_low = (forward - table_high.astype(jnp.float32)).astype(jnp.bfloat16)
    parity = 1.0 - 2.0 * (jnp.arange(period) % 2).astype(jnp.float32)
    parity = jnp.concatenate([parity, parity])
    stacked = jnp.stack([query_rows, key_rows, value_rows])
    rims = passed_along(stacked[:, -2:, :], "ctx", 1)
    extended = jnp.concatenate([rims, stacked], axis=1).astype(jnp.float32)
    mixed = (
        short_weight[0][:, None, :] * extended[:, 2:]
        + short_weight[1][:, None, :] * extended[:, 1:-1]
        + short_weight[2][:, None, :] * extended[:, :span]
    )
    gated_in = (mixed[1] * mixed[2]).astype(jnp.bfloat16)
    gated_t = gated_in.T
    inputs_local, taps_local = (
        lax.all_to_all(gated_t, "ctx", split_axis=0, concat_axis=1, tiled=True),
        lax.all_to_all(filter_taps, "ctx", split_axis=0, concat_axis=1, tiled=True),
    )
    spectra = inner_spectrum(
        taps_local.reshape(group * blocks, span), table_high, table_low
    ).reshape(group, blocks, 2 * period)
    earlier = jnp.concatenate(
        [jnp.zeros((group, 1, 2 * period), jnp.float32), spectra[:, :-1]], axis=1
    )
    kernel_spec = earlier + parity * spectra
    input_spec = inner_spectrum(
        inputs_local.reshape(group * blocks, span), table_high, table_low
    ).reshape(group, blocks, 2 * period)
    block_angle = angle_table(padded, blocks, 0, padded)
    cos_fwd = jnp.cos(block_angle)
    sin_fwd = jnp.sin(block_angle)
    input_re, input_im = block_mix(
        input_spec[..., :period], input_spec[..., period:], cos_fwd, sin_fwd, 1.0
    )
    kernel_re, kernel_im = block_mix(
        kernel_spec[..., :period], kernel_spec[..., period:], cos_fwd, sin_fwd, 1.0
    )
    product_re = input_re * kernel_re - input_im * kernel_im
    product_im = input_re * kernel_im + input_im * kernel_re
    back_angle = angle_table(blocks, padded, 0, padded)
    out_re, out_im = block_mix(
        product_re, product_im, jnp.cos(back_angle), jnp.sin(back_angle), -1.0
    )
    inverse = angle_table(period, span, span, period)
    inverse = jnp.concatenate([jnp.cos(inverse), -jnp.sin(inverse)], axis=0) * (
        1.0 / (period * padded)
    )
    joined = jnp.concatenate([out_re, out_im], axis=2).reshape(group * blocks, 2 * period)
    long_local = jnp.dot(
        joined, inverse, precision=TRIPLE, preferred_element_type=jnp.float32
    ).reshape(group, blocks * span)
    long_t = lax.all_to_all(
        long_local.astype(jnp.bfloat16), "ctx", split_axis=1, concat_axis=0, tiled=True
    ).astype(long_local.dtype)
    conv_t = (long_t + skip_gain[:, None] * gated_t.astype(jnp.float32)).astype(jnp.bfloat16)
    gated_out = (mixed[0].T * conv_t.astype(jnp.float32)).astype(jnp.bfloat16)
    term = lax.dot_general(
        gated_out, out_weight, (((0,), (0,)), ((), ())), preferred_element_type=jnp.float32
    )
    return lax.psum_scatter(term.astype(jnp.bfloat16), "tp", scatter_dimension=1, tiled=True)


SUB = 128
F32 = jnp.float32
BF16 = jnp.bfloat16


def split_table(matrix):
    high = matrix.astype(jnp.bfloat16)
    low = (matrix - high.astype(np.float32)).astype(jnp.bfloat16)
    return np.concatenate([high, high, low], axis=1)


def dft_tables(period):
    index = np.arange(SUB)
    turns = np.outer(index, index) % SUB * (2.0 * np.pi / SUB)
    cos, sin = np.cos(turns), np.sin(turns)
    forward = np.block([[cos, sin], [-sin, cos]]).astype(np.float32)
    inverse = (np.block([[cos, -sin], [sin, cos]]) / period).astype(np.float32)
    return split_table(forward), split_table(inverse)


def twiddle_table(radix):
    half = radix // 2
    turns = np.outer(np.arange(SUB), np.arange(half + 1)) * (2.0 * np.pi / (radix * SUB))
    return np.concatenate([np.cos(turns), -np.sin(turns)], axis=1).astype(np.float32)


def times(value, factor):
    return None if value is None else value * factor


def plus(left, right):
    if left is None:
        return right
    return left if right is None else left + right


def minus(left, right):
    if right is None:
        return left
    return -right if left is None else left - right


def rotate(value, turn):
    real, imag = value
    cos, sin = math.cos(2 * math.pi * turn), math.sin(2 * math.pi * turn)
    if abs(cos - sin) < 1e-12 and imag is not None:
        return (real + imag) * cos, (imag - real) * cos
    return plus(times(real, cos), times(imag, sin)), minus(times(imag, cos), times(real, sin))


def real_forward(values):
    points = 2 * len(values)
    if points == 2:
        return [(values[0], None), (values[0], None)]
    even, odd = real_forward(values[0::2]), real_forward(values[1::2])
    bins = [None] * (points // 2 + 1)
    bins[0] = (even[0][0] + odd[0][0], None)
    bins[points // 2] = (even[0][0] - odd[0][0], None)
    quarter = points // 4
    for k in range(1, quarter):
        turned = rotate(odd[k], k / points)
        bins[k] = (even[k][0] + turned[0], even[k][1] + turned[1])
        bins[points // 2 - k] = (even[k][0] - turned[0], turned[1] - even[k][1])
    bins[quarter] = (even[quarter][0], -odd[quarter][0])
    return bins


def real_inverse(bins):
    half = len(bins) - 1
    points = 2 * half
    if points == 2:
        return [bins[0][0] + bins[1][0]]
    even, odd = [], []
    for k in range(half // 2 + 1):
        ahead, back = bins[k], bins[half - k]
        if k == 0:
            even.append((ahead[0] + back[0], None))
            odd.append((ahead[0] - back[0], None))
        elif k == half // 2:
            even.append((ahead[0] * 2.0, None))
            odd.append((ahead[1] * -2.0, None))
        else:
            even.append((ahead[0] + back[0], ahead[1] - back[1]))
            difference = (ahead[0] - back[0], ahead[1] + back[1])
            odd.append(rotate(difference, -k / points))
    even, odd = real_inverse(even), real_inverse(odd)
    return [value for pair in zip(even, odd) for value in pair]


def split_dot(table, data):
    high = data.astype(BF16)
    low = (data - high.astype(F32)).astype(BF16)
    return jnp.dot(
        table[...], jnp.concatenate([high, low, high], axis=0), preferred_element_type=F32
    )


def over_pairs(count, pair):
    whole = count // 4 * 4
    lax.fori_loop(0, whole, pair, 0, unroll=4)
    for p in range(whole, count):
        pair(p, 0)


def first_stage(series, spectra, twiddle):
    half = series.shape[0] // SUB
    lanes = series.shape[1]

    def slab(step, carry):
        row = pl.multiple_of(step * 8, 8)
        values = [series[pl.ds(SUB * n + row, 8), :] for n in range(half)]
        factors = twiddle[pl.ds(row, 8), :]
        for k, (real, imag) in enumerate(real_forward(values)):
            if k == 0:
                spectra[0, pl.ds(row, 8), :] = real
                spectra[0, pl.ds(SUB + row, 8), :] = jnp.zeros_like(real)
                continue
            cos = jnp.broadcast_to(factors[:, k : k + 1], (8, lanes))
            sin = jnp.broadcast_to(factors[:, half + 1 + k : half + 2 + k], (8, lanes))
            if imag is None:
                spectra[k, pl.ds(row, 8), :] = real * cos
                spectra[k, pl.ds(SUB + row, 8), :] = real * sin
            else:
                spectra[k, pl.ds(row, 8), :] = real * cos - imag * sin
                spectra[k, pl.ds(SUB + row, 8), :] = real * sin + imag * cos
        return carry

    lax.fori_loop(0, SUB // 8, slab, 0)
    for k in range(half + 1, spectra.shape[0]):
        spectra[k] = jnp.zeros(spectra.shape[1:], F32)


def last_stage(spectra, series, twiddle):
    half = series.shape[0] // SUB
    lanes = series.shape[1]

    def slab(step, carry):
        row = pl.multiple_of(step * 8, 8)
        factors = twiddle[pl.ds(row, 8), :]
        bins = []
        for k in range(half + 1):
            real = spectra[k, pl.ds(row, 8), :]
            if k == 0:
                bins.append((real, None))
                continue
            imag = spectra[k, pl.ds(SUB + row, 8), :]
            cos = jnp.broadcast_to(factors[:, k : k + 1], (8, lanes))
            sin = jnp.broadcast_to(factors[:, half + 1 + k : half + 2 + k], (8, lanes))
            turned = real * cos + imag * sin
            bins.append((turned, None if k == half else imag * cos - real * sin))
        for n, value in enumerate(real_inverse(bins)):
            series[pl.ds(SUB * n + row, 8), :] = value
        return carry

    lax.fori_loop(0, SUB // 8, slab, 0)


def taps_kernel(chips, me_ref, *refs):
    pairs, (swapped, twiddle, forward, spectra_out, series, spectra) = refs[:chips], refs[chips:]
    _, lanes, span = swapped.shape
    mine = pl.ds(pl.multiple_of(me_ref[0] % 2 * lanes, lanes), lanes)
    for q in range(chips):
        for m, piece in ((2 * q, pairs[q][mine, :]), (2 * q + 1, swapped[q])):
            start = pl.multiple_of((me_ref[0] ^ m) * span, span)
            series[pl.ds(start, span), :] = piece.astype(F32).T
    first_stage(series, spectra, twiddle)

    def pair(p, carry):
        data = jnp.concatenate([spectra[2 * p], spectra[2 * p + 1]], axis=1)
        spectra_out[p] = split_dot(forward, data)
        return carry

    over_pairs(spectra_out.shape[0], pair)


def conv_kernel(blocks, me_ref, stay, swapped, *refs):
    others = refs[: blocks // 2 - 1]
    taps_spectra, twiddle, forward, inverse, skip = refs[blocks // 2 - 1 : blocks // 2 + 4]
    out, series, spectra = refs[blocks // 2 + 4 :]
    span, lanes = stay.shape
    pieces = [stay, swapped.at[0]] + [ref.at[core] for ref in others for core in range(2)]
    for m in range(blocks):
        start = pl.multiple_of((me_ref[0] ^ m) * span, span)
        series[pl.ds(start, span), :] = pieces[m][...].astype(F32)
    first_stage(series, spectra, twiddle)

    def pair(p, carry):
        data = jnp.concatenate([spectra[2 * p], spectra[2 * p + 1]], axis=1)
        signal = split_dot(forward, data)
        signal_re, signal_im = signal[:SUB], signal[SUB:]
        taps_re, taps_im = taps_spectra[p, :SUB, :], taps_spectra[p, SUB:, :]
        product = jnp.concatenate(
            [
                signal_re * taps_re - signal_im * taps_im,
                signal_re * taps_im + signal_im * taps_re,
            ],
            axis=0,
        )
        back = split_dot(inverse, product)
        spectra[2 * p] = back[:, :lanes]
        spectra[2 * p + 1] = back[:, lanes:]
        return carry

    over_pairs(taps_spectra.shape[0], pair)
    last_stage(spectra, out, twiddle)
    for m in range(blocks):
        window = pl.ds(m * span, span)
        out[window, :] += skip[...] * series[window, :]


def spread_kernel(me_ref, conv, *outs):
    span = outs[0].shape[0]
    for m, out in enumerate(outs):
        start = pl.multiple_of((me_ref[0] ^ m) * span, span)
        out[...] = conv[pl.ds(start, span), :].astype(BF16)


VMEM = pl.BlockSpec(memory_space=pltpu.VMEM)
SMEM = pl.BlockSpec(memory_space=pltpu.SMEM)
HBM = pl.BlockSpec(memory_space=pltpu.HBM)


def grant(mebibytes):
    return pltpu.CompilerParams(vmem_limit_bytes=mebibytes * 2**20)


def cost(microseconds):
    return pl.CostEstimate(flops=microseconds * 10**9, bytes_accessed=0, transcendentals=0)


GRANT = grant(16)


def taps_spectra_of(me, pairs, swapped, twiddle, forward):
    chips, lanes, span = swapped.shape
    length = 2 * chips * span
    count = (length // SUB + 2) // 2
    return pl.pallas_call(
        partial(taps_kernel, chips),
        out_shape=jax.ShapeDtypeStruct((count, 2 * SUB, 2 * lanes), F32),
        in_specs=[SMEM] + [VMEM] * (chips + 3),
        out_specs=VMEM,
        scratch_shapes=[
            pltpu.VMEM((length, lanes), F32),
            pltpu.VMEM((2 * count, 2 * SUB, lanes), F32),
        ],
        compiler_params=GRANT,
        cost_estimate=cost(8),
        name="taps_spectra",
    )(me, *pairs, swapped, twiddle, forward)


def long_conv(me, stay, swapped, others, taps_spectra, twiddle, forward, inverse, skip):
    span, lanes = stay.shape
    blocks = 2 * len(others) + 2
    pairs = taps_spectra.shape[0]
    return pl.pallas_call(
        partial(conv_kernel, blocks),
        out_shape=jax.ShapeDtypeStruct((blocks * span, lanes), F32),
        in_specs=[SMEM] + [VMEM] * (len(others) + 7),
        out_specs=VMEM,
        scratch_shapes=[
            pltpu.VMEM((blocks * span, lanes), F32),
            pltpu.VMEM((2 * pairs, 2 * SUB, lanes), F32),
        ],
        compiler_params=grant(20),
        cost_estimate=cost(20),
        name="long_conv",
    )(me, stay, swapped, *others, taps_spectra, twiddle, forward, inverse, skip)


def spread(me, conv, blocks):
    rows, lanes = conv.shape
    return pl.pallas_call(
        spread_kernel,
        out_shape=[jax.ShapeDtypeStruct((rows // blocks, lanes), BF16)] * blocks,
        in_specs=[SMEM, VMEM],
        out_specs=[VMEM] * blocks,
        compiler_params=GRANT,
        name="spread",
    )(me, conv)


def shifted_mix(stream, edge, weight):
    row = lax.broadcasted_iota(jnp.int32, stream.shape, 0)
    first = jnp.where(row == 0, edge[1:2], pltpu.roll(stream, 1, 0))
    second = pltpu.roll(stream, 2, 0)
    second = jnp.where(row == 0, edge[0:1], jnp.where(row == 1, edge[1:2], second))
    return weight[0:1] * stream + weight[1:2] * first + weight[2:3] * second


def rims_kernel(query, key, value, out, held, sems):
    span = query.shape[0]
    copies = [
        pltpu.make_async_copy(ref.at[pl.ds(span - 16, 16), :], held.at[s], sems.at[s])
        for s, ref in enumerate((query, key, value))
    ]
    for copy in copies:
        copy.start()
    for s, copy in enumerate(copies):
        copy.wait()
        out[2 * s : 2 * s + 2, :] = held[s, 14:16, :]


def rims(*streams):
    chans = streams[0].shape[1]
    return pl.pallas_call(
        rims_kernel,
        in_specs=[HBM] * 3,
        out_specs=VMEM,
        out_shape=jax.ShapeDtypeStruct((6, chans), BF16),
        scratch_shapes=[pltpu.VMEM((3, 16, chans), BF16), pltpu.SemaphoreType.DMA((3,))],
        compiler_params=grant(56),
        name="rims",
    )(*streams)


def gate_in_kernel(me_ref, key, value, edges, weight, stay, same, swap, held, sems):
    lanes = stay.shape[1]
    chips = swap.shape[0]
    mine = me_ref[0] % 2
    copies = []
    for q in range(chips):
        start = pl.multiple_of(((me_ref[0] // 2) ^ q) * 2 * lanes, 2 * lanes)
        for s, ref in enumerate((key, value)):
            source = ref.at[:, pl.ds(start, 2 * lanes)]
            copies.append(pltpu.make_async_copy(source, held.at[q, s], sems.at[q, s]))
            copies[-1].start()
    for q in range(chips):
        start = ((me_ref[0] // 2) ^ q) * 2 * lanes
        for copy in copies[2 * q : 2 * q + 2]:
            copy.wait()
        for side in range(2):
            inner = pl.ds(pl.multiple_of((mine ^ side) * lanes, lanes), lanes)
            outer = pl.ds(pl.multiple_of(start + (mine ^ side) * lanes, lanes), lanes)
            mixed = [
                shifted_mix(
                    held[q, s, :, inner].astype(F32),
                    edges[2 * s + 2 : 2 * s + 4, outer].astype(F32),
                    weight[:, s + 1, outer],
                )
                for s in range(2)
            ]
            gated = (mixed[0] * mixed[1]).astype(BF16)
            if side:
                swap[q] = gated
            elif q:
                same[q - 1] = gated
            else:
                stay[...] = gated


def gate_in(me, key_rows, value_rows, edges, short_weight, blocks):
    span, chans = key_rows.shape
    lanes = chans // blocks
    chips = blocks // 2
    shapes = [(span, lanes), (chips - 1, span, lanes), (chips, span, lanes)]
    return pl.pallas_call(
        gate_in_kernel,
        in_specs=[SMEM, HBM, HBM, VMEM, VMEM],
        out_specs=[VMEM] * 3,
        out_shape=[jax.ShapeDtypeStruct(shape, BF16) for shape in shapes],
        scratch_shapes=[
            pltpu.VMEM((chips, 2, span, 2 * lanes), BF16),
            pltpu.SemaphoreType.DMA((chips, 2)),
        ],
        compiler_params=grant(56),
        name="gate_in",
    )(me, key_rows, value_rows, edges, short_weight)


def split_taps_kernel(me_ref, taps, *refs):
    outs, sems = refs[:-1], refs[-1]
    rows = outs[0].shape[0]
    copies = []
    for q, out in enumerate(outs):
        window = pl.ds(pl.multiple_of(((me_ref[0] // 2) ^ q) * rows, rows), rows)
        copies.append(pltpu.make_async_copy(taps.at[window, :], out, sems.at[q]))
        copies[-1].start()
    for copy in copies:
        copy.wait()


def split_taps(me, filter_taps, chips):
    chans, span = filter_taps.shape
    return pl.pallas_call(
        split_taps_kernel,
        in_specs=[SMEM, HBM],
        out_specs=[VMEM] * chips,
        out_shape=[jax.ShapeDtypeStruct((chans // chips, span), BF16)] * chips,
        scratch_shapes=[pltpu.SemaphoreType.DMA((chips,))],
        compiler_params=GRANT,
        name="split_taps",
    )(me, filter_taps)


def other_core_kernel(me_ref, *refs):
    pairs, out = refs[:-1], refs[-1]
    rows = out.shape[1]
    for q, pair in enumerate(pairs):
        window = pl.ds(pl.multiple_of((1 - me_ref[0] % 2) * rows, rows), rows)
        out[q] = pair[window, :]


def other_core(me, pairs):
    rows, span = pairs[0].shape
    return pl.pallas_call(
        other_core_kernel,
        in_specs=[SMEM] + [VMEM] * len(pairs),
        out_specs=VMEM,
        out_shape=jax.ShapeDtypeStruct((len(pairs), rows // 2, span), BF16),
        compiler_params=GRANT,
        name="other_core",
    )(me, *pairs)


def pair_kernel(same, swapped, *outs):
    for q, out in enumerate(outs):
        out[0] = same[q]
        out[1] = swapped[q + 1]


def pair_up(same, swapped):
    count, span, lanes = same.shape
    return pl.pallas_call(
        pair_kernel,
        out_shape=[jax.ShapeDtypeStruct((2, span, lanes), BF16)] * count,
        in_specs=[VMEM] * 2,
        out_specs=[VMEM] * count,
        compiler_params=GRANT,
        name="pair_up",
    )(same, swapped)


def mix_query_kernel(query, edges, weight, out):
    out[...] = shifted_mix(query[...].astype(F32), edges[0:2].astype(F32), weight[:, 0, :])


def mix_query(query_rows, edges, short_weight):
    span, chans = query_rows.shape
    lanes = chans // 4
    return pl.pallas_call(
        mix_query_kernel,
        grid=(4,),
        in_specs=[
            pl.BlockSpec((span, lanes), lambda g: (0, g)),
            pl.BlockSpec((6, lanes), lambda g: (0, g)),
            pl.BlockSpec((3, 3, lanes), lambda g: (0, 0, g)),
        ],
        out_specs=pl.BlockSpec((span, lanes), lambda g: (0, g)),
        out_shape=jax.ShapeDtypeStruct((span, chans), F32),
        compiler_params=GRANT,
        name="mix_query",
    )(query_rows, edges, short_weight)


def exchange(pieces, axis):
    devices = range(lax.axis_size(axis))
    return [pieces[0]] + [
        lax.ppermute(piece, axis, [(i, i ^ m) for i in devices])
        for m, piece in enumerate(pieces)
        if m
    ]


def after(values, others):
    return lax.optimization_barrier((values, others))[0]


HEAD, PASS, ADD = 0, 1, 2
SENT = np.array(
    [
        (HEAD, ADD, ADD, 2, 1),
        (ADD, PASS, ADD, 3, 2),
        (PASS, ADD, PASS, 3, 3),
        (PASS, PASS, PASS, 3, 3),
    ],
    np.int32,
)


def gate_out_kernel(blocks, spot, *refs):
    convs, (mixed, far_weight, gated, sent) = refs[:blocks], refs[blocks:]
    lanes = convs[0].shape[1]
    rows = gated.shape[1]
    for m in range(blocks):
        window = pl.ds(pl.multiple_of((spot[0] ^ m) * lanes, lanes), lanes)
        piece = (mixed[:, window] * convs[m][...].astype(F32)).astype(BF16)
        gated[0, :, window] = piece[:rows]
        gated[1, :, window] = piece[rows:]
    first_sent(spot, gated, far_weight, sent)


def first_sent(spot, gated, far_weight, sent):
    @pl.when(spot[1] == 0)
    def _():
        term = jnp.dot(gated[1], far_weight[...], preferred_element_type=F32)
        sent[...] = term.astype(BF16)

    @pl.when(spot[1] != 0)
    def _():
        sent[...] = gated[0]


def gate_out(spot, convs, mixed, far_weight):
    span, chans = mixed.shape
    return pl.pallas_call(
        partial(gate_out_kernel, len(convs)),
        in_specs=[SMEM] + [VMEM] * (len(convs) + 2),
        out_specs=[VMEM] * 2,
        out_shape=[
            jax.ShapeDtypeStruct((2, span // 2, chans), BF16),
            jax.ShapeDtypeStruct((span // 2, chans), BF16),
        ],
        compiler_params=GRANT,
        name="gate_out",
    )(spot, *convs, mixed, far_weight)


def partner_sent(spot, gated, far_weight):
    return pl.pallas_call(
        first_sent,
        in_specs=[SMEM, VMEM, VMEM],
        out_specs=VMEM,
        out_shape=jax.ShapeDtypeStruct(gated.shape[1:], BF16),
        compiler_params=GRANT,
        cost_estimate=cost(1),
        name="partner_sent",
    )(spot, gated, far_weight)


def step_kernel(step, plan, head, term, got, out):
    mode = plan[step - 1]

    @pl.when(mode == HEAD)
    def _():
        out[...] = head[...]

    @pl.when(mode == PASS)
    def _():
        out[...] = got[...]

    @pl.when(mode == ADD)
    def _():
        out[...] = (term[...].astype(F32) + got[...].astype(F32)).astype(BF16)


def next_step(plan, step, chain, gated, terms, got):
    rows, chans = got.shape
    whole = pl.BlockSpec((rows, chans), lambda g, plan: (0, 0))
    return pl.pallas_call(
        partial(step_kernel, step),
        grid_spec=pltpu.PrefetchScalarGridSpec(
            num_scalar_prefetch=1,
            grid=(1,),
            in_specs=[
                pl.BlockSpec((None, rows, chans), lambda g, plan: (0, 0, 0)),
                pl.BlockSpec(
                    (None, None, rows, chans), lambda g, plan: (chain, step // 3, 0, 0)
                ),
                whole,
            ],
            out_specs=whole,
        ),
        out_shape=jax.ShapeDtypeStruct((rows, chans), BF16),
        compiler_params=GRANT,
        cost_estimate=cost(1),
        name="next_step",
    )(plan, gated, terms, got)


def terms_kernel(plan, mine, partners, weight, out, held, sems):
    count, chans = held.shape[:2]
    copies = []
    for k in range(count):
        columns = pl.ds(pl.multiple_of(plan[3 + k] * chans, chans), chans)
        copies.append(pltpu.make_async_copy(weight.at[:, columns], held.at[k], sems.at[k]))
        copies[-1].start()
    for k, copy in enumerate(copies):
        copy.wait()
        for chain, gated in enumerate((mine, partners)):
            term = jnp.dot(gated[1], held[k], preferred_element_type=F32)
            out[chain, k] = term.astype(BF16)


def sent_terms(plan, mine, partners, out_weight):
    _, rows, chans = mine.shape
    return pl.pallas_call(
        terms_kernel,
        in_specs=[SMEM, VMEM, VMEM, HBM],
        out_specs=VMEM,
        out_shape=jax.ShapeDtypeStruct((2, 2, rows, chans), BF16),
        scratch_shapes=[pltpu.VMEM((2, chans, chans), BF16), pltpu.SemaphoreType.DMA((2,))],
        compiler_params=GRANT,
        cost_estimate=cost(4),
        name="sent_terms",
    )(plan, mine, partners, out_weight)


def spread_weight(out_weight, ready):
    stages, blocks = lax.axis_size("tp"), lax.axis_size("ctx")
    stage, place = lax.axis_index("tp"), lax.axis_index("ctx")
    chans = out_weight.shape[0]
    hops = jnp.where(place % 2 == 0, 1, stages - 1)
    corners = jnp.stack([place // 2, (stage + hops) % stages, place, (stage + 2) % stages])
    parts = weight_corners(after(corners.astype(jnp.int32), ready), out_weight, blocks)
    found = []
    for part, static in zip(parts, ((1, stages - 1), (2, 2))):
        route = [
            (c * stages + k, c * stages + (k + static[c % 2]) % stages)
            for c in range(blocks)
            for k in range(stages)
        ]
        found.append(lax.ppermute(part, ("ctx", "tp"), route))
    return found


def corners_kernel(corners, weight, *refs):
    outs, sems = refs[:-1], refs[-1]
    copies = []
    for n, out in enumerate(outs):
        rows, chans = out.shape
        row = pl.multiple_of(corners[2 * n] * rows, rows)
        column = pl.multiple_of(corners[2 * n + 1] * chans, chans)
        source = weight.at[pl.ds(row, rows), pl.ds(column, chans)]
        copies.append(pltpu.make_async_copy(source, out, sems.at[n]))
        copies[-1].start()
    for copy in copies:
        copy.wait()


def weight_corners(corners, out_weight, blocks):
    chans = out_weight.shape[0]
    shapes = [(2 * chans // blocks, chans), (chans // blocks, chans)]
    return pl.pallas_call(
        corners_kernel,
        in_specs=[SMEM, HBM],
        out_specs=[VMEM] * 2,
        out_shape=[jax.ShapeDtypeStruct(shape, BF16) for shape in shapes],
        scratch_shapes=[pltpu.SemaphoreType.DMA((2,))],
        compiler_params=grant(56),
        name="weight_corners",
    )(corners, out_weight)


def gather_weight(part):
    devices = range(lax.axis_size("ctx"))
    near = [(i, i ^ (4 if i & 1 else 2)) for i in devices]
    other = [(i, i ^ (2 if i & 1 else 4)) for i in devices]
    two = [part, lax.ppermute(part, "ctx", near)]
    return jnp.stack(two), jnp.stack([lax.ppermute(x, "ctx", other) for x in two])


def pairs_of(refs):
    return list(zip(refs[::2], refs[1::2]))


def spots(first, pair):
    return (first, pair[0]), (first + 2, pair[1])


def add_parts(order, data, *weights):
    total = None
    for first, weight in weights:
        count, lanes, columns = weight.shape
        picked = []
        for q in range(count):
            index = order[first + q]
            index = index // 2 if lanes == 2 * SUB else index
            picked.append(data[:, pl.ds(pl.multiple_of(index * lanes, lanes), lanes)])
        block = weight[...].reshape(count * lanes, columns)
        picked = jnp.concatenate(picked, axis=1)
        term = jnp.dot(picked, block, preferred_element_type=F32)
        total = term if total is None else total + term
    return total


def early_kernel(order, mine, got0, got1, partner0, partner1, weight, *refs):
    (near, near2, far2), (out, own, first, own_weight, sem) = pairs_of(refs[:6]), refs[6:]
    turn_count = order[8]
    rows, chans = got0.shape
    columns = pl.ds(pl.multiple_of(order[9] * chans, chans), chans)
    copy = pltpu.make_async_copy(weight.at[:, columns], own_weight, sem)
    copy.start()

    @pl.when(turn_count >= 2)
    def _():
        first[:rows, :] = got0[...]
        first[rows:, :] = partner0[...]

    @pl.when(turn_count < 2)
    def _():
        first[:rows, :] = got1[...]
        first[rows:, :] = partner1[...]

    @pl.when(turn_count >= 1)
    def _():
        out[...] = add_parts(order, first, *spots(0, near))

    @pl.when(turn_count < 1)
    def _():
        out[...] = jnp.zeros_like(out)

    @pl.when(turn_count == 3)
    def _():
        first[:rows, :] = got1[...]
        first[rows:, :] = partner1[...]
        out[...] += add_parts(order, first, *spots(0, near2), *spots(4, far2))

    copy.wait()
    out[:rows, :] += jnp.dot(mine[0], own_weight[...], preferred_element_type=F32)
    own[...] = jnp.dot(mine[1], own_weight[...], preferred_element_type=F32)


def early_sum(order, mine, arrivals, out_weight, weights):
    _, rows, chans = mine.shape
    whole = lambda shape: pl.BlockSpec(shape, lambda g, order: (0,) * len(shape))
    return pl.pallas_call(
        early_kernel,
        grid_spec=pltpu.PrefetchScalarGridSpec(
            num_scalar_prefetch=1,
            grid=(1,),
            in_specs=[whole(mine.shape)]
            + [whole((rows, chans))] * 4
            + [HBM]
            + [whole(x.shape) for x in weights],
            out_specs=[whole((2 * rows, chans)), whole((rows, chans))],
            scratch_shapes=[
                pltpu.VMEM((2 * rows, chans), BF16),
                pltpu.VMEM((chans, chans), BF16),
                pltpu.SemaphoreType.DMA,
            ],
        ),
        out_shape=[
            jax.ShapeDtypeStruct((2 * rows, chans), F32),
            jax.ShapeDtypeStruct((rows, chans), F32),
        ],
        compiler_params=grant(24),
        cost_estimate=cost(5),
        name="early_sum",
    )(order, mine, *arrivals, out_weight, *weights)


def late_sum(order, early, got2, got3, weights, total):
    behind = order[8]

    @pl.when(behind < 2)
    def _():
        total[...] = early[...]

    @pl.when(behind == 2)
    def _():
        total[...] = early[...] + add_parts(order, got2, *spots(0, weights[0]), *spots(4, weights[1]))

    @pl.when(behind == 3)
    def _():
        total[...] = early[...] + add_parts(order, got3, *spots(4, weights[2]))

    summed = jnp.where(behind == 3, got2[...].astype(F32), got3[...].astype(F32))
    return jnp.where(behind == 0, 0.0, summed)


def partner_kernel(order, early, got2, got3, *refs):
    weights, (out, total) = pairs_of(refs[:6]), refs[6:]
    out[1] = late_sum(order, early, got2, got3, weights, total).astype(BF16)
    out[0] = total[...].astype(BF16)


def partner_sum(order, early, arrivals, weights):
    rows, chans = arrivals[0].shape
    whole = lambda shape: pl.BlockSpec(shape, lambda g, order: (0,) * len(shape))
    return pl.pallas_call(
        partner_kernel,
        grid_spec=pltpu.PrefetchScalarGridSpec(
            num_scalar_prefetch=1,
            grid=(1,),
            in_specs=[pl.BlockSpec((rows, chans), lambda g, order: (1, 0))]
            + [whole((rows, chans))] * 2
            + [whole(x.shape) for x in weights],
            out_specs=whole((2, rows, chans)),
            scratch_shapes=[pltpu.VMEM((rows, chans), F32)],
        ),
        out_shape=jax.ShapeDtypeStruct((2, rows, chans), BF16),
        compiler_params=grant(24),
        cost_estimate=cost(2),
        name="partner_sum",
    )(order, early, *arrivals, *weights)


def mine_kernel(order, early, own, got2, got3, *refs):
    weights, (out, total) = pairs_of(refs[:6]), refs[6:]
    rows = early.shape[0]
    out[rows:, :] = late_sum(order, early, got2, got3, weights, total) + own[...]
    out[:rows, :] = total[...]


def mine_sum(order, early, own, arrivals, weights):
    rows, chans = arrivals[0].shape
    whole = lambda shape: pl.BlockSpec(shape, lambda g, order: (0,) * len(shape))
    return pl.pallas_call(
        mine_kernel,
        grid_spec=pltpu.PrefetchScalarGridSpec(
            num_scalar_prefetch=1,
            grid=(1,),
            in_specs=[pl.BlockSpec((rows, chans), lambda g, order: (0, 0))]
            + [whole((rows, chans))] * 3
            + [whole(x.shape) for x in weights],
            out_specs=whole((2 * rows, chans)),
            scratch_shapes=[pltpu.VMEM((rows, chans), F32)],
        ),
        out_shape=jax.ShapeDtypeStruct((2 * rows, chans), F32),
        compiler_params=grant(24),
        cost_estimate=cost(3),
        name="mine_sum",
    )(order, early, own, *arrivals, *weights)


def join_kernel(mine, partners, out):
    rows = partners.shape[1]
    for half in range(2):
        part = slice(half * rows, (half + 1) * rows)
        out[part, :] = (mine[part, :] + partners[half].astype(F32)).astype(BF16)


def join_sums(mine, partners):
    return pl.pallas_call(
        join_kernel,
        in_specs=[VMEM] * 2,
        out_specs=VMEM,
        out_shape=jax.ShapeDtypeStruct(mine.shape, BF16),
        compiler_params=GRANT,
        name="join_sums",
    )(mine, partners)


def weight_order():
    place, stage = lax.axis_index("ctx"), lax.axis_index("tp")
    up = place % 2 == 0
    last = lax.axis_size("tp") - 1
    a = jnp.where(up, 2, 4)
    masks = [0 * a, a, 6 - a, 0 * a + 6]
    swapped = [0 * a + 1, (6 - a) ^ 1, a ^ 1, 0 * a + 7]
    parts = [place ^ mask for mask in masks + swapped]
    return jnp.stack(parts + [jnp.where(up, stage, last - stage), stage]).astype(jnp.int32)


def project(spot, plan, order, convs, mixed, out_weight, weight_parts):
    stages, blocks = lax.axis_size("tp"), lax.axis_size("ctx")
    chans = out_weight.shape[0]
    far_weight = lax.dynamic_slice(out_weight, (0, spot[2] * chans), (chans, chans))
    mine, sent = gate_out(spot, convs, mixed, far_weight)
    route = []
    for c in range(blocks):
        for k in range(stages):
            to = k + (1 if c % 2 == 0 else -1)
            if 0 <= to < stages:
                route.append((c * stages + k, c * stages + to))
    onward = lambda x: lax.ppermute(x, ("ctx", "tp"), route)
    core_swap = lambda x: lax.ppermute(x, "ctx", [(i, i ^ 1) for i in range(blocks)])
    partners = core_swap(mine)
    partner_first = partner_sent(spot, partners, far_weight)
    got = [[onward(sent), onward(partner_first)]]
    terms = sent_terms(plan, mine, partners, out_weight)
    steps = []
    for step in range(1, stages):
        row = []
        for chain, gated in enumerate((mine, partners)):
            row.append(next_step(plan, step, chain, gated, terms, got[-1][chain]))
        steps.append(row)
        got.append([onward(x) for x in row])

    near, near2 = (gather_weight(part) for part in after(weight_parts, partner_first))
    far2, far = ([core_swap(x) for x in pair] for pair in (near2, near))
    arrivals = [got[0][0], got[1][0], got[0][1], got[1][1]]
    early, own = early_sum(order, mine, arrivals, out_weight, (*near, *near2, *far2))
    late = (*near2, *far2, *far)
    theirs = partner_sum(after(order, got[3][0]), early, [got[2][1], got[3][1]], late)
    ours = mine_sum(order, early, own, [got[2][0], got[3][0]], late)
    return join_sums(ours, core_swap(theirs))


def fast_per_device(
    query_rows, key_rows, value_rows, short_weight, skip_gain, filter_taps, out_weight
):
    span, chans = query_rows.shape
    blocks, stages = lax.axis_size("ctx"), lax.axis_size("tp")
    lanes = chans // blocks
    length = span * blocks
    radix = 2 * length // SUB
    place, stage = lax.axis_index("ctx"), lax.axis_index("tp")
    me = place.astype(jnp.int32).reshape(1)
    up = place % 2 == 0
    behind = jnp.where(up, stage, stages - 1 - stage)
    far = jnp.where(up, stages - 1, 0)
    spot = jnp.stack([place, behind, far]).astype(jnp.int32)
    plan = lax.dynamic_index_in_dim(jnp.asarray(SENT), behind, keepdims=False)
    plan = jnp.where(up | (jnp.arange(5) < 3), plan, stages - 1 - plan)
    me, spot, plan, order = lax.optimization_barrier((me, spot, plan, weight_order()))
    skip = lax.dynamic_slice(skip_gain, (place * lanes,), (lanes,)).reshape(1, lanes)
    forward, inverse = (jnp.asarray(t) for t in dft_tables(2 * length))
    twiddle = jnp.asarray(twiddle_table(radix))
    devices = range(blocks)
    core_swap = lambda x: lax.ppermute(x, "ctx", [(i, i ^ 1) for i in devices])
    to_chips = lambda xs: [
        lax.ppermute(x, "ctx", [(i, i ^ (2 * q + 2)) for i in devices])
        for q, x in enumerate(xs)
    ]
    edges = passed_along(rims(query_rows, key_rows, value_rows), "ctx", 1)
    pairs = split_taps(after(me, edges), filter_taps, blocks // 2)
    pairs = [pairs[0]] + to_chips(pairs[1:])
    stay, same, swap = gate_in(me, key_rows, value_rows, edges, short_weight, blocks)
    swapped = core_swap(swap)
    packed = pair_up(same, swapped)
    others = to_chips(packed)
    taps_swapped = core_swap(other_core(me, pairs))
    mixed = mix_query(query_rows, edges, short_weight)
    spectra = taps_spectra_of(me, pairs, taps_swapped, twiddle, forward)
    weight_parts = spread_weight(out_weight, taps_swapped)
    conv = long_conv(me, stay, swapped, others, spectra, twiddle, forward, inverse, skip)
    convs = exchange(spread(after(me, weight_parts), conv, blocks), "ctx")
    return project(spot, plan, order, convs, mixed, out_weight, weight_parts)


def per_device(*arrays):
    span, chans = arrays[0].shape
    blocks = lax.axis_size("ctx")
    suits = blocks == 8 and lax.axis_size("tp") == 4 and span == 512 and chans == 8 * SUB
    return (fast_per_device if suits else general_per_device)(*arrays)


def solution(mesh):
    placed = (
        P("ctx", "tp"),
        P("ctx", "tp"),
        P("ctx", "tp"),
        P(None, None, "tp"),
        P("tp"),
        P("tp", "ctx"),
        P("tp", None),
    )
    return jax.shard_map(
        per_device, mesh=mesh, in_specs=placed, out_specs=P("ctx", "tp"), check_vma=False
    )
```

```python
from functools import partial
import math

import jax
import jax.numpy as jnp
import numpy as np
from jax import lax
from jax.experimental import pallas as pl
from jax.experimental.pallas import tpu as pltpu
from jax.sharding import PartitionSpec as P

TRIPLE = lax.Precision.HIGH


def passed_along(block, axis, distance):
    devices = range(lax.axis_size(axis))
    route = [(i - distance, i) for i in devices if i - distance in devices]
    return lax.ppermute(block, axis, route)


def angle_table(left, right, offset, period):
    rows = lax.broadcasted_iota(jnp.int32, (left, right), 0)
    cols = lax.broadcasted_iota(jnp.int32, (left, right), 1) + offset
    turns = rows * cols % period
    return turns.astype(jnp.float32) * (2.0 * math.pi / period)


def inner_spectrum(rows, table_high, table_low):
    upper = jnp.dot(rows, table_high, preferred_element_type=jnp.float32)
    lower = jnp.dot(rows, table_low, preferred_element_type=jnp.float32)
    return upper + lower


def block_mix(real_component, imaginary_component, cosine_lookup, sine_lookup, sign):
    multiplier = partial(jnp.einsum, precision=TRIPLE, preferred_element_type=jnp.float32)
    cosine_real = multiplier("id,rdy->riy", cosine_lookup, real_component)
    cosine_imaginary = multiplier("id,rdy->riy", cosine_lookup, imaginary_component)
    sine_real = multiplier("id,rdy->riy", sine_lookup, real_component)
    sine_imaginary = multiplier("id,rdy->riy", sine_lookup, imaginary_component)
    return (cosine_real + sign * sine_imaginary, cosine_imaginary - sign * sine_real)


def general_per_device(query_rows, key_rows, value_rows, short_weight, skip_gain, filter_taps, out_weight):
    span = query_rows.shape[0]
    chans = query_rows.shape[1]
    blocks = lax.axis_size("ctx")
    group = chans // blocks
    period = 2 * span
    padded = 2 * blocks
    forward = angle_table(span, period, 0, period)
    forward = jnp.concatenate([jnp.cos(forward), -jnp.sin(forward)], axis=1)
    table_high = forward.astype(jnp.bfloat16)
    table_low = (forward - table_high.astype(jnp.float32)).astype(jnp.bfloat16)
    parity = 1.0 - 2.0 * (jnp.arange(period) % 2).astype(jnp.float32)
    parity = jnp.concatenate([parity, parity])
    stacked = jnp.stack([query_rows, key_rows, value_rows])
    rims = passed_along(stacked[:, -2:, :], "ctx", 1)
    extended = jnp.concatenate([rims, stacked], axis=1).astype(jnp.float32)
    mixed = (
        short_weight[0][:, None, :] * extended[:, 2:]
        + short_weight[1][:, None, :] * extended[:, 1:-1]
        + short_weight[2][:, None, :] * extended[:, :span]
    )
    gated_in = (mixed[1] * mixed[2]).astype(jnp.bfloat16)
    gated_t = gated_in.T
    inputs_local, taps_local = (
        lax.all_to_all(gated_t, "ctx", split_axis=0, concat_axis=1, tiled=True),
        lax.all_to_all(filter_taps, "ctx", split_axis=0, concat_axis=1, tiled=True),
    )
    spectra = inner_spectrum(
        taps_local.reshape(group * blocks, span), table_high, table_low
    ).reshape(group, blocks, 2 * period)
    earlier = jnp.concatenate(
        [jnp.zeros((group, 1, 2 * period), jnp.float32), spectra[:, :-1]], axis=1
    )
    kernel_spec = earlier + parity * spectra
    input_spec = inner_spectrum(
        inputs_local.reshape(group * blocks, span), table_high, table_low
    ).reshape(group, blocks, 2 * period)
    block_angle = angle_table(padded, blocks, 0, padded)
    cos_fwd = jnp.cos(block_angle)
    sin_fwd = jnp.sin(block_angle)
    input_re, input_im = block_mix(
        input_spec[..., :period], input_spec[..., period:], cos_fwd, sin_fwd, 1.0
    )
    kernel_re, kernel_im = block_mix(
        kernel_spec[..., :period], kernel_spec[..., period:], cos_fwd, sin_fwd, 1.0
    )
    product_re = input_re * kernel_re - input_im * kernel_im
    product_im = input_re * kernel_im + input_im * kernel_re
    back_angle = angle_table(blocks, padded, 0, padded)
    out_re, out_im = block_mix(
        product_re, product_im, jnp.cos(back_angle), jnp.sin(back_angle), -1.0
    )
    inverse = angle_table(period, span, span, period)
    inverse = jnp.concatenate([jnp.cos(inverse), -jnp.sin(inverse)], axis=0) * (
        1.0 / (period * padded)
    )
    joined = jnp.concatenate([out_re, out_im], axis=2).reshape(group * blocks, 2 * period)
    long_local = jnp.dot(
        joined, inverse, precision=TRIPLE, preferred_element_type=jnp.float32
    ).reshape(group, blocks * span)
    long_t = lax.all_to_all(
        long_local.astype(jnp.bfloat16), "ctx", split_axis=1, concat_axis=0, tiled=True
    ).astype(long_local.dtype)
    conv_t = (long_t + skip_gain[:, None] * gated_t.astype(jnp.float32)).astype(jnp.bfloat16)
    gated_out = (mixed[0].T * conv_t.astype(jnp.float32)).astype(jnp.bfloat16)
    term = lax.dot_general(
        gated_out, out_weight, (((0,), (0,)), ((), ())), preferred_element_type=jnp.float32
    )
    return lax.psum_scatter(term.astype(jnp.bfloat16), "tp", scatter_dimension=1, tiled=True)


SUB = 128
F32 = jnp.float32
BF16 = jnp.bfloat16


def split_table(matrix):
    high = matrix.astype(jnp.bfloat16)
    low = (matrix - high.astype(np.float32)).astype(jnp.bfloat16)
    return np.concatenate([high, high, low], axis=1)


def dft_tables(period):
    index = np.arange(SUB)
    turns = np.outer(index, index) % SUB * (2.0 * np.pi / SUB)
    cos, sin = np.cos(turns), np.sin(turns)
    forward = np.block([[cos, sin], [-sin, cos]]).astype(np.float32)
    inverse = (np.block([[cos, -sin], [sin, cos]]) / period).astype(np.float32)
    return split_table(forward), split_table(inverse)


def twiddle_table(radix):
    half = radix // 2
    turns = np.outer(np.arange(SUB), np.arange(half + 1)) * (2.0 * np.pi / (radix * SUB))
    return np.concatenate([np.cos(turns), -np.sin(turns)], axis=1).astype(np.float32)


def times(value, factor):
    return None if value is None else value * factor


def plus(left, right):
    if left is None:
        return right
    return left if right is None else left + right


def minus(left, right):
    if right is None:
        return left
    return -right if left is None else left - right


def rotate(value, turn):
    real, imag = value
    cos, sin = math.cos(2 * math.pi * turn), math.sin(2 * math.pi * turn)
    if abs(cos - sin) < 1e-12 and imag is not None:
        return (real + imag) * cos, (imag - real) * cos
    return plus(times(real, cos), times(imag, sin)), minus(times(imag, cos), times(real, sin))


def real_forward(values):
    points = 2 * len(values)
    if points == 2:
        return [(values[0], None), (values[0], None)]
    even, odd = real_forward(values[0::2]), real_forward(values[1::2])
    bins = [None] * (points // 2 + 1)
    bins[0] = (even[0][0] + odd[0][0], None)
    bins[points // 2] = (even[0][0] - odd[0][0], None)
    quarter = points // 4
    for k in range(1, quarter):
        turned = rotate(odd[k], k / points)
        bins[k] = (even[k][0] + turned[0], even[k][1] + turned[1])
        bins[points // 2 - k] = (even[k][0] - turned[0], turned[1] - even[k][1])
    bins[quarter] = (even[quarter][0], -odd[quarter][0])
    return bins


def real_inverse(bins):
    half = len(bins) - 1
    points = 2 * half
    if points == 2:
        return [bins[0][0] + bins[1][0]]
    even, odd = [], []
    for k in range(half // 2 + 1):
        ahead, back = bins[k], bins[half - k]
        if k == 0:
            even.append((ahead[0] + back[0], None))
            odd.append((ahead[0] - back[0], None))
        elif k == half // 2:
            even.append((ahead[0] * 2.0, None))
            odd.append((ahead[1] * -2.0, None))
        else:
            even.append((ahead[0] + back[0], ahead[1] - back[1]))
            difference = (ahead[0] - back[0], ahead[1] + back[1])
            odd.append(rotate(difference, -k / points))
    even, odd = real_inverse(even), real_inverse(odd)
    return [value for pair in zip(even, odd) for value in pair]


def split_dot(table, data):
    high = data.astype(BF16)
    low = (data - high.astype(F32)).astype(BF16)
    return jnp.dot(
        table[...], jnp.concatenate([high, low, high], axis=0), preferred_element_type=F32
    )


def over_pairs(count, pair):
    whole = count // 4 * 4
    lax.fori_loop(0, whole, pair, 0, unroll=4)
    for p in range(whole, count):
        pair(p, 0)


def first_stage(series, spectra, twiddle):
    half = series.shape[0] // SUB
    lanes = series.shape[1]

    def slab(step, carry):
        row = pl.multiple_of(step * 8, 8)
        values = [series[pl.ds(SUB * n + row, 8), :] for n in range(half)]
        factors = twiddle[pl.ds(row, 8), :]
        for k, (real, imag) in enumerate(real_forward(values)):
            if k == 0:
                spectra[0, pl.ds(row, 8), :] = real
                spectra[0, pl.ds(SUB + row, 8), :] = jnp.zeros_like(real)
                continue
            cos = jnp.broadcast_to(factors[:, k : k + 1], (8, lanes))
            sin = jnp.broadcast_to(factors[:, half + 1 + k : half + 2 + k], (8, lanes))
            if imag is None:
                spectra[k, pl.ds(row, 8), :] = real * cos
                spectra[k, pl.ds(SUB + row, 8), :] = real * sin
            else:
                spectra[k, pl.ds(row, 8), :] = real * cos - imag * sin
                spectra[k, pl.ds(SUB + row, 8), :] = real * sin + imag * cos
        return carry

    lax.fori_loop(0, SUB // 8, slab, 0)
    for k in range(half + 1, spectra.shape[0]):
        spectra[k] = jnp.zeros(spectra.shape[1:], F32)


def last_stage(spectra, series, twiddle):
    half = series.shape[0] // SUB
    lanes = series.shape[1]

    def slab(step, carry):
        row = pl.multiple_of(step * 8, 8)
        factors = twiddle[pl.ds(row, 8), :]
        bins = []
        for k in range(half + 1):
            real = spectra[k, pl.ds(row, 8), :]
            if k == 0:
                bins.append((real, None))
                continue
            imag = spectra[k, pl.ds(SUB + row, 8), :]
            cos = jnp.broadcast_to(factors[:, k : k + 1], (8, lanes))
            sin = jnp.broadcast_to(factors[:, half + 1 + k : half + 2 + k], (8, lanes))
            turned = real * cos + imag * sin
            bins.append((turned, None if k == half else imag * cos - real * sin))
        for n, value in enumerate(real_inverse(bins)):
            series[pl.ds(SUB * n + row, 8), :] = value
        return carry

    lax.fori_loop(0, SUB // 8, slab, 0)


def taps_kernel(chips, me_ref, *refs):
    pairs, (swapped, twiddle, forward, spectra_out, series, spectra) = refs[:chips], refs[chips:]
    _, lanes, span = swapped.shape
    mine = pl.ds(pl.multiple_of(me_ref[0] % 2 * lanes, lanes), lanes)
    for q in range(chips):
        for m, piece in ((2 * q, pairs[q][mine, :]), (2 * q + 1, swapped[q])):
            start = pl.multiple_of((me_ref[0] ^ m) * span, span)
            series[pl.ds(start, span), :] = piece.astype(F32).T
    first_stage(series, spectra, twiddle)

    def pair(p, carry):
        data = jnp.concatenate([spectra[2 * p], spectra[2 * p + 1]], axis=1)
        spectra_out[p] = split_dot(forward, data)
        return carry

    over_pairs(spectra_out.shape[0], pair)


def conv_kernel(blocks, me_ref, stay, swapped, *refs):
    others = refs[: blocks // 2 - 1]
    taps_spectra, twiddle, forward, inverse, skip = refs[blocks // 2 - 1 : blocks // 2 + 4]
    out, series, spectra = refs[blocks // 2 + 4 :]
    span, lanes = stay.shape
    pieces = [stay, swapped.at[0]] + [ref.at[core] for ref in others for core in range(2)]
    for m in range(blocks):
        start = pl.multiple_of((me_ref[0] ^ m) * span, span)
        series[pl.ds(start, span), :] = pieces[m][...].astype(F32)
    first_stage(series, spectra, twiddle)

    def pair(p, carry):
        data = jnp.concatenate([spectra[2 * p], spectra[2 * p + 1]], axis=1)
        signal = split_dot(forward, data)
        signal_re, signal_im = signal[:SUB], signal[SUB:]
        taps_re, taps_im = taps_spectra[p, :SUB, :], taps_spectra[p, SUB:, :]
        product = jnp.concatenate(
            [
                signal_re * taps_re - signal_im * taps_im,
                signal_re * taps_im + signal_im * taps_re,
            ],
            axis=0,
        )
        back = split_dot(inverse, product)
        spectra[2 * p] = back[:, :lanes]
        spectra[2 * p + 1] = back[:, lanes:]
        return carry

    over_pairs(taps_spectra.shape[0], pair)
    last_stage(spectra, out, twiddle)
    for m in range(blocks):
        window = pl.ds(m * span, span)
        out[window, :] += skip[...] * series[window, :]


def spread_kernel(me_ref, conv, stay, same, swap):
    chips, span, _ = swap.shape
    for m in range(2 * chips):
        start = pl.multiple_of((me_ref[0] ^ m) * span, span)
        piece = conv[pl.ds(start, span), :].astype(BF16)
        if m % 2:
            swap[m // 2] = piece
        elif m:
            same[m // 2 - 1] = piece
        else:
            stay[...] = piece


VMEM = pl.BlockSpec(memory_space=pltpu.VMEM)
SMEM = pl.BlockSpec(memory_space=pltpu.SMEM)
HBM = pl.BlockSpec(memory_space=pltpu.HBM)


def grant(mebibytes):
    return pltpu.CompilerParams(vmem_limit_bytes=mebibytes * 2**20)


def cost(microseconds):
    return pl.CostEstimate(flops=microseconds * 10**9, bytes_accessed=0, transcendentals=0)


GRANT = grant(16)


def taps_spectra_of(me, pairs, swapped, twiddle, forward):
    chips, lanes, span = swapped.shape
    length = 2 * chips * span
    count = (length // SUB + 2) // 2
    return pl.pallas_call(
        partial(taps_kernel, chips),
        out_shape=jax.ShapeDtypeStruct((count, 2 * SUB, 2 * lanes), F32),
        in_specs=[SMEM] + [VMEM] * (chips + 3),
        out_specs=VMEM,
        scratch_shapes=[
            pltpu.VMEM((length, lanes), F32),
            pltpu.VMEM((2 * count, 2 * SUB, lanes), F32),
        ],
        compiler_params=GRANT,
        cost_estimate=cost(8),
        name="taps_spectra",
    )(me, *pairs, swapped, twiddle, forward)


def long_conv(me, stay, swapped, others, taps_spectra, twiddle, forward, inverse, skip):
    span, lanes = stay.shape
    blocks = 2 * len(others) + 2
    pairs = taps_spectra.shape[0]
    return pl.pallas_call(
        partial(conv_kernel, blocks),
        out_shape=jax.ShapeDtypeStruct((blocks * span, lanes), F32),
        in_specs=[SMEM] + [VMEM] * (len(others) + 7),
        out_specs=VMEM,
        scratch_shapes=[
            pltpu.VMEM((blocks * span, lanes), F32),
            pltpu.VMEM((2 * pairs, 2 * SUB, lanes), F32),
        ],
        compiler_params=grant(20),
        cost_estimate=cost(20),
        name="long_conv",
    )(me, stay, swapped, *others, taps_spectra, twiddle, forward, inverse, skip)


def spread(me, conv, blocks):
    rows, lanes = conv.shape
    span, chips = rows // blocks, blocks // 2
    shapes = [(span, lanes), (chips - 1, span, lanes), (chips, span, lanes)]
    return pl.pallas_call(
        spread_kernel,
        out_shape=[jax.ShapeDtypeStruct(shape, BF16) for shape in shapes],
        in_specs=[SMEM, VMEM],
        out_specs=[VMEM] * 3,
        compiler_params=GRANT,
        name="spread",
    )(me, conv)


def shifted_mix(stream, edge, weight):
    row = lax.broadcasted_iota(jnp.int32, stream.shape, 0)
    first = jnp.where(row == 0, edge[1:2], pltpu.roll(stream, 1, 0))
    second = pltpu.roll(stream, 2, 0)
    second = jnp.where(row == 0, edge[0:1], jnp.where(row == 1, edge[1:2], second))
    return weight[0:1] * stream + weight[1:2] * first + weight[2:3] * second


def rims_kernel(query, key, value, out, held, sems):
    span = query.shape[0]
    copies = [
        pltpu.make_async_copy(ref.at[pl.ds(span - 16, 16), :], held.at[s], sems.at[s])
        for s, ref in enumerate((query, key, value))
    ]
    for copy in copies:
        copy.start()
    for s, copy in enumerate(copies):
        copy.wait()
        out[2 * s : 2 * s + 2, :] = held[s, 14:16, :]


def rims(*streams):
    chans = streams[0].shape[1]
    return pl.pallas_call(
        rims_kernel,
        in_specs=[HBM] * 3,
        out_specs=VMEM,
        out_shape=jax.ShapeDtypeStruct((6, chans), BF16),
        scratch_shapes=[pltpu.VMEM((3, 16, chans), BF16), pltpu.SemaphoreType.DMA((3,))],
        compiler_params=grant(56),
        name="rims",
    )(*streams)


def gate_in_kernel(me_ref, key, value, edges, weight, stay, same, swap, held, sems):
    lanes = stay.shape[1]
    chips = swap.shape[0]
    mine = me_ref[0] % 2
    copies = []
    for q in range(chips):
        start = pl.multiple_of(((me_ref[0] // 2) ^ q) * 2 * lanes, 2 * lanes)
        for s, ref in enumerate((key, value)):
            source = ref.at[:, pl.ds(start, 2 * lanes)]
            copies.append(pltpu.make_async_copy(source, held.at[q, s], sems.at[q, s]))
            copies[-1].start()
    for q in range(chips):
        start = ((me_ref[0] // 2) ^ q) * 2 * lanes
        for copy in copies[2 * q : 2 * q + 2]:
            copy.wait()
        for side in range(2):
            inner = pl.ds(pl.multiple_of((mine ^ side) * lanes, lanes), lanes)
            outer = pl.ds(pl.multiple_of(start + (mine ^ side) * lanes, lanes), lanes)
            mixed = [
                shifted_mix(
                    held[q, s, :, inner].astype(F32),
                    edges[2 * s + 2 : 2 * s + 4, outer].astype(F32),
                    weight[:, s + 1, outer],
                )
                for s in range(2)
            ]
            gated = (mixed[0] * mixed[1]).astype(BF16)
            if side:
                swap[q] = gated
            elif q:
                same[q - 1] = gated
            else:
                stay[...] = gated


def gate_in(me, key_rows, value_rows, edges, short_weight, blocks):
    span, chans = key_rows.shape
    lanes = chans // blocks
    chips = blocks // 2
    shapes = [(span, lanes), (chips - 1, span, lanes), (chips, span, lanes)]
    return pl.pallas_call(
        gate_in_kernel,
        in_specs=[SMEM, HBM, HBM, VMEM, VMEM],
        out_specs=[VMEM] * 3,
        out_shape=[jax.ShapeDtypeStruct(shape, BF16) for shape in shapes],
        scratch_shapes=[
            pltpu.VMEM((chips, 2, span, 2 * lanes), BF16),
            pltpu.SemaphoreType.DMA((chips, 2)),
        ],
        compiler_params=grant(56),
        name="gate_in",
    )(me, key_rows, value_rows, edges, short_weight)


def split_taps_kernel(me_ref, taps, *refs):
    outs, sems = refs[:-1], refs[-1]
    rows = outs[0].shape[0]
    copies = []
    for q, out in enumerate(outs):
        window = pl.ds(pl.multiple_of(((me_ref[0] // 2) ^ q) * rows, rows), rows)
        copies.append(pltpu.make_async_copy(taps.at[window, :], out, sems.at[q]))
        copies[-1].start()
    for copy in copies:
        copy.wait()


def split_taps(me, filter_taps, chips):
    chans, span = filter_taps.shape
    return pl.pallas_call(
        split_taps_kernel,
        in_specs=[SMEM, HBM],
        out_specs=[VMEM] * chips,
        out_shape=[jax.ShapeDtypeStruct((chans // chips, span), BF16)] * chips,
        scratch_shapes=[pltpu.SemaphoreType.DMA((chips,))],
        compiler_params=GRANT,
        name="split_taps",
    )(me, filter_taps)


def other_core_kernel(me_ref, *refs):
    pairs, out = refs[:-1], refs[-1]
    rows = out.shape[1]
    for q, pair in enumerate(pairs):
        window = pl.ds(pl.multiple_of((1 - me_ref[0] % 2) * rows, rows), rows)
        out[q] = pair[window, :]


def other_core(me, pairs):
    rows, span = pairs[0].shape
    return pl.pallas_call(
        other_core_kernel,
        in_specs=[SMEM] + [VMEM] * len(pairs),
        out_specs=VMEM,
        out_shape=jax.ShapeDtypeStruct((len(pairs), rows // 2, span), BF16),
        compiler_params=GRANT,
        name="other_core",
    )(me, *pairs)


def pair_kernel(same, swapped, *outs):
    for q, out in enumerate(outs):
        out[0] = same[q]
        out[1] = swapped[q + 1]


def pair_up(same, swapped):
    count, span, lanes = same.shape
    return pl.pallas_call(
        pair_kernel,
        out_shape=[jax.ShapeDtypeStruct((2, span, lanes), BF16)] * count,
        in_specs=[VMEM] * 2,
        out_specs=[VMEM] * count,
        compiler_params=GRANT,
        name="pair_up",
    )(same, swapped)


def mix_query_kernel(query, edges, weight, out):
    out[...] = shifted_mix(query[...].astype(F32), edges[0:2].astype(F32), weight[:, 0, :])


def mix_query(query_rows, edges, short_weight):
    span, chans = query_rows.shape
    lanes = chans // 4
    return pl.pallas_call(
        mix_query_kernel,
        grid=(4,),
        in_specs=[
            pl.BlockSpec((span, lanes), lambda g: (0, g)),
            pl.BlockSpec((6, lanes), lambda g: (0, g)),
            pl.BlockSpec((3, 3, lanes), lambda g: (0, 0, g)),
        ],
        out_specs=pl.BlockSpec((span, lanes), lambda g: (0, g)),
        out_shape=jax.ShapeDtypeStruct((span, chans), F32),
        compiler_params=GRANT,
        name="mix_query",
    )(query_rows, edges, short_weight)


def after(values, others):
    return lax.optimization_barrier((values, others))[0]


HEAD, PASS, ADD = 0, 1, 2
SENT = np.array(
    [
        (HEAD, ADD, ADD, 2, 1),
        (ADD, PASS, ADD, 3, 2),
        (PASS, ADD, PASS, 3, 3),
        (PASS, PASS, PASS, 3, 3),
    ],
    np.int32,
)


def gate_out_kernel(blocks, spot, *refs):
    stay, swapped, *others = refs[: blocks // 2 + 1]
    mixed, far_weight, gated, sent = refs[blocks // 2 + 1 :]
    convs = [stay, swapped.at[0]] + [ref.at[core] for ref in others for core in range(2)]
    lanes = convs[0].shape[1]
    rows = gated.shape[1]
    for m in range(blocks):
        window = pl.ds(pl.multiple_of((spot[0] ^ m) * lanes, lanes), lanes)
        piece = (mixed[:, window] * convs[m][...].astype(F32)).astype(BF16)
        gated[0, :, window] = piece[:rows]
        gated[1, :, window] = piece[rows:]
    first_sent(spot, gated, far_weight, sent)


def first_sent(spot, gated, far_weight, sent):
    @pl.when(spot[1] == 0)
    def _():
        term = jnp.dot(gated[1], far_weight[...], preferred_element_type=F32)
        sent[...] = term.astype(BF16)

    @pl.when(spot[1] != 0)
    def _():
        sent[...] = gated[0]


def gate_out(spot, convs, mixed, far_weight):
    span, chans = mixed.shape
    return pl.pallas_call(
        partial(gate_out_kernel, 2 * len(convs) - 2),
        in_specs=[SMEM] + [VMEM] * (len(convs) + 2),
        out_specs=[VMEM] * 2,
        out_shape=[
            jax.ShapeDtypeStruct((2, span // 2, chans), BF16),
            jax.ShapeDtypeStruct((span // 2, chans), BF16),
        ],
        compiler_params=GRANT,
        name="gate_out",
    )(spot, *convs, mixed, far_weight)


def partner_sent(spot, gated, far_weight):
    return pl.pallas_call(
        first_sent,
        in_specs=[SMEM, VMEM, VMEM],
        out_specs=VMEM,
        out_shape=jax.ShapeDtypeStruct(gated.shape[1:], BF16),
        compiler_params=GRANT,
        cost_estimate=cost(1),
        name="partner_sent",
    )(spot, gated, far_weight)


def step_kernel(step, plan, head, term, got, out):
    mode = plan[step - 1]

    @pl.when(mode == HEAD)
    def _():
        out[...] = head[...]

    @pl.when(mode == PASS)
    def _():
        out[...] = got[...]

    @pl.when(mode == ADD)
    def _():
        out[...] = (term[...].astype(F32) + got[...].astype(F32)).astype(BF16)


def next_step(plan, step, chain, gated, terms, got):
    rows, chans = got.shape
    whole = pl.BlockSpec((rows, chans), lambda g, plan: (0, 0))
    return pl.pallas_call(
        partial(step_kernel, step),
        grid_spec=pltpu.PrefetchScalarGridSpec(
            num_scalar_prefetch=1,
            grid=(1,),
            in_specs=[
                pl.BlockSpec((None, rows, chans), lambda g, plan: (0, 0, 0)),
                pl.BlockSpec(
                    (None, None, rows, chans), lambda g, plan: (chain, step // 3, 0, 0)
                ),
                whole,
            ],
            out_specs=whole,
        ),
        out_shape=jax.ShapeDtypeStruct((rows, chans), BF16),
        compiler_params=GRANT,
        cost_estimate=cost(1),
        name="next_step",
    )(plan, gated, terms, got)


def terms_kernel(plan, mine, partners, weight, out, held, sems):
    count, chans = held.shape[:2]
    copies = []
    for k in range(count):
        columns = pl.ds(pl.multiple_of(plan[3 + k] * chans, chans), chans)
        copies.append(pltpu.make_async_copy(weight.at[:, columns], held.at[k], sems.at[k]))
        copies[-1].start()
    for k, copy in enumerate(copies):
        copy.wait()
        for chain, gated in enumerate((mine, partners)):
            term = jnp.dot(gated[1], held[k], preferred_element_type=F32)
            out[chain, k] = term.astype(BF16)


def sent_terms(plan, mine, partners, out_weight):
    _, rows, chans = mine.shape
    return pl.pallas_call(
        terms_kernel,
        in_specs=[SMEM, VMEM, VMEM, HBM],
        out_specs=VMEM,
        out_shape=jax.ShapeDtypeStruct((2, 2, rows, chans), BF16),
        scratch_shapes=[pltpu.VMEM((2, chans, chans), BF16), pltpu.SemaphoreType.DMA((2,))],
        compiler_params=GRANT,
        cost_estimate=cost(4),
        name="sent_terms",
    )(plan, mine, partners, out_weight)


def pick_weight(out_weight):
    stages, blocks = lax.axis_size("tp"), lax.axis_size("ctx")
    stage, place = lax.axis_index("tp"), lax.axis_index("ctx")
    chans = out_weight.shape[0]
    hops = jnp.where(place % 2 == 0, 1, stages - 1)
    corners = jnp.stack([place // 2, (stage + hops) % stages, place, (stage + 2) % stages])
    return weight_corners(corners.astype(jnp.int32), out_weight, blocks)


def turn_weight(parts):
    stages, blocks = lax.axis_size("tp"), lax.axis_size("ctx")
    found = []
    for part, static in zip(parts, ((1, stages - 1), (2, 2))):
        route = [
            (c * stages + k, c * stages + (k + static[c % 2]) % stages)
            for c in range(blocks)
            for k in range(stages)
        ]
        found.append(lax.ppermute(part, ("ctx", "tp"), route))
    return found


def corners_kernel(corners, weight, *refs):
    outs, sems = refs[:-1], refs[-1]
    copies = []
    for n, out in enumerate(outs):
        rows, chans = out.shape
        row = pl.multiple_of(corners[2 * n] * rows, rows)
        column = pl.multiple_of(corners[2 * n + 1] * chans, chans)
        source = weight.at[pl.ds(row, rows), pl.ds(column, chans)]
        copies.append(pltpu.make_async_copy(source, out, sems.at[n]))
        copies[-1].start()
    for copy in copies:
        copy.wait()


def weight_corners(corners, out_weight, blocks):
    chans = out_weight.shape[0]
    shapes = [(2 * chans // blocks, chans), (chans // blocks, chans)]
    return pl.pallas_call(
        corners_kernel,
        in_specs=[SMEM, HBM],
        out_specs=[VMEM] * 2,
        out_shape=[jax.ShapeDtypeStruct(shape, BF16) for shape in shapes],
        scratch_shapes=[pltpu.SemaphoreType.DMA((2,))],
        compiler_params=grant(56),
        name="weight_corners",
    )(corners, out_weight)


def gather_weight(part):
    devices = range(lax.axis_size("ctx"))
    near = [(i, i ^ (4 if i & 1 else 2)) for i in devices]
    other = [(i, i ^ (2 if i & 1 else 4)) for i in devices]
    two = [part, lax.ppermute(part, "ctx", near)]
    return jnp.stack(two), jnp.stack([lax.ppermute(x, "ctx", other) for x in two])


def pairs_of(refs):
    return list(zip(refs[::2], refs[1::2]))


def spots(first, pair):
    return (first, pair[0]), (first + 2, pair[1])


def add_parts(order, data, *weights):
    total = None
    for first, weight in weights:
        count, lanes, columns = weight.shape
        picked = []
        for q in range(count):
            index = order[first + q]
            index = index // 2 if lanes == 2 * SUB else index
            picked.append(data[:, pl.ds(pl.multiple_of(index * lanes, lanes), lanes)])
        block = weight[...].reshape(count * lanes, columns)
        picked = jnp.concatenate(picked, axis=1)
        term = jnp.dot(picked, block, preferred_element_type=F32)
        total = term if total is None else total + term
    return total


def early_kernel(order, mine, got0, got1, partner0, partner1, weight, *refs):
    (near, near2, far2), (out, own, first, own_weight, sem) = pairs_of(refs[:6]), refs[6:]
    turn_count = order[8]
    rows, chans = got0.shape
    columns = pl.ds(pl.multiple_of(order[9] * chans, chans), chans)
    copy = pltpu.make_async_copy(weight.at[:, columns], own_weight, sem)
    copy.start()

    @pl.when(turn_count >= 2)
    def _():
        first[:rows, :] = got0[...]
        first[rows:, :] = partner0[...]

    @pl.when(turn_count < 2)
    def _():
        first[:rows, :] = got1[...]
        first[rows:, :] = partner1[...]

    @pl.when(turn_count >= 1)
    def _():
        out[...] = add_parts(order, first, *spots(0, near))

    @pl.when(turn_count < 1)
    def _():
        out[...] = jnp.zeros_like(out)

    @pl.when(turn_count == 3)
    def _():
        first[:rows, :] = got1[...]
        first[rows:, :] = partner1[...]
        out[...] += add_parts(order, first, *spots(0, near2), *spots(4, far2))

    copy.wait()
    out[:rows, :] += jnp.dot(mine[0], own_weight[...], preferred_element_type=F32)
    own[...] = jnp.dot(mine[1], own_weight[...], preferred_element_type=F32)


def early_sum(order, mine, arrivals, out_weight, weights):
    _, rows, chans = mine.shape
    whole = lambda shape: pl.BlockSpec(shape, lambda g, order: (0,) * len(shape))
    return pl.pallas_call(
        early_kernel,
        grid_spec=pltpu.PrefetchScalarGridSpec(
            num_scalar_prefetch=1,
            grid=(1,),
            in_specs=[whole(mine.shape)]
            + [whole((rows, chans))] * 4
            + [HBM]
            + [whole(x.shape) for x in weights],
            out_specs=[whole((2 * rows, chans)), whole((rows, chans))],
            scratch_shapes=[
                pltpu.VMEM((2 * rows, chans), BF16),
                pltpu.VMEM((chans, chans), BF16),
                pltpu.SemaphoreType.DMA,
            ],
        ),
        out_shape=[
            jax.ShapeDtypeStruct((2 * rows, chans), F32),
            jax.ShapeDtypeStruct((rows, chans), F32),
        ],
        compiler_params=grant(24),
        cost_estimate=cost(5),
        name="early_sum",
    )(order, mine, *arrivals, out_weight, *weights)


def late_sum(order, early, got2, got3, weights, total):
    behind = order[8]

    @pl.when(behind < 2)
    def _():
        total[...] = early[...]

    @pl.when(behind == 2)
    def _():
        total[...] = early[...] + add_parts(order, got2, *spots(0, weights[0]), *spots(4, weights[1]))

    @pl.when(behind == 3)
    def _():
        total[...] = early[...] + add_parts(order, got3, *spots(4, weights[2]))

    summed = jnp.where(behind == 3, got2[...].astype(F32), got3[...].astype(F32))
    return jnp.where(behind == 0, 0.0, summed)


def partner_kernel(order, early, got2, got3, *refs):
    weights, (out, total) = pairs_of(refs[:6]), refs[6:]
    out[1] = late_sum(order, early, got2, got3, weights, total).astype(BF16)
    out[0] = total[...].astype(BF16)


def partner_sum(order, early, arrivals, weights):
    rows, chans = arrivals[0].shape
    whole = lambda shape: pl.BlockSpec(shape, lambda g, order: (0,) * len(shape))
    return pl.pallas_call(
        partner_kernel,
        grid_spec=pltpu.PrefetchScalarGridSpec(
            num_scalar_prefetch=1,
            grid=(1,),
            in_specs=[pl.BlockSpec((rows, chans), lambda g, order: (1, 0))]
            + [whole((rows, chans))] * 2
            + [whole(x.shape) for x in weights],
            out_specs=whole((2, rows, chans)),
            scratch_shapes=[pltpu.VMEM((rows, chans), F32)],
        ),
        out_shape=jax.ShapeDtypeStruct((2, rows, chans), BF16),
        compiler_params=grant(24),
        cost_estimate=cost(2),
        name="partner_sum",
    )(order, early, *arrivals, *weights)


def mine_kernel(order, early, own, got2, got3, *refs):
    weights, (out, total) = pairs_of(refs[:6]), refs[6:]
    rows = early.shape[0]
    out[rows:, :] = late_sum(order, early, got2, got3, weights, total) + own[...]
    out[:rows, :] = total[...]


def mine_sum(order, early, own, arrivals, weights):
    rows, chans = arrivals[0].shape
    whole = lambda shape: pl.BlockSpec(shape, lambda g, order: (0,) * len(shape))
    return pl.pallas_call(
        mine_kernel,
        grid_spec=pltpu.PrefetchScalarGridSpec(
            num_scalar_prefetch=1,
            grid=(1,),
            in_specs=[pl.BlockSpec((rows, chans), lambda g, order: (0, 0))]
            + [whole((rows, chans))] * 3
            + [whole(x.shape) for x in weights],
            out_specs=whole((2 * rows, chans)),
            scratch_shapes=[pltpu.VMEM((rows, chans), F32)],
        ),
        out_shape=jax.ShapeDtypeStruct((2 * rows, chans), F32),
        compiler_params=grant(24),
        cost_estimate=cost(3),
        name="mine_sum",
    )(order, early, own, *arrivals, *weights)


def join_kernel(mine, partners, out):
    rows = partners.shape[1]
    for half in range(2):
        part = slice(half * rows, (half + 1) * rows)
        out[part, :] = (mine[part, :] + partners[half].astype(F32)).astype(BF16)


def join_sums(mine, partners):
    return pl.pallas_call(
        join_kernel,
        in_specs=[VMEM] * 2,
        out_specs=VMEM,
        out_shape=jax.ShapeDtypeStruct(mine.shape, BF16),
        compiler_params=GRANT,
        name="join_sums",
    )(mine, partners)


def weight_order():
    place, stage = lax.axis_index("ctx"), lax.axis_index("tp")
    up = place % 2 == 0
    last = lax.axis_size("tp") - 1
    a = jnp.where(up, 2, 4)
    masks = [0 * a, a, 6 - a, 0 * a + 6]
    swapped = [0 * a + 1, (6 - a) ^ 1, a ^ 1, 0 * a + 7]
    parts = [place ^ mask for mask in masks + swapped]
    return jnp.stack(parts + [jnp.where(up, stage, last - stage), stage]).astype(jnp.int32)


def project(spot, plan, order, convs, mixed, out_weight, weight_parts):
    stages, blocks = lax.axis_size("tp"), lax.axis_size("ctx")
    chans = out_weight.shape[0]
    far_weight = lax.dynamic_slice(out_weight, (0, spot[2] * chans), (chans, chans))
    mine, sent = gate_out(spot, convs, mixed, far_weight)
    route = []
    for c in range(blocks):
        for k in range(stages):
            to = k + (1 if c % 2 == 0 else -1)
            if 0 <= to < stages:
                route.append((c * stages + k, c * stages + to))
    onward = lambda x: lax.ppermute(x, ("ctx", "tp"), route)
    core_swap = lambda x: lax.ppermute(x, "ctx", [(i, i ^ 1) for i in range(blocks)])
    partners = core_swap(mine)
    partner_first = partner_sent(spot, partners, far_weight)
    got = [[onward(sent), onward(partner_first)]]
    terms = sent_terms(plan, mine, partners, out_weight)
    steps = []
    for step in range(1, stages):
        row = []
        for chain, gated in enumerate((mine, partners)):
            row.append(next_step(plan, step, chain, gated, terms, got[-1][chain]))
        steps.append(row)
        got.append([onward(x) for x in row])

    near, near2 = (gather_weight(part) for part in after(weight_parts, partner_first))
    far2, far = ([core_swap(x) for x in pair] for pair in (near2, near))
    arrivals = [got[0][0], got[1][0], got[0][1], got[1][1]]
    early, own = early_sum(order, mine, arrivals, out_weight, (*near, *near2, *far2))
    late = (*near2, *far2, *far)
    theirs = partner_sum(after(order, got[3][0]), early, [got[2][1], got[3][1]], late)
    ours = mine_sum(order, early, own, [got[2][0], got[3][0]], late)
    return join_sums(ours, core_swap(theirs))


def fast_per_device(
    query_rows, key_rows, value_rows, short_weight, skip_gain, filter_taps, out_weight
):
    span, chans = query_rows.shape
    blocks, stages = lax.axis_size("ctx"), lax.axis_size("tp")
    lanes = chans // blocks
    length = span * blocks
    radix = 2 * length // SUB
    place, stage = lax.axis_index("ctx"), lax.axis_index("tp")
    me = place.astype(jnp.int32).reshape(1)
    up = place % 2 == 0
    behind = jnp.where(up, stage, stages - 1 - stage)
    far = jnp.where(up, stages - 1, 0)
    spot = jnp.stack([place, behind, far]).astype(jnp.int32)
    plan = lax.dynamic_index_in_dim(jnp.asarray(SENT), behind, keepdims=False)
    plan = jnp.where(up | (jnp.arange(5) < 3), plan, stages - 1 - plan)
    me, spot, plan, order = lax.optimization_barrier((me, spot, plan, weight_order()))
    skip = lax.dynamic_slice(skip_gain, (place * lanes,), (lanes,)).reshape(1, lanes)
    forward, inverse = (jnp.asarray(t) for t in dft_tables(2 * length))
    twiddle = jnp.asarray(twiddle_table(radix))
    devices = range(blocks)
    core_swap = lambda x: lax.ppermute(x, "ctx", [(i, i ^ 1) for i in devices])
    to_chips = lambda xs: [
        lax.ppermute(x, "ctx", [(i, i ^ (2 * q + 2)) for i in devices])
        for q, x in enumerate(xs)
    ]
    edges = passed_along(rims(query_rows, key_rows, value_rows), "ctx", 1)
    pairs = split_taps(after(me, edges), filter_taps, blocks // 2)
    pairs = [pairs[0]] + to_chips(pairs[1:])
    weight_parts = pick_weight(out_weight)
    stay, same, swap = gate_in(after(me, weight_parts), key_rows, value_rows, edges, short_weight, blocks)
    swapped = core_swap(swap)
    packed = pair_up(same, swapped)
    others = to_chips(packed)
    taps_swapped = core_swap(other_core(me, pairs))
    mixed = mix_query(query_rows, edges, short_weight)
    spectra = taps_spectra_of(me, pairs, taps_swapped, twiddle, forward)
    weight_parts = turn_weight(after(weight_parts, taps_swapped))
    conv = long_conv(me, stay, swapped, others, spectra, twiddle, forward, inverse, skip)
    stay, same, swap = spread(after(me, weight_parts), conv, blocks)
    swapped = core_swap(swap)
    convs = [stay, swapped] + to_chips(pair_up(same, swapped))
    return project(spot, plan, order, convs, mixed, out_weight, weight_parts)


def per_device(*arrays):
    span, chans = arrays[0].shape
    blocks = lax.axis_size("ctx")
    suits = blocks == 8 and lax.axis_size("tp") == 4 and span == 512 and chans == 8 * SUB
    return (fast_per_device if suits else general_per_device)(*arrays)


def solution(mesh):
    placed = (
        P("ctx", "tp"),
        P("ctx", "tp"),
        P("ctx", "tp"),
        P(None, None, "tp"),
        P("tp"),
        P("tp", "ctx"),
        P("tp", None),
    )
    return jax.shard_map(
        per_device, mesh=mesh, in_specs=placed, out_specs=P("ctx", "tp"), check_vma=False
    )
```

```python
from functools import partial
import math

import jax
import jax.numpy as jnp
import numpy as np
from jax import lax
from jax.experimental import pallas as pl
from jax.experimental.pallas import tpu as pltpu
from jax.sharding import PartitionSpec as P

TRIPLE = lax.Precision.HIGH


def passed_along(block, axis, distance):
    devices = range(lax.axis_size(axis))
    route = [(i - distance, i) for i in devices if i - distance in devices]
    return lax.ppermute(block, axis, route)


def angle_table(left, right, offset, period):
    rows = lax.broadcasted_iota(jnp.int32, (left, right), 0)
    cols = lax.broadcasted_iota(jnp.int32, (left, right), 1) + offset
    turns = rows * cols % period
    return turns.astype(jnp.float32) * (2.0 * math.pi / period)


def inner_spectrum(rows, table_high, table_low):
    upper = jnp.dot(rows, table_high, preferred_element_type=jnp.float32)
    lower = jnp.dot(rows, table_low, preferred_element_type=jnp.float32)
    return upper + lower


def block_mix(real_component, imaginary_component, cosine_lookup, sine_lookup, sign):
    multiplier = partial(jnp.einsum, precision=TRIPLE, preferred_element_type=jnp.float32)
    cosine_real = multiplier("id,rdy->riy", cosine_lookup, real_component)
    cosine_imaginary = multiplier("id,rdy->riy", cosine_lookup, imaginary_component)
    sine_real = multiplier("id,rdy->riy", sine_lookup, real_component)
    sine_imaginary = multiplier("id,rdy->riy", sine_lookup, imaginary_component)
    return (cosine_real + sign * sine_imaginary, cosine_imaginary - sign * sine_real)


def general_per_device(query_rows, key_rows, value_rows, short_weight, skip_gain, filter_taps, out_weight):
    span = query_rows.shape[0]
    chans = query_rows.shape[1]
    blocks = lax.axis_size("ctx")
    group = chans // blocks
    period = 2 * span
    padded = 2 * blocks
    forward = angle_table(span, period, 0, period)
    forward = jnp.concatenate([jnp.cos(forward), -jnp.sin(forward)], axis=1)
    table_high = forward.astype(jnp.bfloat16)
    table_low = (forward - table_high.astype(jnp.float32)).astype(jnp.bfloat16)
    parity = 1.0 - 2.0 * (jnp.arange(period) % 2).astype(jnp.float32)
    parity = jnp.concatenate([parity, parity])
    stacked = jnp.stack([query_rows, key_rows, value_rows])
    rims = passed_along(stacked[:, -2:, :], "ctx", 1)
    extended = jnp.concatenate([rims, stacked], axis=1).astype(jnp.float32)
    mixed = (
        short_weight[0][:, None, :] * extended[:, 2:]
        + short_weight[1][:, None, :] * extended[:, 1:-1]
        + short_weight[2][:, None, :] * extended[:, :span]
    )
    gated_in = (mixed[1] * mixed[2]).astype(jnp.bfloat16)
    gated_t = gated_in.T
    inputs_local, taps_local = (
        lax.all_to_all(gated_t, "ctx", split_axis=0, concat_axis=1, tiled=True),
        lax.all_to_all(filter_taps, "ctx", split_axis=0, concat_axis=1, tiled=True),
    )
    spectra = inner_spectrum(
        taps_local.reshape(group * blocks, span), table_high, table_low
    ).reshape(group, blocks, 2 * period)
    earlier = jnp.concatenate(
        [jnp.zeros((group, 1, 2 * period), jnp.float32), spectra[:, :-1]], axis=1
    )
    kernel_spec = earlier + parity * spectra
    input_spec = inner_spectrum(
        inputs_local.reshape(group * blocks, span), table_high, table_low
    ).reshape(group, blocks, 2 * period)
    block_angle = angle_table(padded, blocks, 0, padded)
    cos_fwd = jnp.cos(block_angle)
    sin_fwd = jnp.sin(block_angle)
    input_re, input_im = block_mix(
        input_spec[..., :period], input_spec[..., period:], cos_fwd, sin_fwd, 1.0
    )
    kernel_re, kernel_im = block_mix(
        kernel_spec[..., :period], kernel_spec[..., period:], cos_fwd, sin_fwd, 1.0
    )
    product_re = input_re * kernel_re - input_im * kernel_im
    product_im = input_re * kernel_im + input_im * kernel_re
    back_angle = angle_table(blocks, padded, 0, padded)
    out_re, out_im = block_mix(
        product_re, product_im, jnp.cos(back_angle), jnp.sin(back_angle), -1.0
    )
    inverse = angle_table(period, span, span, period)
    inverse = jnp.concatenate([jnp.cos(inverse), -jnp.sin(inverse)], axis=0) * (
        1.0 / (period * padded)
    )
    joined = jnp.concatenate([out_re, out_im], axis=2).reshape(group * blocks, 2 * period)
    long_local = jnp.dot(
        joined, inverse, precision=TRIPLE, preferred_element_type=jnp.float32
    ).reshape(group, blocks * span)
    long_t = lax.all_to_all(
        long_local.astype(jnp.bfloat16), "ctx", split_axis=1, concat_axis=0, tiled=True
    ).astype(long_local.dtype)
    conv_t = (long_t + skip_gain[:, None] * gated_t.astype(jnp.float32)).astype(jnp.bfloat16)
    gated_out = (mixed[0].T * conv_t.astype(jnp.float32)).astype(jnp.bfloat16)
    term = lax.dot_general(
        gated_out, out_weight, (((0,), (0,)), ((), ())), preferred_element_type=jnp.float32
    )
    return lax.psum_scatter(term.astype(jnp.bfloat16), "tp", scatter_dimension=1, tiled=True)


SUB = 128
F32 = jnp.float32
BF16 = jnp.bfloat16


def split_table(matrix):
    high = matrix.astype(jnp.bfloat16)
    low = (matrix - high.astype(np.float32)).astype(jnp.bfloat16)
    return np.concatenate([high, high, low], axis=1)


def dft_tables(period):
    index = np.arange(SUB)
    turns = np.outer(index, index) % SUB * (2.0 * np.pi / SUB)
    cos, sin = np.cos(turns), np.sin(turns)
    forward = np.block([[cos, sin], [-sin, cos]]).astype(np.float32)
    inverse = (np.block([[cos, -sin], [sin, cos]]) / period).astype(np.float32)
    return split_table(forward), split_table(inverse)


def twiddle_table(radix):
    half = radix // 2
    turns = np.outer(np.arange(SUB), np.arange(half + 1)) * (2.0 * np.pi / (radix * SUB))
    return np.concatenate([np.cos(turns), -np.sin(turns)], axis=1).astype(np.float32)


def times(value, factor):
    return None if value is None else value * factor


def plus(left, right):
    if left is None:
        return right
    return left if right is None else left + right


def minus(left, right):
    if right is None:
        return left
    return -right if left is None else left - right


def rotate(value, turn):
    real, imag = value
    cos, sin = math.cos(2 * math.pi * turn), math.sin(2 * math.pi * turn)
    if abs(cos - sin) < 1e-12 and imag is not None:
        return (real + imag) * cos, (imag - real) * cos
    return plus(times(real, cos), times(imag, sin)), minus(times(imag, cos), times(real, sin))


def real_forward(values):
    points = 2 * len(values)
    if points == 2:
        return [(values[0], None), (values[0], None)]
    even, odd = real_forward(values[0::2]), real_forward(values[1::2])
    bins = [None] * (points // 2 + 1)
    bins[0] = (even[0][0] + odd[0][0], None)
    bins[points // 2] = (even[0][0] - odd[0][0], None)
    quarter = points // 4
    for k in range(1, quarter):
        turned = rotate(odd[k], k / points)
        bins[k] = (even[k][0] + turned[0], even[k][1] + turned[1])
        bins[points // 2 - k] = (even[k][0] - turned[0], turned[1] - even[k][1])
    bins[quarter] = (even[quarter][0], -odd[quarter][0])
    return bins


def real_inverse(bins):
    half = len(bins) - 1
    points = 2 * half
    if points == 2:
        return [bins[0][0] + bins[1][0]]
    even, odd = [], []
    for k in range(half // 2 + 1):
        ahead, back = bins[k], bins[half - k]
        if k == 0:
            even.append((ahead[0] + back[0], None))
            odd.append((ahead[0] - back[0], None))
        elif k == half // 2:
            even.append((ahead[0] * 2.0, None))
            odd.append((ahead[1] * -2.0, None))
        else:
            even.append((ahead[0] + back[0], ahead[1] - back[1]))
            difference = (ahead[0] - back[0], ahead[1] + back[1])
            odd.append(rotate(difference, -k / points))
    even, odd = real_inverse(even), real_inverse(odd)
    return [value for pair in zip(even, odd) for value in pair]


def split_dot(table, data):
    high = data.astype(BF16)
    low = (data - high.astype(F32)).astype(BF16)
    return jnp.dot(
        table[...], jnp.concatenate([high, low, high], axis=0), preferred_element_type=F32
    )


def over_pairs(count, pair):
    whole = count // 4 * 4
    lax.fori_loop(0, whole, pair, 0, unroll=4)
    for p in range(whole, count):
        pair(p, 0)


def first_stage(series, spectra, twiddle):
    half = series.shape[0] // SUB
    lanes = series.shape[1]

    def slab(step, carry):
        row = pl.multiple_of(step * 8, 8)
        values = [series[pl.ds(SUB * n + row, 8), :] for n in range(half)]
        factors = twiddle[pl.ds(row, 8), :]
        for k, (real, imag) in enumerate(real_forward(values)):
            if k == 0:
                spectra[0, pl.ds(row, 8), :] = real
                spectra[0, pl.ds(SUB + row, 8), :] = jnp.zeros_like(real)
                continue
            cos = jnp.broadcast_to(factors[:, k : k + 1], (8, lanes))
            sin = jnp.broadcast_to(factors[:, half + 1 + k : half + 2 + k], (8, lanes))
            if imag is None:
                spectra[k, pl.ds(row, 8), :] = real * cos
                spectra[k, pl.ds(SUB + row, 8), :] = real * sin
            else:
                spectra[k, pl.ds(row, 8), :] = real * cos - imag * sin
                spectra[k, pl.ds(SUB + row, 8), :] = real * sin + imag * cos
        return carry

    lax.fori_loop(0, SUB // 8, slab, 0)
    for k in range(half + 1, spectra.shape[0]):
        spectra[k] = jnp.zeros(spectra.shape[1:], F32)


def last_stage(spectra, series, twiddle):
    half = series.shape[0] // SUB
    lanes = series.shape[1]

    def slab(step, carry):
        row = pl.multiple_of(step * 8, 8)
        factors = twiddle[pl.ds(row, 8), :]
        bins = []
        for k in range(half + 1):
            real = spectra[k, pl.ds(row, 8), :]
            if k == 0:
                bins.append((real, None))
                continue
            imag = spectra[k, pl.ds(SUB + row, 8), :]
            cos = jnp.broadcast_to(factors[:, k : k + 1], (8, lanes))
            sin = jnp.broadcast_to(factors[:, half + 1 + k : half + 2 + k], (8, lanes))
            turned = real * cos + imag * sin
            bins.append((turned, None if k == half else imag * cos - real * sin))
        for n, value in enumerate(real_inverse(bins)):
            series[pl.ds(SUB * n + row, 8), :] = value
        return carry

    lax.fori_loop(0, SUB // 8, slab, 0)


def taps_kernel(chips, me_ref, *refs):
    pairs, (swapped, twiddle, forward, spectra_out, series, spectra) = refs[:chips], refs[chips:]
    _, lanes, span = swapped.shape
    mine = pl.ds(pl.multiple_of(me_ref[0] % 2 * lanes, lanes), lanes)
    for q in range(chips):
        for m, piece in ((2 * q, pairs[q][mine, :]), (2 * q + 1, swapped[q])):
            start = pl.multiple_of((me_ref[0] ^ m) * span, span)
            series[pl.ds(start, span), :] = piece.astype(F32).T
    first_stage(series, spectra, twiddle)

    def pair(p, carry):
        data = jnp.concatenate([spectra[2 * p], spectra[2 * p + 1]], axis=1)
        spectra_out[p] = split_dot(forward, data)
        return carry

    over_pairs(spectra_out.shape[0], pair)


def conv_kernel(blocks, me_ref, stay, swapped, *refs):
    others = refs[: blocks // 2 - 1]
    taps_spectra, twiddle, forward, inverse, skip = refs[blocks // 2 - 1 : blocks // 2 + 4]
    out, series, spectra = refs[blocks // 2 + 4 :]
    span, lanes = stay.shape
    pieces = [stay, swapped.at[0]] + [ref.at[core] for ref in others for core in range(2)]
    for m in range(blocks):
        start = pl.multiple_of((me_ref[0] ^ m) * span, span)
        series[pl.ds(start, span), :] = pieces[m][...].astype(F32)
    first_stage(series, spectra, twiddle)

    def pair(p, carry):
        data = jnp.concatenate([spectra[2 * p], spectra[2 * p + 1]], axis=1)
        signal = split_dot(forward, data)
        signal_re, signal_im = signal[:SUB], signal[SUB:]
        taps_re, taps_im = taps_spectra[p, :SUB, :], taps_spectra[p, SUB:, :]
        product = jnp.concatenate(
            [
                signal_re * taps_re - signal_im * taps_im,
                signal_re * taps_im + signal_im * taps_re,
            ],
            axis=0,
        )
        back = split_dot(inverse, product)
        spectra[2 * p] = back[:, :lanes]
        spectra[2 * p + 1] = back[:, lanes:]
        return carry

    over_pairs(taps_spectra.shape[0], pair)
    last_stage(spectra, out, twiddle)
    for m in range(blocks):
        window = pl.ds(m * span, span)
        out[window, :] += skip[...] * series[window, :]


def spread_kernel(me_ref, conv, stay, same, swap):
    chips, span, _ = swap.shape
    for m in range(2 * chips):
        start = pl.multiple_of((me_ref[0] ^ m) * span, span)
        piece = conv[pl.ds(start, span), :].astype(BF16)
        if m % 2:
            swap[m // 2] = piece
        elif m:
            same[m // 2 - 1] = piece
        else:
            stay[...] = piece


VMEM = pl.BlockSpec(memory_space=pltpu.VMEM)
SMEM = pl.BlockSpec(memory_space=pltpu.SMEM)
HBM = pl.BlockSpec(memory_space=pltpu.HBM)


def grant(mebibytes):
    return pltpu.CompilerParams(vmem_limit_bytes=mebibytes * 2**20)


def cost(microseconds):
    return pl.CostEstimate(flops=microseconds * 10**9, bytes_accessed=0, transcendentals=0)


GRANT = grant(16)


def taps_spectra_of(me, pairs, swapped, twiddle, forward):
    chips, lanes, span = swapped.shape
    length = 2 * chips * span
    count = (length // SUB + 2) // 2
    return pl.pallas_call(
        partial(taps_kernel, chips),
        out_shape=jax.ShapeDtypeStruct((count, 2 * SUB, 2 * lanes), F32),
        in_specs=[SMEM] + [VMEM] * (chips + 3),
        out_specs=VMEM,
        scratch_shapes=[
            pltpu.VMEM((length, lanes), F32),
            pltpu.VMEM((2 * count, 2 * SUB, lanes), F32),
        ],
        compiler_params=GRANT,
        cost_estimate=cost(8),
        name="taps_spectra",
    )(me, *pairs, swapped, twiddle, forward)


def long_conv(me, stay, swapped, others, taps_spectra, twiddle, forward, inverse, skip):
    span, lanes = stay.shape
    blocks = 2 * len(others) + 2
    pairs = taps_spectra.shape[0]
    return pl.pallas_call(
        partial(conv_kernel, blocks),
        out_shape=jax.ShapeDtypeStruct((blocks * span, lanes), F32),
        in_specs=[SMEM] + [VMEM] * (len(others) + 7),
        out_specs=VMEM,
        scratch_shapes=[
            pltpu.VMEM((blocks * span, lanes), F32),
            pltpu.VMEM((2 * pairs, 2 * SUB, lanes), F32),
        ],
        compiler_params=grant(20),
        cost_estimate=cost(20),
        name="long_conv",
    )(me, stay, swapped, *others, taps_spectra, twiddle, forward, inverse, skip)


def spread(me, conv, blocks):
    rows, lanes = conv.shape
    span, chips = rows // blocks, blocks // 2
    shapes = [(span, lanes), (chips - 1, span, lanes), (chips, span, lanes)]
    return pl.pallas_call(
        spread_kernel,
        out_shape=[jax.ShapeDtypeStruct(shape, BF16) for shape in shapes],
        in_specs=[SMEM, VMEM],
        out_specs=[VMEM] * 3,
        compiler_params=GRANT,
        name="spread",
    )(me, conv)


def shifted_mix(stream, edge, weight):
    row = lax.broadcasted_iota(jnp.int32, stream.shape, 0)
    first = jnp.where(row == 0, edge[1:2], pltpu.roll(stream, 1, 0))
    second = pltpu.roll(stream, 2, 0)
    second = jnp.where(row == 0, edge[0:1], jnp.where(row == 1, edge[1:2], second))
    return weight[0:1] * stream + weight[1:2] * first + weight[2:3] * second


def rims_kernel(query, key, value, out, held, sems):
    span = query.shape[0]
    copies = [
        pltpu.make_async_copy(ref.at[pl.ds(span - 16, 16), :], held.at[s], sems.at[s])
        for s, ref in enumerate((query, key, value))
    ]
    for copy in copies:
        copy.start()
    for s, copy in enumerate(copies):
        copy.wait()
        out[2 * s : 2 * s + 2, :] = held[s, 14:16, :]


def rims(*streams):
    chans = streams[0].shape[1]
    return pl.pallas_call(
        rims_kernel,
        in_specs=[HBM] * 3,
        out_specs=VMEM,
        out_shape=jax.ShapeDtypeStruct((6, chans), BF16),
        scratch_shapes=[pltpu.VMEM((3, 16, chans), BF16), pltpu.SemaphoreType.DMA((3,))],
        compiler_params=grant(56),
        name="rims",
    )(*streams)


def gate_in_kernel(me_ref, key, value, edges, weight, stay, same, swap, held, sems):
    lanes = stay.shape[1]
    chips = swap.shape[0]
    mine = me_ref[0] % 2
    copies = []
    for q in range(chips):
        start = pl.multiple_of(((me_ref[0] // 2) ^ q) * 2 * lanes, 2 * lanes)
        for s, ref in enumerate((key, value)):
            source = ref.at[:, pl.ds(start, 2 * lanes)]
            copies.append(pltpu.make_async_copy(source, held.at[q, s], sems.at[q, s]))
            copies[-1].start()
    for q in range(chips):
        start = ((me_ref[0] // 2) ^ q) * 2 * lanes
        for copy in copies[2 * q : 2 * q + 2]:
            copy.wait()
        for side in range(2):
            inner = pl.ds(pl.multiple_of((mine ^ side) * lanes, lanes), lanes)
            outer = pl.ds(pl.multiple_of(start + (mine ^ side) * lanes, lanes), lanes)
            mixed = [
                shifted_mix(
                    held[q, s, :, inner].astype(F32),
                    edges[2 * s + 2 : 2 * s + 4, outer].astype(F32),
                    weight[:, s + 1, outer],
                )
                for s in range(2)
            ]
            gated = (mixed[0] * mixed[1]).astype(BF16)
            if side:
                swap[q] = gated
            elif q:
                same[q - 1] = gated
            else:
                stay[...] = gated


def gate_in(me, key_rows, value_rows, edges, short_weight, blocks):
    span, chans = key_rows.shape
    lanes = chans // blocks
    chips = blocks // 2
    shapes = [(span, lanes), (chips - 1, span, lanes), (chips, span, lanes)]
    return pl.pallas_call(
        gate_in_kernel,
        in_specs=[SMEM, HBM, HBM, VMEM, VMEM],
        out_specs=[VMEM] * 3,
        out_shape=[jax.ShapeDtypeStruct(shape, BF16) for shape in shapes],
        scratch_shapes=[
            pltpu.VMEM((chips, 2, span, 2 * lanes), BF16),
            pltpu.SemaphoreType.DMA((chips, 2)),
        ],
        compiler_params=grant(56),
        name="gate_in",
    )(me, key_rows, value_rows, edges, short_weight)


def split_taps_kernel(me_ref, taps, *refs):
    outs, sems = refs[:-1], refs[-1]
    rows = outs[0].shape[0]
    copies = []
    for q, out in enumerate(outs):
        window = pl.ds(pl.multiple_of(((me_ref[0] // 2) ^ q) * rows, rows), rows)
        copies.append(pltpu.make_async_copy(taps.at[window, :], out, sems.at[q]))
        copies[-1].start()
    for copy in copies:
        copy.wait()


def split_taps(me, filter_taps, chips):
    chans, span = filter_taps.shape
    return pl.pallas_call(
        split_taps_kernel,
        in_specs=[SMEM, HBM],
        out_specs=[VMEM] * chips,
        out_shape=[jax.ShapeDtypeStruct((chans // chips, span), BF16)] * chips,
        scratch_shapes=[pltpu.SemaphoreType.DMA((chips,))],
        compiler_params=GRANT,
        name="split_taps",
    )(me, filter_taps)


def other_core_kernel(me_ref, *refs):
    pairs, out = refs[:-1], refs[-1]
    rows = out.shape[1]
    for q, pair in enumerate(pairs):
        window = pl.ds(pl.multiple_of((1 - me_ref[0] % 2) * rows, rows), rows)
        out[q] = pair[window, :]


def other_core(me, pairs):
    rows, span = pairs[0].shape
    return pl.pallas_call(
        other_core_kernel,
        in_specs=[SMEM] + [VMEM] * len(pairs),
        out_specs=VMEM,
        out_shape=jax.ShapeDtypeStruct((len(pairs), rows // 2, span), BF16),
        compiler_params=GRANT,
        name="other_core",
    )(me, *pairs)


def pair_kernel(same, swapped, *outs):
    for q, out in enumerate(outs):
        out[0] = same[q]
        out[1] = swapped[q + 1]


def pair_up(same, swapped):
    count, span, lanes = same.shape
    return pl.pallas_call(
        pair_kernel,
        out_shape=[jax.ShapeDtypeStruct((2, span, lanes), BF16)] * count,
        in_specs=[VMEM] * 2,
        out_specs=[VMEM] * count,
        compiler_params=GRANT,
        name="pair_up",
    )(same, swapped)


def mix_query_kernel(query, edges, weight, out):
    out[...] = shifted_mix(query[...].astype(F32), edges[0:2].astype(F32), weight[:, 0, :])


def mix_query(query_rows, edges, short_weight):
    span, chans = query_rows.shape
    lanes = chans // 4
    return pl.pallas_call(
        mix_query_kernel,
        grid=(4,),
        in_specs=[
            pl.BlockSpec((span, lanes), lambda g: (0, g)),
            pl.BlockSpec((6, lanes), lambda g: (0, g)),
            pl.BlockSpec((3, 3, lanes), lambda g: (0, 0, g)),
        ],
        out_specs=pl.BlockSpec((span, lanes), lambda g: (0, g)),
        out_shape=jax.ShapeDtypeStruct((span, chans), F32),
        compiler_params=GRANT,
        name="mix_query",
    )(query_rows, edges, short_weight)


def after(values, others):
    return lax.optimization_barrier((values, others))[0]


HEAD, PASS, ADD = 0, 1, 2
SENT = np.array(
    [
        (HEAD, ADD, ADD, 2, 1),
        (ADD, PASS, ADD, 3, 2),
        (PASS, ADD, PASS, 3, 3),
        (PASS, PASS, PASS, 3, 3),
    ],
    np.int32,
)


def gate_out_kernel(blocks, spot, *refs):
    stay, swapped, *others = refs[: blocks // 2 + 1]
    mixed, far_weight, gated, sent = refs[blocks // 2 + 1 :]
    convs = [stay, swapped.at[0]] + [ref.at[core] for ref in others for core in range(2)]
    lanes = convs[0].shape[1]
    rows = gated.shape[1]
    for m in range(blocks):
        window = pl.ds(pl.multiple_of((spot[0] ^ m) * lanes, lanes), lanes)
        piece = (mixed[:, window] * convs[m][...].astype(F32)).astype(BF16)
        gated[0, :, window] = piece[:rows]
        gated[1, :, window] = piece[rows:]
    first_sent(spot, gated, far_weight, sent)


def first_sent(spot, gated, far_weight, sent):
    @pl.when(spot[1] == 0)
    def _():
        term = jnp.dot(gated[1], far_weight[...], preferred_element_type=F32)
        sent[...] = term.astype(BF16)

    @pl.when(spot[1] != 0)
    def _():
        sent[...] = gated[0]


def gate_out(spot, convs, mixed, far_weight):
    span, chans = mixed.shape
    return pl.pallas_call(
        partial(gate_out_kernel, 2 * len(convs) - 2),
        in_specs=[SMEM] + [VMEM] * (len(convs) + 2),
        out_specs=[VMEM] * 2,
        out_shape=[
            jax.ShapeDtypeStruct((2, span // 2, chans), BF16),
            jax.ShapeDtypeStruct((span // 2, chans), BF16),
        ],
        compiler_params=GRANT,
        name="gate_out",
    )(spot, *convs, mixed, far_weight)


def partner_sent(spot, gated, far_weight):
    return pl.pallas_call(
        first_sent,
        in_specs=[SMEM, VMEM, VMEM],
        out_specs=VMEM,
        out_shape=jax.ShapeDtypeStruct(gated.shape[1:], BF16),
        compiler_params=GRANT,
        cost_estimate=cost(1),
        name="partner_sent",
    )(spot, gated, far_weight)


def step_kernel(step, plan, head, term, got, out):
    mode = plan[step - 1]

    @pl.when(mode == HEAD)
    def _():
        out[...] = head[...]

    @pl.when(mode == PASS)
    def _():
        out[...] = got[...]

    @pl.when(mode == ADD)
    def _():
        out[...] = (term[...].astype(F32) + got[...].astype(F32)).astype(BF16)


def next_step(plan, step, chain, gated, terms, got):
    rows, chans = got.shape
    whole = pl.BlockSpec((rows, chans), lambda g, plan: (0, 0))
    return pl.pallas_call(
        partial(step_kernel, step),
        grid_spec=pltpu.PrefetchScalarGridSpec(
            num_scalar_prefetch=1,
            grid=(1,),
            in_specs=[
                pl.BlockSpec((None, rows, chans), lambda g, plan: (0, 0, 0)),
                pl.BlockSpec(
                    (None, None, rows, chans), lambda g, plan: (chain, step // 3, 0, 0)
                ),
                whole,
            ],
            out_specs=whole,
        ),
        out_shape=jax.ShapeDtypeStruct((rows, chans), BF16),
        compiler_params=GRANT,
        cost_estimate=cost(1),
        name="next_step",
    )(plan, gated, terms, got)


def terms_kernel(plan, mine, partners, weight, out, held, sems):
    count, chans = held.shape[:2]
    copies = []
    for k in range(count):
        columns = pl.ds(pl.multiple_of(plan[3 + k] * chans, chans), chans)
        copies.append(pltpu.make_async_copy(weight.at[:, columns], held.at[k], sems.at[k]))
        copies[-1].start()
    for k, copy in enumerate(copies):
        copy.wait()
        for chain, gated in enumerate((mine, partners)):
            term = jnp.dot(gated[1], held[k], preferred_element_type=F32)
            out[chain, k] = term.astype(BF16)


def sent_terms(plan, mine, partners, out_weight):
    _, rows, chans = mine.shape
    return pl.pallas_call(
        terms_kernel,
        in_specs=[SMEM, VMEM, VMEM, HBM],
        out_specs=VMEM,
        out_shape=jax.ShapeDtypeStruct((2, 2, rows, chans), BF16),
        scratch_shapes=[pltpu.VMEM((2, chans, chans), BF16), pltpu.SemaphoreType.DMA((2,))],
        compiler_params=GRANT,
        cost_estimate=cost(4),
        name="sent_terms",
    )(plan, mine, partners, out_weight)


def pick_weight(out_weight):
    stages, blocks = lax.axis_size("tp"), lax.axis_size("ctx")
    stage, place = lax.axis_index("tp"), lax.axis_index("ctx")
    chans = out_weight.shape[0]
    hops = jnp.where(place % 2 == 0, 1, stages - 1)
    corners = jnp.stack([place // 2, (stage + hops) % stages, place, (stage + 2) % stages])
    return weight_corners(corners.astype(jnp.int32), out_weight, blocks)


def turn_weight(parts):
    stages, blocks = lax.axis_size("tp"), lax.axis_size("ctx")
    found = []
    for part, static in zip(parts, ((1, stages - 1), (2, 2))):
        route = [
            (c * stages + k, c * stages + (k + static[c % 2]) % stages)
            for c in range(blocks)
            for k in range(stages)
        ]
        found.append(lax.ppermute(part, ("ctx", "tp"), route))
    return found


def corners_kernel(corners, weight, *refs):
    outs, sems = refs[:-1], refs[-1]
    copies = []
    for n, out in enumerate(outs):
        rows, chans = out.shape
        row = pl.multiple_of(corners[2 * n] * rows, rows)
        column = pl.multiple_of(corners[2 * n + 1] * chans, chans)
        source = weight.at[pl.ds(row, rows), pl.ds(column, chans)]
        copies.append(pltpu.make_async_copy(source, out, sems.at[n]))
        copies[-1].start()
    for copy in copies:
        copy.wait()


def weight_corners(corners, out_weight, blocks):
    chans = out_weight.shape[0]
    shapes = [(2 * chans // blocks, chans), (chans // blocks, chans)]
    return pl.pallas_call(
        corners_kernel,
        in_specs=[SMEM, HBM],
        out_specs=[VMEM] * 2,
        out_shape=[jax.ShapeDtypeStruct(shape, BF16) for shape in shapes],
        scratch_shapes=[pltpu.SemaphoreType.DMA((2,))],
        compiler_params=grant(56),
        name="weight_corners",
    )(corners, out_weight)


def swap_weight(part):
    devices = range(lax.axis_size("ctx"))
    return lax.ppermute(part, "ctx", [(i, i ^ (4 if i & 1 else 2)) for i in devices])


def gather_weight(two, ready):
    devices = range(lax.axis_size("ctx"))
    other = [(i, i ^ (2 if i & 1 else 4)) for i in devices]
    near = [*two, *[lax.ppermute(x, "ctx", other) for x in two]]
    apart = near[:2] + after(near[2:], ready)
    return near + [lax.ppermute(x, "ctx", [(i, i ^ 1) for i in devices]) for x in apart]


def add_parts(order, data, parts, hops):
    chans = data.shape[1]
    if hops == 2:
        rows, row, chosen = chans // 8, chans // 4, range(8)
    else:
        rows, row, chosen = chans // 4, 0, range(4) if hops == 1 else range(4, 8)
    picked = []
    for q in chosen:
        index = order[q] if hops == 2 else order[q] // 2
        picked.append(data[:, pl.ds(pl.multiple_of(index * rows, rows), rows)])
    block = jnp.concatenate([parts[q][row : row + rows, :] for q in chosen], axis=0)
    return jnp.dot(jnp.concatenate(picked, axis=1), block, preferred_element_type=F32)


def early_kernel(order, mine, got0, got1, partner0, partner1, weight, *refs):
    parts, (out, own, first, own_weight, sem) = refs[:8], refs[8:]
    turn_count = order[8]
    rows, chans = got0.shape
    columns = pl.ds(pl.multiple_of(order[9] * chans, chans), chans)
    copy = pltpu.make_async_copy(weight.at[:, columns], own_weight, sem)
    copy.start()

    @pl.when(turn_count >= 2)
    def _():
        first[:rows, :] = got0[...]
        first[rows:, :] = partner0[...]

    @pl.when(turn_count < 2)
    def _():
        first[:rows, :] = got1[...]
        first[rows:, :] = partner1[...]

    @pl.when(turn_count >= 1)
    def _():
        out[...] = add_parts(order, first, parts, 1)

    @pl.when(turn_count < 1)
    def _():
        out[...] = jnp.zeros_like(out)

    @pl.when(turn_count == 3)
    def _():
        first[:rows, :] = got1[...]
        first[rows:, :] = partner1[...]
        out[...] += add_parts(order, first, parts, 2)

    copy.wait()
    out[:rows, :] += jnp.dot(mine[0], own_weight[...], preferred_element_type=F32)
    own[...] = jnp.dot(mine[1], own_weight[...], preferred_element_type=F32)


def early_sum(order, mine, arrivals, out_weight, weights):
    _, rows, chans = mine.shape
    whole = lambda shape: pl.BlockSpec(shape, lambda g, order: (0,) * len(shape))
    return pl.pallas_call(
        early_kernel,
        grid_spec=pltpu.PrefetchScalarGridSpec(
            num_scalar_prefetch=1,
            grid=(1,),
            in_specs=[whole(mine.shape)]
            + [whole((rows, chans))] * 4
            + [HBM]
            + [whole(x.shape) for x in weights],
            out_specs=[whole((2 * rows, chans)), whole((rows, chans))],
            scratch_shapes=[
                pltpu.VMEM((2 * rows, chans), BF16),
                pltpu.VMEM((chans, chans), BF16),
                pltpu.SemaphoreType.DMA,
            ],
        ),
        out_shape=[
            jax.ShapeDtypeStruct((2 * rows, chans), F32),
            jax.ShapeDtypeStruct((rows, chans), F32),
        ],
        compiler_params=grant(24),
        cost_estimate=cost(1),
        name="early_sum",
    )(order, mine, *arrivals, out_weight, *weights)


def late_sum(order, early, got2, got3, weights, total):
    behind = order[8]

    @pl.when(behind < 2)
    def _():
        total[...] = early[...]

    @pl.when(behind == 2)
    def _():
        total[...] = early[...] + add_parts(order, got2, weights, 2)

    @pl.when(behind == 3)
    def _():
        total[...] = early[...] + add_parts(order, got3, weights, 3)

    summed = jnp.where(behind == 3, got2[...].astype(F32), got3[...].astype(F32))
    return jnp.where(behind == 0, 0.0, summed)


def partner_kernel(order, early, got2, got3, *refs):
    weights, (out, total) = refs[:8], refs[8:]
    out[1] = late_sum(order, early, got2, got3, weights, total).astype(BF16)
    out[0] = total[...].astype(BF16)


def partner_sum(order, early, arrivals, weights):
    rows, chans = arrivals[0].shape
    whole = lambda shape: pl.BlockSpec(shape, lambda g, order: (0,) * len(shape))
    return pl.pallas_call(
        partner_kernel,
        grid_spec=pltpu.PrefetchScalarGridSpec(
            num_scalar_prefetch=1,
            grid=(1,),
            in_specs=[pl.BlockSpec((rows, chans), lambda g, order: (1, 0))]
            + [whole((rows, chans))] * 2
            + [whole(x.shape) for x in weights],
            out_specs=whole((2, rows, chans)),
            scratch_shapes=[pltpu.VMEM((rows, chans), F32)],
        ),
        out_shape=jax.ShapeDtypeStruct((2, rows, chans), BF16),
        compiler_params=grant(24),
        cost_estimate=cost(2),
        name="partner_sum",
    )(order, early, *arrivals, *weights)


def mine_kernel(order, early, own, got2, got3, *refs):
    weights, (out, total) = refs[:8], refs[8:]
    rows = early.shape[0]
    out[rows:, :] = late_sum(order, early, got2, got3, weights, total) + own[...]
    out[:rows, :] = total[...]


def mine_sum(order, early, own, arrivals, weights):
    rows, chans = arrivals[0].shape
    whole = lambda shape: pl.BlockSpec(shape, lambda g, order: (0,) * len(shape))
    return pl.pallas_call(
        mine_kernel,
        grid_spec=pltpu.PrefetchScalarGridSpec(
            num_scalar_prefetch=1,
            grid=(1,),
            in_specs=[pl.BlockSpec((rows, chans), lambda g, order: (0, 0))]
            + [whole((rows, chans))] * 3
            + [whole(x.shape) for x in weights],
            out_specs=whole((2 * rows, chans)),
            scratch_shapes=[pltpu.VMEM((rows, chans), F32)],
        ),
        out_shape=jax.ShapeDtypeStruct((2 * rows, chans), F32),
        compiler_params=grant(24),
        cost_estimate=cost(3),
        name="mine_sum",
    )(order, early, own, *arrivals, *weights)


def join_kernel(mine, partners, out):
    rows = partners.shape[1]
    for half in range(2):
        part = slice(half * rows, (half + 1) * rows)
        out[part, :] = (mine[part, :] + partners[half].astype(F32)).astype(BF16)


def join_sums(mine, partners):
    return pl.pallas_call(
        join_kernel,
        in_specs=[VMEM] * 2,
        out_specs=VMEM,
        out_shape=jax.ShapeDtypeStruct(mine.shape, BF16),
        compiler_params=GRANT,
        name="join_sums",
    )(mine, partners)


def weight_order():
    place, stage = lax.axis_index("ctx"), lax.axis_index("tp")
    up = place % 2 == 0
    last = lax.axis_size("tp") - 1
    a = jnp.where(up, 2, 4)
    masks = [0 * a, a, 6 - a, 0 * a + 6]
    swapped = [0 * a + 1, (6 - a) ^ 1, a ^ 1, 0 * a + 7]
    parts = [place ^ mask for mask in masks + swapped]
    return jnp.stack(parts + [jnp.where(up, stage, last - stage), stage]).astype(jnp.int32)


def project(spot, plan, order, convs, mixed, out_weight, weight_parts):
    stages, blocks = lax.axis_size("tp"), lax.axis_size("ctx")
    chans = out_weight.shape[0]
    far_weight = lax.dynamic_slice(out_weight, (0, spot[2] * chans), (chans, chans))
    mine, sent = gate_out(spot, convs, mixed, far_weight)
    route = []
    for c in range(blocks):
        for k in range(stages):
            to = k + (1 if c % 2 == 0 else -1)
            if 0 <= to < stages:
                route.append((c * stages + k, c * stages + to))
    onward = lambda x: lax.ppermute(x, ("ctx", "tp"), route)
    core_swap = lambda x: lax.ppermute(x, "ctx", [(i, i ^ 1) for i in range(blocks)])
    partners = core_swap(mine)
    partner_first = partner_sent(spot, partners, far_weight)
    got = [[onward(sent), onward(partner_first)]]
    terms = sent_terms(plan, mine, partners, out_weight)
    weight_part = after(jnp.concatenate(weight_parts), partner_first)
    weight_two = [weight_part, swap_weight(weight_part)]
    steps = []
    for step in range(1, stages):
        row = []
        for chain, gated in enumerate((mine, partners)):
            row.append(next_step(plan, step, chain, gated, terms, got[-1][chain]))
        steps.append(row)
        got.append([onward(x) for x in row])

    weights = gather_weight(weight_two, steps[2][0])
    arrivals = [got[0][0], got[1][0], got[0][1], got[1][1]]
    early, own = early_sum(order, mine, arrivals, out_weight, weights)
    theirs = partner_sum(after(order, got[3][0]), early, [got[2][1], got[3][1]], weights)
    ours = mine_sum(order, early, own, [got[2][0], got[3][0]], weights)
    return join_sums(ours, core_swap(theirs))


def fast_per_device(
    query_rows, key_rows, value_rows, short_weight, skip_gain, filter_taps, out_weight
):
    span, chans = query_rows.shape
    blocks, stages = lax.axis_size("ctx"), lax.axis_size("tp")
    lanes = chans // blocks
    length = span * blocks
    radix = 2 * length // SUB
    place, stage = lax.axis_index("ctx"), lax.axis_index("tp")
    me = place.astype(jnp.int32).reshape(1)
    up = place % 2 == 0
    behind = jnp.where(up, stage, stages - 1 - stage)
    far = jnp.where(up, stages - 1, 0)
    spot = jnp.stack([place, behind, far]).astype(jnp.int32)
    plan = lax.dynamic_index_in_dim(jnp.asarray(SENT), behind, keepdims=False)
    plan = jnp.where(up | (jnp.arange(5) < 3), plan, stages - 1 - plan)
    me, spot, plan, order = lax.optimization_barrier((me, spot, plan, weight_order()))
    skip = lax.dynamic_slice(skip_gain, (place * lanes,), (lanes,)).reshape(1, lanes)
    forward, inverse = (jnp.asarray(t) for t in dft_tables(2 * length))
    twiddle = jnp.asarray(twiddle_table(radix))
    devices = range(blocks)
    core_swap = lambda x: lax.ppermute(x, "ctx", [(i, i ^ 1) for i in devices])
    to_chips = lambda xs: [
        lax.ppermute(x, "ctx", [(i, i ^ (2 * q + 2)) for i in devices])
        for q, x in enumerate(xs)
    ]
    edges = passed_along(rims(query_rows, key_rows, value_rows), "ctx", 1)
    pairs = split_taps(after(me, edges), filter_taps, blocks // 2)
    pairs = [pairs[0]] + to_chips(pairs[1:])
    weight_parts = pick_weight(out_weight)
    stay, same, swap = gate_in(after(me, weight_parts), key_rows, value_rows, edges, short_weight, blocks)
    swapped = core_swap(swap)
    packed = pair_up(same, swapped)
    others = to_chips(packed)
    taps_swapped = core_swap(other_core(me, pairs))
    mixed = mix_query(query_rows, edges, short_weight)
    spectra = taps_spectra_of(me, pairs, taps_swapped, twiddle, forward)
    weight_parts = turn_weight(after(weight_parts, taps_swapped))
    conv = long_conv(me, stay, swapped, others, spectra, twiddle, forward, inverse, skip)
    stay, same, swap = spread(after(me, weight_parts), conv, blocks)
    swapped = core_swap(swap)
    convs = [stay, swapped] + to_chips(pair_up(same, swapped))
    return project(spot, plan, order, convs, mixed, out_weight, weight_parts)


def per_device(*arrays):
    span, chans = arrays[0].shape
    blocks = lax.axis_size("ctx")
    suits = blocks == 8 and lax.axis_size("tp") == 4 and span == 512 and chans == 8 * SUB
    return (fast_per_device if suits else general_per_device)(*arrays)


def solution(mesh):
    placed = (
        P("ctx", "tp"),
        P("ctx", "tp"),
        P("ctx", "tp"),
        P(None, None, "tp"),
        P("tp"),
        P("tp", "ctx"),
        P("tp", None),
    )
    return jax.shard_map(
        per_device, mesh=mesh, in_specs=placed, out_specs=P("ctx", "tp"), check_vma=False
    )
```

```python
from functools import partial
import math

import jax
import jax.numpy as jnp
import numpy as np
from jax import lax
from jax.experimental import pallas as pl
from jax.experimental.pallas import tpu as pltpu
from jax.sharding import PartitionSpec as P

TRIPLE = lax.Precision.HIGH


def passed_along(block, axis, distance):
    devices = range(lax.axis_size(axis))
    route = [(i - distance, i) for i in devices if i - distance in devices]
    return lax.ppermute(block, axis, route)


def angle_table(left, right, offset, period):
    rows = lax.broadcasted_iota(jnp.int32, (left, right), 0)
    cols = lax.broadcasted_iota(jnp.int32, (left, right), 1) + offset
    turns = rows * cols % period
    return turns.astype(jnp.float32) * (2.0 * math.pi / period)


def inner_spectrum(rows, table_high, table_low):
    upper = jnp.dot(rows, table_high, preferred_element_type=jnp.float32)
    lower = jnp.dot(rows, table_low, preferred_element_type=jnp.float32)
    return upper + lower


def block_mix(real_component, imaginary_component, cosine_lookup, sine_lookup, sign):
    multiplier = partial(jnp.einsum, precision=TRIPLE, preferred_element_type=jnp.float32)
    cosine_real = multiplier("id,rdy->riy", cosine_lookup, real_component)
    cosine_imaginary = multiplier("id,rdy->riy", cosine_lookup, imaginary_component)
    sine_real = multiplier("id,rdy->riy", sine_lookup, real_component)
    sine_imaginary = multiplier("id,rdy->riy", sine_lookup, imaginary_component)
    return (cosine_real + sign * sine_imaginary, cosine_imaginary - sign * sine_real)


def general_per_device(query_rows, key_rows, value_rows, short_weight, skip_gain, filter_taps, out_weight):
    span = query_rows.shape[0]
    chans = query_rows.shape[1]
    blocks = lax.axis_size("ctx")
    group = chans // blocks
    period = 2 * span
    padded = 2 * blocks
    forward = angle_table(span, period, 0, period)
    forward = jnp.concatenate([jnp.cos(forward), -jnp.sin(forward)], axis=1)
    table_high = forward.astype(jnp.bfloat16)
    table_low = (forward - table_high.astype(jnp.float32)).astype(jnp.bfloat16)
    parity = 1.0 - 2.0 * (jnp.arange(period) % 2).astype(jnp.float32)
    parity = jnp.concatenate([parity, parity])
    stacked = jnp.stack([query_rows, key_rows, value_rows])
    rims = passed_along(stacked[:, -2:, :], "ctx", 1)
    extended = jnp.concatenate([rims, stacked], axis=1).astype(jnp.float32)
    mixed = (
        short_weight[0][:, None, :] * extended[:, 2:]
        + short_weight[1][:, None, :] * extended[:, 1:-1]
        + short_weight[2][:, None, :] * extended[:, :span]
    )
    gated_in = (mixed[1] * mixed[2]).astype(jnp.bfloat16)
    gated_t = gated_in.T
    inputs_local, taps_local = (
        lax.all_to_all(gated_t, "ctx", split_axis=0, concat_axis=1, tiled=True),
        lax.all_to_all(filter_taps, "ctx", split_axis=0, concat_axis=1, tiled=True),
    )
    spectra = inner_spectrum(
        taps_local.reshape(group * blocks, span), table_high, table_low
    ).reshape(group, blocks, 2 * period)
    earlier = jnp.concatenate(
        [jnp.zeros((group, 1, 2 * period), jnp.float32), spectra[:, :-1]], axis=1
    )
    kernel_spec = earlier + parity * spectra
    input_spec = inner_spectrum(
        inputs_local.reshape(group * blocks, span), table_high, table_low
    ).reshape(group, blocks, 2 * period)
    block_angle = angle_table(padded, blocks, 0, padded)
    cos_fwd = jnp.cos(block_angle)
    sin_fwd = jnp.sin(block_angle)
    input_re, input_im = block_mix(
        input_spec[..., :period], input_spec[..., period:], cos_fwd, sin_fwd, 1.0
    )
    kernel_re, kernel_im = block_mix(
        kernel_spec[..., :period], kernel_spec[..., period:], cos_fwd, sin_fwd, 1.0
    )
    product_re = input_re * kernel_re - input_im * kernel_im
    product_im = input_re * kernel_im + input_im * kernel_re
    back_angle = angle_table(blocks, padded, 0, padded)
    out_re, out_im = block_mix(
        product_re, product_im, jnp.cos(back_angle), jnp.sin(back_angle), -1.0
    )
    inverse = angle_table(period, span, span, period)
    inverse = jnp.concatenate([jnp.cos(inverse), -jnp.sin(inverse)], axis=0) * (
        1.0 / (period * padded)
    )
    joined = jnp.concatenate([out_re, out_im], axis=2).reshape(group * blocks, 2 * period)
    long_local = jnp.dot(
        joined, inverse, precision=TRIPLE, preferred_element_type=jnp.float32
    ).reshape(group, blocks * span)
    long_t = lax.all_to_all(
        long_local.astype(jnp.bfloat16), "ctx", split_axis=1, concat_axis=0, tiled=True
    ).astype(long_local.dtype)
    conv_t = (long_t + skip_gain[:, None] * gated_t.astype(jnp.float32)).astype(jnp.bfloat16)
    gated_out = (mixed[0].T * conv_t.astype(jnp.float32)).astype(jnp.bfloat16)
    term = lax.dot_general(
        gated_out, out_weight, (((0,), (0,)), ((), ())), preferred_element_type=jnp.float32
    )
    return lax.psum_scatter(term.astype(jnp.bfloat16), "tp", scatter_dimension=1, tiled=True)


SUB = 128
F32 = jnp.float32
BF16 = jnp.bfloat16


def split_table(matrix):
    high = matrix.astype(jnp.bfloat16)
    low = (matrix - high.astype(np.float32)).astype(jnp.bfloat16)
    return np.concatenate([high, high, low], axis=1)


def dft_tables(period):
    index = np.arange(SUB)
    turns = np.outer(index, index) % SUB * (2.0 * np.pi / SUB)
    cos, sin = np.cos(turns), np.sin(turns)
    forward = np.block([[cos, sin], [-sin, cos]]).astype(np.float32)
    inverse = (np.block([[cos, -sin], [sin, cos]]) / period).astype(np.float32)
    return split_table(forward), split_table(inverse)


def twiddle_table(radix):
    half = radix // 2
    turns = np.outer(np.arange(SUB), np.arange(half + 1)) * (2.0 * np.pi / (radix * SUB))
    return np.concatenate([np.cos(turns), -np.sin(turns)], axis=1).astype(np.float32)


def times(value, factor):
    return None if value is None else value * factor


def plus(left, right):
    if left is None:
        return right
    return left if right is None else left + right


def minus(left, right):
    if right is None:
        return left
    return -right if left is None else left - right


def rotate(value, turn):
    real, imag = value
    cos, sin = math.cos(2 * math.pi * turn), math.sin(2 * math.pi * turn)
    if abs(cos - sin) < 1e-12 and imag is not None:
        return (real + imag) * cos, (imag - real) * cos
    return plus(times(real, cos), times(imag, sin)), minus(times(imag, cos), times(real, sin))


def real_forward(values):
    points = 2 * len(values)
    if points == 2:
        return [(values[0], None), (values[0], None)]
    even, odd = real_forward(values[0::2]), real_forward(values[1::2])
    bins = [None] * (points // 2 + 1)
    bins[0] = (even[0][0] + odd[0][0], None)
    bins[points // 2] = (even[0][0] - odd[0][0], None)
    quarter = points // 4
    for k in range(1, quarter):
        turned = rotate(odd[k], k / points)
        bins[k] = (even[k][0] + turned[0], even[k][1] + turned[1])
        bins[points // 2 - k] = (even[k][0] - turned[0], turned[1] - even[k][1])
    bins[quarter] = (even[quarter][0], -odd[quarter][0])
    return bins


def real_inverse(bins):
    half = len(bins) - 1
    points = 2 * half
    if points == 2:
        return [bins[0][0] + bins[1][0]]
    even, odd = [], []
    for k in range(half // 2 + 1):
        ahead, back = bins[k], bins[half - k]
        if k == 0:
            even.append((ahead[0] + back[0], None))
            odd.append((ahead[0] - back[0], None))
        elif k == half // 2:
            even.append((ahead[0] * 2.0, None))
            odd.append((ahead[1] * -2.0, None))
        else:
            even.append((ahead[0] + back[0], ahead[1] - back[1]))
            difference = (ahead[0] - back[0], ahead[1] + back[1])
            odd.append(rotate(difference, -k / points))
    even, odd = real_inverse(even), real_inverse(odd)
    return [value for pair in zip(even, odd) for value in pair]


def split_dot(table, data):
    high = data.astype(BF16)
    low = (data - high.astype(F32)).astype(BF16)
    return jnp.dot(
        table[...], jnp.concatenate([high, low, high], axis=0), preferred_element_type=F32
    )


def over_pairs(count, pair):
    whole = count // 4 * 4
    lax.fori_loop(0, whole, pair, 0, unroll=4)
    for p in range(whole, count):
        pair(p, 0)


def first_stage(series, spectra, twiddle):
    half = series.shape[0] // SUB
    lanes = series.shape[1]

    def slab(step, carry):
        row = pl.multiple_of(step * 8, 8)
        values = [series[pl.ds(SUB * n + row, 8), :] for n in range(half)]
        factors = twiddle[pl.ds(row, 8), :]
        for k, (real, imag) in enumerate(real_forward(values)):
            if k == 0:
                spectra[0, pl.ds(row, 8), :] = real
                spectra[0, pl.ds(SUB + row, 8), :] = jnp.zeros_like(real)
                continue
            cos = jnp.broadcast_to(factors[:, k : k + 1], (8, lanes))
            sin = jnp.broadcast_to(factors[:, half + 1 + k : half + 2 + k], (8, lanes))
            if imag is None:
                spectra[k, pl.ds(row, 8), :] = real * cos
                spectra[k, pl.ds(SUB + row, 8), :] = real * sin
            else:
                spectra[k, pl.ds(row, 8), :] = real * cos - imag * sin
                spectra[k, pl.ds(SUB + row, 8), :] = real * sin + imag * cos
        return carry

    lax.fori_loop(0, SUB // 8, slab, 0, unroll=2)
    for k in range(half + 1, spectra.shape[0]):
        spectra[k] = jnp.zeros(spectra.shape[1:], F32)


def last_stage(spectra, series, twiddle, signal, skip):
    half = series.shape[0] // SUB
    lanes = series.shape[1]

    def slab(step, carry):
        row = pl.multiple_of(step * 8, 8)
        factors = twiddle[pl.ds(row, 8), :]
        bins = []
        for k in range(half + 1):
            real = spectra[k, pl.ds(row, 8), :]
            if k == 0:
                bins.append((real, None))
                continue
            imag = spectra[k, pl.ds(SUB + row, 8), :]
            cos = jnp.broadcast_to(factors[:, k : k + 1], (8, lanes))
            sin = jnp.broadcast_to(factors[:, half + 1 + k : half + 2 + k], (8, lanes))
            turned = real * cos + imag * sin
            bins.append((turned, None if k == half else imag * cos - real * sin))
        gain = jnp.broadcast_to(skip[...], (8, lanes))
        for n, value in enumerate(real_inverse(bins)):
            rows = pl.ds(SUB * n + row, 8)
            series[rows, :] = value + gain * signal[rows, :]
        return carry

    lax.fori_loop(0, SUB // 8, slab, 0, unroll=2)


def taps_kernel(chips, me_ref, *refs):
    pairs, (swapped, twiddle, forward, spectra_out, series, spectra) = refs[:chips], refs[chips:]
    _, lanes, span = swapped.shape
    mine = pl.ds(pl.multiple_of(me_ref[0] % 2 * lanes, lanes), lanes)
    for q in range(chips):
        for m, piece in ((2 * q, pairs[q][mine, :]), (2 * q + 1, swapped[q])):
            start = pl.multiple_of((me_ref[0] ^ m) * span, span)
            series[pl.ds(start, span), :] = piece.astype(F32).T
    first_stage(series, spectra, twiddle)

    def pair(p, carry):
        data = jnp.concatenate([spectra[2 * p], spectra[2 * p + 1]], axis=1)
        spectra_out[p] = split_dot(forward, data)
        return carry

    over_pairs(spectra_out.shape[0], pair)


def conv_kernel(blocks, me_ref, stay, swapped, *refs):
    others = refs[: blocks // 2 - 1]
    taps_spectra, twiddle, forward, inverse, skip = refs[blocks // 2 - 1 : blocks // 2 + 4]
    out, series, spectra = refs[blocks // 2 + 4 :]
    span, lanes = stay.shape
    pieces = [stay, swapped.at[0]] + [ref.at[core] for ref in others for core in range(2)]
    for m in range(blocks):
        start = pl.multiple_of((me_ref[0] ^ m) * span, span)
        series[pl.ds(start, span), :] = pieces[m][...].astype(F32)
    first_stage(series, spectra, twiddle)

    def pair(p, carry):
        data = jnp.concatenate([spectra[2 * p], spectra[2 * p + 1]], axis=1)
        signal = split_dot(forward, data)
        signal_re, signal_im = signal[:SUB], signal[SUB:]
        taps_re, taps_im = taps_spectra[p, :SUB, :], taps_spectra[p, SUB:, :]
        product = jnp.concatenate(
            [
                signal_re * taps_re - signal_im * taps_im,
                signal_re * taps_im + signal_im * taps_re,
            ],
            axis=0,
        )
        back = split_dot(inverse, product)
        spectra[2 * p] = back[:, :lanes]
        spectra[2 * p + 1] = back[:, lanes:]
        return carry

    over_pairs(taps_spectra.shape[0], pair)
    last_stage(spectra, out, twiddle, series, skip)


def spread_kernel(me_ref, conv, stay, same, swap):
    chips, span, _ = swap.shape
    for m in range(2 * chips):
        start = pl.multiple_of((me_ref[0] ^ m) * span, span)
        piece = conv[pl.ds(start, span), :].astype(BF16)
        if m % 2:
            swap[m // 2] = piece
        elif m:
            same[m // 2 - 1] = piece
        else:
            stay[...] = piece


VMEM = pl.BlockSpec(memory_space=pltpu.VMEM)
SMEM = pl.BlockSpec(memory_space=pltpu.SMEM)
HBM = pl.BlockSpec(memory_space=pltpu.HBM)


def grant(mebibytes):
    return pltpu.CompilerParams(vmem_limit_bytes=mebibytes * 2**20)


def cost(microseconds):
    return pl.CostEstimate(flops=microseconds * 10**9, bytes_accessed=0, transcendentals=0)


GRANT = grant(16)


def taps_spectra_of(me, pairs, swapped, twiddle, forward):
    chips, lanes, span = swapped.shape
    length = 2 * chips * span
    count = (length // SUB + 2) // 2
    return pl.pallas_call(
        partial(taps_kernel, chips),
        out_shape=jax.ShapeDtypeStruct((count, 2 * SUB, 2 * lanes), F32),
        in_specs=[SMEM] + [VMEM] * (chips + 3),
        out_specs=VMEM,
        scratch_shapes=[
            pltpu.VMEM((length, lanes), F32),
            pltpu.VMEM((2 * count, 2 * SUB, lanes), F32),
        ],
        compiler_params=GRANT,
        cost_estimate=cost(8),
        name="taps_spectra",
    )(me, *pairs, swapped, twiddle, forward)


def long_conv(me, stay, swapped, others, taps_spectra, twiddle, forward, inverse, skip):
    span, lanes = stay.shape
    blocks = 2 * len(others) + 2
    pairs = taps_spectra.shape[0]
    return pl.pallas_call(
        partial(conv_kernel, blocks),
        out_shape=jax.ShapeDtypeStruct((blocks * span, lanes), F32),
        in_specs=[SMEM] + [VMEM] * (len(others) + 7),
        out_specs=VMEM,
        scratch_shapes=[
            pltpu.VMEM((blocks * span, lanes), F32),
            pltpu.VMEM((2 * pairs, 2 * SUB, lanes), F32),
        ],
        compiler_params=grant(20),
        cost_estimate=cost(20),
        name="long_conv",
    )(me, stay, swapped, *others, taps_spectra, twiddle, forward, inverse, skip)


def spread(me, conv, blocks):
    rows, lanes = conv.shape
    span, chips = rows // blocks, blocks // 2
    shapes = [(span, lanes), (chips - 1, span, lanes), (chips, span, lanes)]
    return pl.pallas_call(
        spread_kernel,
        out_shape=[jax.ShapeDtypeStruct(shape, BF16) for shape in shapes],
        in_specs=[SMEM, VMEM],
        out_specs=[VMEM] * 3,
        compiler_params=GRANT,
        name="spread",
    )(me, conv)


def shifted_mix(stream, edge, weight):
    row = lax.broadcasted_iota(jnp.int32, stream.shape, 0)
    first = jnp.where(row == 0, edge[1:2], pltpu.roll(stream, 1, 0))
    second = pltpu.roll(stream, 2, 0)
    second = jnp.where(row == 0, edge[0:1], jnp.where(row == 1, edge[1:2], second))
    return weight[0:1] * stream + weight[1:2] * first + weight[2:3] * second


def rims_kernel(query, key, value, out, held, sems):
    span = query.shape[0]
    copies = [
        pltpu.make_async_copy(ref.at[pl.ds(span - 16, 16), :], held.at[s], sems.at[s])
        for s, ref in enumerate((query, key, value))
    ]
    for copy in copies:
        copy.start()
    for s, copy in enumerate(copies):
        copy.wait()
        out[2 * s : 2 * s + 2, :] = held[s, 14:16, :]


def rims(*streams):
    chans = streams[0].shape[1]
    return pl.pallas_call(
        rims_kernel,
        in_specs=[HBM] * 3,
        out_specs=VMEM,
        out_shape=jax.ShapeDtypeStruct((6, chans), BF16),
        scratch_shapes=[pltpu.VMEM((3, 16, chans), BF16), pltpu.SemaphoreType.DMA((3,))],
        compiler_params=grant(56),
        name="rims",
    )(*streams)


def gate_in_kernel(me_ref, key, value, edges, weight, stay, same, swap, held, sems):
    lanes = stay.shape[1]
    chips = swap.shape[0]
    mine = me_ref[0] % 2
    copies = []
    for q in range(chips):
        start = pl.multiple_of(((me_ref[0] // 2) ^ q) * 2 * lanes, 2 * lanes)
        for s, ref in enumerate((key, value)):
            source = ref.at[:, pl.ds(start, 2 * lanes)]
            copies.append(pltpu.make_async_copy(source, held.at[q, s], sems.at[q, s]))
            copies[-1].start()
    for q in range(chips):
        start = ((me_ref[0] // 2) ^ q) * 2 * lanes
        for copy in copies[2 * q : 2 * q + 2]:
            copy.wait()
        for side in range(2):
            inner = pl.ds(pl.multiple_of((mine ^ side) * lanes, lanes), lanes)
            outer = pl.ds(pl.multiple_of(start + (mine ^ side) * lanes, lanes), lanes)
            mixed = [
                shifted_mix(
                    held[q, s, :, inner].astype(F32),
                    edges[2 * s + 2 : 2 * s + 4, outer].astype(F32),
                    weight[:, s + 1, outer],
                )
                for s in range(2)
            ]
            gated = (mixed[0] * mixed[1]).astype(BF16)
            if side:
                swap[q] = gated
            elif q:
                same[q - 1] = gated
            else:
                stay[...] = gated


def gate_in(me, key_rows, value_rows, edges, short_weight, blocks):
    span, chans = key_rows.shape
    lanes = chans // blocks
    chips = blocks // 2
    shapes = [(span, lanes), (chips - 1, span, lanes), (chips, span, lanes)]
    return pl.pallas_call(
        gate_in_kernel,
        in_specs=[SMEM, HBM, HBM, VMEM, VMEM],
        out_specs=[VMEM] * 3,
        out_shape=[jax.ShapeDtypeStruct(shape, BF16) for shape in shapes],
        scratch_shapes=[
            pltpu.VMEM((chips, 2, span, 2 * lanes), BF16),
            pltpu.SemaphoreType.DMA((chips, 2)),
        ],
        compiler_params=grant(56),
        name="gate_in",
    )(me, key_rows, value_rows, edges, short_weight)


def split_taps_kernel(me_ref, taps, *refs):
    outs, sems = refs[:-1], refs[-1]
    rows = outs[0].shape[0]
    copies = []
    for q, out in enumerate(outs):
        window = pl.ds(pl.multiple_of(((me_ref[0] // 2) ^ q) * rows, rows), rows)
        copies.append(pltpu.make_async_copy(taps.at[window, :], out, sems.at[q]))
        copies[-1].start()
    for copy in copies:
        copy.wait()


def split_taps(me, filter_taps, chips):
    chans, span = filter_taps.shape
    return pl.pallas_call(
        split_taps_kernel,
        in_specs=[SMEM, HBM],
        out_specs=[VMEM] * chips,
        out_shape=[jax.ShapeDtypeStruct((chans // chips, span), BF16)] * chips,
        scratch_shapes=[pltpu.SemaphoreType.DMA((chips,))],
        compiler_params=GRANT,
        name="split_taps",
    )(me, filter_taps)


def other_core_kernel(me_ref, *refs):
    pairs, out = refs[:-1], refs[-1]
    rows = out.shape[1]
    for q, pair in enumerate(pairs):
        window = pl.ds(pl.multiple_of((1 - me_ref[0] % 2) * rows, rows), rows)
        out[q] = pair[window, :]


def other_core(me, pairs):
    rows, span = pairs[0].shape
    return pl.pallas_call(
        other_core_kernel,
        in_specs=[SMEM] + [VMEM] * len(pairs),
        out_specs=VMEM,
        out_shape=jax.ShapeDtypeStruct((len(pairs), rows // 2, span), BF16),
        compiler_params=GRANT,
        name="other_core",
    )(me, *pairs)


def pair_kernel(same, swapped, *outs):
    for q, out in enumerate(outs):
        out[0] = same[q]
        out[1] = swapped[q + 1]


def pair_up(same, swapped):
    count, span, lanes = same.shape
    return pl.pallas_call(
        pair_kernel,
        out_shape=[jax.ShapeDtypeStruct((2, span, lanes), BF16)] * count,
        in_specs=[VMEM] * 2,
        out_specs=[VMEM] * count,
        compiler_params=GRANT,
        name="pair_up",
    )(same, swapped)


def mix_query_kernel(query, edges, weight, out):
    out[...] = shifted_mix(query[...].astype(F32), edges[0:2].astype(F32), weight[:, 0, :])


def mix_query(query_rows, edges, short_weight):
    span, chans = query_rows.shape
    lanes = chans // 4
    return pl.pallas_call(
        mix_query_kernel,
        grid=(4,),
        in_specs=[
            pl.BlockSpec((span, lanes), lambda g: (0, g)),
            pl.BlockSpec((6, lanes), lambda g: (0, g)),
            pl.BlockSpec((3, 3, lanes), lambda g: (0, 0, g)),
        ],
        out_specs=pl.BlockSpec((span, lanes), lambda g: (0, g)),
        out_shape=jax.ShapeDtypeStruct((span, chans), F32),
        compiler_params=GRANT,
        name="mix_query",
    )(query_rows, edges, short_weight)


def after(values, others):
    return lax.optimization_barrier((values, others))[0]


HEAD, PASS, ADD = 0, 1, 2
SENT = np.array(
    [
        (HEAD, ADD, ADD, 2, 1),
        (ADD, PASS, ADD, 3, 2),
        (PASS, ADD, PASS, 3, 3),
        (PASS, PASS, PASS, 3, 3),
    ],
    np.int32,
)


def gate_out_kernel(blocks, spot, *refs):
    stay, swapped, *others = refs[: blocks // 2 + 1]
    mixed, far_weight, gated, sent = refs[blocks // 2 + 1 :]
    convs = [stay, swapped.at[0]] + [ref.at[core] for ref in others for core in range(2)]
    lanes = convs[0].shape[1]
    rows = gated.shape[1]
    for m in range(blocks):
        window = pl.ds(pl.multiple_of((spot[0] ^ m) * lanes, lanes), lanes)
        piece = (mixed[:, window] * convs[m][...].astype(F32)).astype(BF16)
        gated[0, :, window] = piece[:rows]
        gated[1, :, window] = piece[rows:]
    first_sent(spot, gated, far_weight, sent)


def first_sent(spot, gated, far_weight, sent):
    @pl.when(spot[1] == 0)
    def _():
        term = jnp.dot(gated[1], far_weight[...], preferred_element_type=F32)
        sent[...] = term.astype(BF16)

    @pl.when(spot[1] != 0)
    def _():
        sent[...] = gated[0]


def gate_out(spot, convs, mixed, far_weight):
    span, chans = mixed.shape
    return pl.pallas_call(
        partial(gate_out_kernel, 2 * len(convs) - 2),
        in_specs=[SMEM] + [VMEM] * (len(convs) + 2),
        out_specs=[VMEM] * 2,
        out_shape=[
            jax.ShapeDtypeStruct((2, span // 2, chans), BF16),
            jax.ShapeDtypeStruct((span // 2, chans), BF16),
        ],
        compiler_params=GRANT,
        name="gate_out",
    )(spot, *convs, mixed, far_weight)


def partner_sent(spot, gated, far_weight):
    return pl.pallas_call(
        first_sent,
        in_specs=[SMEM, VMEM, VMEM],
        out_specs=VMEM,
        out_shape=jax.ShapeDtypeStruct(gated.shape[1:], BF16),
        compiler_params=GRANT,
        cost_estimate=cost(1),
        name="partner_sent",
    )(spot, gated, far_weight)


def step_kernel(step, plan, head, term, got, out):
    mode = plan[step - 1]

    @pl.when(mode == HEAD)
    def _():
        out[...] = head[...]

    @pl.when(mode == PASS)
    def _():
        out[...] = got[...]

    @pl.when(mode == ADD)
    def _():
        out[...] = (term[...].astype(F32) + got[...].astype(F32)).astype(BF16)


def next_step(plan, step, chain, gated, terms, got):
    rows, chans = got.shape
    whole = pl.BlockSpec((rows, chans), lambda g, plan: (0, 0))
    return pl.pallas_call(
        partial(step_kernel, step),
        grid_spec=pltpu.PrefetchScalarGridSpec(
            num_scalar_prefetch=1,
            grid=(1,),
            in_specs=[
                pl.BlockSpec((None, rows, chans), lambda g, plan: (0, 0, 0)),
                pl.BlockSpec(
                    (None, None, rows, chans), lambda g, plan: (chain, step // 3, 0, 0)
                ),
                whole,
            ],
            out_specs=whole,
        ),
        out_shape=jax.ShapeDtypeStruct((rows, chans), BF16),
        compiler_params=GRANT,
        cost_estimate=cost(1),
        name="next_step",
    )(plan, gated, terms, got)


def terms_kernel(plan, mine, partners, weight, out, held, sems):
    count, chans = held.shape[:2]
    copies = []
    for k in range(count):
        columns = pl.ds(pl.multiple_of(plan[3 + k] * chans, chans), chans)
        copies.append(pltpu.make_async_copy(weight.at[:, columns], held.at[k], sems.at[k]))
        copies[-1].start()
    for k, copy in enumerate(copies):
        copy.wait()
        for chain, gated in enumerate((mine, partners)):
            term = jnp.dot(gated[1], held[k], preferred_element_type=F32)
            out[chain, k] = term.astype(BF16)


def sent_terms(plan, mine, partners, out_weight):
    _, rows, chans = mine.shape
    return pl.pallas_call(
        terms_kernel,
        in_specs=[SMEM, VMEM, VMEM, HBM],
        out_specs=VMEM,
        out_shape=jax.ShapeDtypeStruct((2, 2, rows, chans), BF16),
        scratch_shapes=[pltpu.VMEM((2, chans, chans), BF16), pltpu.SemaphoreType.DMA((2,))],
        compiler_params=GRANT,
        cost_estimate=cost(4),
        name="sent_terms",
    )(plan, mine, partners, out_weight)


def pick_weight(out_weight):
    stages, blocks = lax.axis_size("tp"), lax.axis_size("ctx")
    stage, place = lax.axis_index("tp"), lax.axis_index("ctx")
    chans = out_weight.shape[0]
    hops = jnp.where(place % 2 == 0, 1, stages - 1)
    corners = jnp.stack([place // 2, (stage + hops) % stages, place, (stage + 2) % stages])
    return weight_corners(corners.astype(jnp.int32), out_weight, blocks)


def turn_weight(parts):
    stages, blocks = lax.axis_size("tp"), lax.axis_size("ctx")
    found = []
    for part, static in zip(parts, ((1, stages - 1), (2, 2))):
        route = [
            (c * stages + k, c * stages + (k + static[c % 2]) % stages)
            for c in range(blocks)
            for k in range(stages)
        ]
        found.append(lax.ppermute(part, ("ctx", "tp"), route))
    return found


def corners_kernel(corners, weight, *refs):
    outs, sems = refs[:-1], refs[-1]
    copies = []
    for n, out in enumerate(outs):
        rows, chans = out.shape
        row = pl.multiple_of(corners[2 * n] * rows, rows)
        column = pl.multiple_of(corners[2 * n + 1] * chans, chans)
        source = weight.at[pl.ds(row, rows), pl.ds(column, chans)]
        copies.append(pltpu.make_async_copy(source, out, sems.at[n]))
        copies[-1].start()
    for copy in copies:
        copy.wait()


def weight_corners(corners, out_weight, blocks):
    chans = out_weight.shape[0]
    shapes = [(2 * chans // blocks, chans), (chans // blocks, chans)]
    return pl.pallas_call(
        corners_kernel,
        in_specs=[SMEM, HBM],
        out_specs=[VMEM] * 2,
        out_shape=[jax.ShapeDtypeStruct(shape, BF16) for shape in shapes],
        scratch_shapes=[pltpu.SemaphoreType.DMA((2,))],
        compiler_params=grant(56),
        name="weight_corners",
    )(corners, out_weight)


def swap_weight(part):
    devices = range(lax.axis_size("ctx"))
    return lax.ppermute(part, "ctx", [(i, i ^ (4 if i & 1 else 2)) for i in devices])


def gather_weight(two, ready):
    devices = range(lax.axis_size("ctx"))
    other = [(i, i ^ (2 if i & 1 else 4)) for i in devices]
    near = [*two, *[lax.ppermute(x, "ctx", other) for x in two]]
    apart = near[:2] + after(near[2:], ready)
    return near + [lax.ppermute(x, "ctx", [(i, i ^ 1) for i in devices]) for x in apart]


def add_parts(order, data, parts, hops):
    chans = data.shape[1]
    if hops == 2:
        rows, row, chosen = chans // 8, chans // 4, range(8)
    else:
        rows, row, chosen = chans // 4, 0, range(4) if hops == 1 else range(4, 8)
    picked = []
    for q in chosen:
        index = order[q] if hops == 2 else order[q] // 2
        picked.append(data[:, pl.ds(pl.multiple_of(index * rows, rows), rows)])
    block = jnp.concatenate([parts[q][row : row + rows, :] for q in chosen], axis=0)
    return jnp.dot(jnp.concatenate(picked, axis=1), block, preferred_element_type=F32)


def early_kernel(order, mine, got0, got1, partner0, partner1, weight, *refs):
    parts, (out, own, first, own_weight, sem) = refs[:8], refs[8:]
    turn_count = order[8]
    rows, chans = got0.shape
    columns = pl.ds(pl.multiple_of(order[9] * chans, chans), chans)
    copy = pltpu.make_async_copy(weight.at[:, columns], own_weight, sem)
    copy.start()

    @pl.when(turn_count >= 2)
    def _():
        first[:rows, :] = got0[...]
        first[rows:, :] = partner0[...]

    @pl.when(turn_count < 2)
    def _():
        first[:rows, :] = got1[...]
        first[rows:, :] = partner1[...]

    @pl.when(turn_count >= 1)
    def _():
        out[...] = add_parts(order, first, parts, 1)

    @pl.when(turn_count < 1)
    def _():
        out[...] = jnp.zeros_like(out)

    @pl.when(turn_count == 3)
    def _():
        first[:rows, :] = got1[...]
        first[rows:, :] = partner1[...]
        out[...] += add_parts(order, first, parts, 2)

    copy.wait()
    out[:rows, :] += jnp.dot(mine[0], own_weight[...], preferred_element_type=F32)
    own[...] = jnp.dot(mine[1], own_weight[...], preferred_element_type=F32)


def early_sum(order, mine, arrivals, out_weight, weights):
    _, rows, chans = mine.shape
    whole = lambda shape: pl.BlockSpec(shape, lambda g, order: (0,) * len(shape))
    return pl.pallas_call(
        early_kernel,
        grid_spec=pltpu.PrefetchScalarGridSpec(
            num_scalar_prefetch=1,
            grid=(1,),
            in_specs=[whole(mine.shape)]
            + [whole((rows, chans))] * 4
            + [HBM]
            + [whole(x.shape) for x in weights],
            out_specs=[whole((2 * rows, chans)), whole((rows, chans))],
            scratch_shapes=[
                pltpu.VMEM((2 * rows, chans), BF16),
                pltpu.VMEM((chans, chans), BF16),
                pltpu.SemaphoreType.DMA,
            ],
        ),
        out_shape=[
            jax.ShapeDtypeStruct((2 * rows, chans), F32),
            jax.ShapeDtypeStruct((rows, chans), F32),
        ],
        compiler_params=grant(24),
        cost_estimate=cost(1),
        name="early_sum",
    )(order, mine, *arrivals, out_weight, *weights)


def late_sum(order, early, got2, got3, weights, total):
    behind = order[8]

    @pl.when(behind < 2)
    def _():
        total[...] = early[...]

    @pl.when(behind == 2)
    def _():
        total[...] = early[...] + add_parts(order, got2, weights, 2)

    @pl.when(behind == 3)
    def _():
        total[...] = early[...] + add_parts(order, got3, weights, 3)

    summed = jnp.where(behind == 3, got2[...].astype(F32), got3[...].astype(F32))
    return jnp.where(behind == 0, 0.0, summed)


def partner_kernel(order, early, got2, got3, *refs):
    weights, (out, total) = refs[:8], refs[8:]
    out[1] = late_sum(order, early, got2, got3, weights, total).astype(BF16)
    out[0] = total[...].astype(BF16)


def partner_sum(order, early, arrivals, weights):
    rows, chans = arrivals[0].shape
    whole = lambda shape: pl.BlockSpec(shape, lambda g, order: (0,) * len(shape))
    return pl.pallas_call(
        partner_kernel,
        grid_spec=pltpu.PrefetchScalarGridSpec(
            num_scalar_prefetch=1,
            grid=(1,),
            in_specs=[pl.BlockSpec((rows, chans), lambda g, order: (1, 0))]
            + [whole((rows, chans))] * 2
            + [whole(x.shape) for x in weights],
            out_specs=whole((2, rows, chans)),
            scratch_shapes=[pltpu.VMEM((rows, chans), F32)],
        ),
        out_shape=jax.ShapeDtypeStruct((2, rows, chans), BF16),
        compiler_params=grant(24),
        cost_estimate=cost(2),
        name="partner_sum",
    )(order, early, *arrivals, *weights)


def mine_kernel(order, early, own, got2, got3, *refs):
    weights, (out, total) = refs[:8], refs[8:]
    rows = early.shape[0]
    out[rows:, :] = late_sum(order, early, got2, got3, weights, total) + own[...]
    out[:rows, :] = total[...]


def mine_sum(order, early, own, arrivals, weights):
    rows, chans = arrivals[0].shape
    whole = lambda shape: pl.BlockSpec(shape, lambda g, order: (0,) * len(shape))
    return pl.pallas_call(
        mine_kernel,
        grid_spec=pltpu.PrefetchScalarGridSpec(
            num_scalar_prefetch=1,
            grid=(1,),
            in_specs=[pl.BlockSpec((rows, chans), lambda g, order: (0, 0))]
            + [whole((rows, chans))] * 3
            + [whole(x.shape) for x in weights],
            out_specs=whole((2 * rows, chans)),
            scratch_shapes=[pltpu.VMEM((rows, chans), F32)],
        ),
        out_shape=jax.ShapeDtypeStruct((2 * rows, chans), F32),
        compiler_params=grant(24),
        cost_estimate=cost(3),
        name="mine_sum",
    )(order, early, own, *arrivals, *weights)


def join_kernel(mine, partners, out):
    rows = partners.shape[1]
    for half in range(2):
        part = slice(half * rows, (half + 1) * rows)
        out[part, :] = (mine[part, :] + partners[half].astype(F32)).astype(BF16)


def join_sums(mine, partners):
    return pl.pallas_call(
        join_kernel,
        in_specs=[VMEM] * 2,
        out_specs=VMEM,
        out_shape=jax.ShapeDtypeStruct(mine.shape, BF16),
        compiler_params=GRANT,
        name="join_sums",
    )(mine, partners)


def weight_order():
    place, stage = lax.axis_index("ctx"), lax.axis_index("tp")
    up = place % 2 == 0
    last = lax.axis_size("tp") - 1
    a = jnp.where(up, 2, 4)
    masks = [0 * a, a, 6 - a, 0 * a + 6]
    swapped = [0 * a + 1, (6 - a) ^ 1, a ^ 1, 0 * a + 7]
    parts = [place ^ mask for mask in masks + swapped]
    return jnp.stack(parts + [jnp.where(up, stage, last - stage), stage]).astype(jnp.int32)


def project(spot, plan, order, convs, mixed, out_weight, weight_parts):
    stages, blocks = lax.axis_size("tp"), lax.axis_size("ctx")
    chans = out_weight.shape[0]
    far_weight = lax.dynamic_slice(out_weight, (0, spot[2] * chans), (chans, chans))
    mine, sent = gate_out(spot, convs, mixed, far_weight)
    route = []
    for c in range(blocks):
        for k in range(stages):
            to = k + (1 if c % 2 == 0 else -1)
            if 0 <= to < stages:
                route.append((c * stages + k, c * stages + to))
    onward = lambda x: lax.ppermute(x, ("ctx", "tp"), route)
    core_swap = lambda x: lax.ppermute(x, "ctx", [(i, i ^ 1) for i in range(blocks)])
    partners = core_swap(mine)
    partner_first = partner_sent(spot, partners, far_weight)
    got = [[onward(sent), onward(partner_first)]]
    terms = sent_terms(plan, mine, partners, out_weight)
    weight_part = after(jnp.concatenate(weight_parts), partner_first)
    weight_two = [weight_part, swap_weight(weight_part)]
    steps = []
    for step in range(1, stages):
        row = []
        for chain, gated in enumerate((mine, partners)):
            row.append(next_step(plan, step, chain, gated, terms, got[-1][chain]))
        steps.append(row)
        got.append([onward(x) for x in row])

    weights = gather_weight(weight_two, steps[2][0])
    arrivals = [got[0][0], got[1][0], got[0][1], got[1][1]]
    early, own = early_sum(order, mine, arrivals, out_weight, weights)
    theirs = partner_sum(after(order, got[3][0]), early, [got[2][1], got[3][1]], weights)
    ours = mine_sum(order, early, own, [got[2][0], got[3][0]], weights)
    return join_sums(ours, core_swap(theirs))


def fast_per_device(
    query_rows, key_rows, value_rows, short_weight, skip_gain, filter_taps, out_weight
):
    span, chans = query_rows.shape
    blocks, stages = lax.axis_size("ctx"), lax.axis_size("tp")
    lanes = chans // blocks
    length = span * blocks
    radix = 2 * length // SUB
    place, stage = lax.axis_index("ctx"), lax.axis_index("tp")
    me = place.astype(jnp.int32).reshape(1)
    up = place % 2 == 0
    behind = jnp.where(up, stage, stages - 1 - stage)
    far = jnp.where(up, stages - 1, 0)
    spot = jnp.stack([place, behind, far]).astype(jnp.int32)
    plan = lax.dynamic_index_in_dim(jnp.asarray(SENT), behind, keepdims=False)
    plan = jnp.where(up | (jnp.arange(5) < 3), plan, stages - 1 - plan)
    me, spot, plan, order = lax.optimization_barrier((me, spot, plan, weight_order()))
    skip = lax.dynamic_slice(skip_gain, (place * lanes,), (lanes,)).reshape(1, lanes)
    forward, inverse = (jnp.asarray(t) for t in dft_tables(2 * length))
    twiddle = jnp.asarray(twiddle_table(radix))
    devices = range(blocks)
    core_swap = lambda x: lax.ppermute(x, "ctx", [(i, i ^ 1) for i in devices])
    to_chips = lambda xs: [
        lax.ppermute(x, "ctx", [(i, i ^ (2 * q + 2)) for i in devices])
        for q, x in enumerate(xs)
    ]
    edges = passed_along(rims(query_rows, key_rows, value_rows), "ctx", 1)
    pairs = split_taps(after(me, edges), filter_taps, blocks // 2)
    pairs = [pairs[0]] + to_chips(pairs[1:])
    weight_parts = pick_weight(out_weight)
    stay, same, swap = gate_in(after(me, weight_parts), key_rows, value_rows, edges, short_weight, blocks)
    swapped = core_swap(swap)
    packed = pair_up(same, swapped)
    others = to_chips(packed)
    taps_swapped = core_swap(other_core(me, pairs))
    mixed = mix_query(query_rows, edges, short_weight)
    spectra = taps_spectra_of(me, pairs, taps_swapped, twiddle, forward)
    weight_parts = turn_weight(after(weight_parts, taps_swapped))
    conv = long_conv(me, stay, swapped, others, spectra, twiddle, forward, inverse, skip)
    stay, same, swap = spread(after(me, weight_parts), conv, blocks)
    swapped = core_swap(swap)
    convs = [stay, swapped] + to_chips(pair_up(same, swapped))
    return project(spot, plan, order, convs, mixed, out_weight, weight_parts)


def per_device(*arrays):
    span, chans = arrays[0].shape
    blocks = lax.axis_size("ctx")
    suits = blocks == 8 and lax.axis_size("tp") == 4 and span == 512 and chans == 8 * SUB
    return (fast_per_device if suits else general_per_device)(*arrays)


def solution(mesh):
    placed = (
        P("ctx", "tp"),
        P("ctx", "tp"),
        P("ctx", "tp"),
        P(None, None, "tp"),
        P("tp"),
        P("tp", "ctx"),
        P("tp", None),
    )
    return jax.shard_map(
        per_device, mesh=mesh, in_specs=placed, out_specs=P("ctx", "tp"), check_vma=False
    )
```

```python
from functools import partial
import math

import jax
import jax.numpy as jnp
import numpy as np
from jax import lax
from jax.experimental import pallas as pl
from jax.experimental.pallas import tpu as pltpu
from jax.sharding import PartitionSpec as P

TRIPLE = lax.Precision.HIGH


def passed_along(block, axis, distance):
    devices = range(lax.axis_size(axis))
    route = [(i - distance, i) for i in devices if i - distance in devices]
    return lax.ppermute(block, axis, route)


def angle_table(left, right, offset, period):
    rows = lax.broadcasted_iota(jnp.int32, (left, right), 0)
    cols = lax.broadcasted_iota(jnp.int32, (left, right), 1) + offset
    turns = rows * cols % period
    return turns.astype(jnp.float32) * (2.0 * math.pi / period)


def inner_spectrum(rows, table_high, table_low):
    upper = jnp.dot(rows, table_high, preferred_element_type=jnp.float32)
    lower = jnp.dot(rows, table_low, preferred_element_type=jnp.float32)
    return upper + lower


def block_mix(real_component, imaginary_component, cosine_lookup, sine_lookup, sign):
    multiplier = partial(jnp.einsum, precision=TRIPLE, preferred_element_type=jnp.float32)
    cosine_real = multiplier("id,rdy->riy", cosine_lookup, real_component)
    cosine_imaginary = multiplier("id,rdy->riy", cosine_lookup, imaginary_component)
    sine_real = multiplier("id,rdy->riy", sine_lookup, real_component)
    sine_imaginary = multiplier("id,rdy->riy", sine_lookup, imaginary_component)
    return (cosine_real + sign * sine_imaginary, cosine_imaginary - sign * sine_real)


def general_per_device(query_rows, key_rows, value_rows, short_weight, skip_gain, filter_taps, out_weight):
    span = query_rows.shape[0]
    chans = query_rows.shape[1]
    blocks = lax.axis_size("ctx")
    group = chans // blocks
    period = 2 * span
    padded = 2 * blocks
    forward = angle_table(span, period, 0, period)
    forward = jnp.concatenate([jnp.cos(forward), -jnp.sin(forward)], axis=1)
    table_high = forward.astype(jnp.bfloat16)
    table_low = (forward - table_high.astype(jnp.float32)).astype(jnp.bfloat16)
    parity = 1.0 - 2.0 * (jnp.arange(period) % 2).astype(jnp.float32)
    parity = jnp.concatenate([parity, parity])
    stacked = jnp.stack([query_rows, key_rows, value_rows])
    rims = passed_along(stacked[:, -2:, :], "ctx", 1)
    extended = jnp.concatenate([rims, stacked], axis=1).astype(jnp.float32)
    mixed = (
        short_weight[0][:, None, :] * extended[:, 2:]
        + short_weight[1][:, None, :] * extended[:, 1:-1]
        + short_weight[2][:, None, :] * extended[:, :span]
    )
    gated_in = (mixed[1] * mixed[2]).astype(jnp.bfloat16)
    gated_t = gated_in.T
    inputs_local, taps_local = (
        lax.all_to_all(gated_t, "ctx", split_axis=0, concat_axis=1, tiled=True),
        lax.all_to_all(filter_taps, "ctx", split_axis=0, concat_axis=1, tiled=True),
    )
    spectra = inner_spectrum(
        taps_local.reshape(group * blocks, span), table_high, table_low
    ).reshape(group, blocks, 2 * period)
    earlier = jnp.concatenate(
        [jnp.zeros((group, 1, 2 * period), jnp.float32), spectra[:, :-1]], axis=1
    )
    kernel_spec = earlier + parity * spectra
    input_spec = inner_spectrum(
        inputs_local.reshape(group * blocks, span), table_high, table_low
    ).reshape(group, blocks, 2 * period)
    block_angle = angle_table(padded, blocks, 0, padded)
    cos_fwd = jnp.cos(block_angle)
    sin_fwd = jnp.sin(block_angle)
    input_re, input_im = block_mix(
        input_spec[..., :period], input_spec[..., period:], cos_fwd, sin_fwd, 1.0
    )
    kernel_re, kernel_im = block_mix(
        kernel_spec[..., :period], kernel_spec[..., period:], cos_fwd, sin_fwd, 1.0
    )
    product_re = input_re * kernel_re - input_im * kernel_im
    product_im = input_re * kernel_im + input_im * kernel_re
    back_angle = angle_table(blocks, padded, 0, padded)
    out_re, out_im = block_mix(
        product_re, product_im, jnp.cos(back_angle), jnp.sin(back_angle), -1.0
    )
    inverse = angle_table(period, span, span, period)
    inverse = jnp.concatenate([jnp.cos(inverse), -jnp.sin(inverse)], axis=0) * (
        1.0 / (period * padded)
    )
    joined = jnp.concatenate([out_re, out_im], axis=2).reshape(group * blocks, 2 * period)
    long_local = jnp.dot(
        joined, inverse, precision=TRIPLE, preferred_element_type=jnp.float32
    ).reshape(group, blocks * span)
    long_t = lax.all_to_all(
        long_local.astype(jnp.bfloat16), "ctx", split_axis=1, concat_axis=0, tiled=True
    ).astype(long_local.dtype)
    conv_t = (long_t + skip_gain[:, None] * gated_t.astype(jnp.float32)).astype(jnp.bfloat16)
    gated_out = (mixed[0].T * conv_t.astype(jnp.float32)).astype(jnp.bfloat16)
    term = lax.dot_general(
        gated_out, out_weight, (((0,), (0,)), ((), ())), preferred_element_type=jnp.float32
    )
    return lax.psum_scatter(term.astype(jnp.bfloat16), "tp", scatter_dimension=1, tiled=True)


SUB = 128
F32 = jnp.float32
BF16 = jnp.bfloat16


def split_table(matrix):
    high = matrix.astype(jnp.bfloat16)
    low = (matrix - high.astype(np.float32)).astype(jnp.bfloat16)
    return np.concatenate([high, high, low], axis=1)


def dft_tables(period):
    index = np.arange(SUB)
    turns = np.outer(index, index) % SUB * (2.0 * np.pi / SUB)
    cos, sin = np.cos(turns), np.sin(turns)
    forward = np.block([[cos, sin], [-sin, cos]]).astype(np.float32)
    inverse = (np.block([[cos, -sin], [sin, cos]]) / period).astype(np.float32)
    return split_table(forward), split_table(inverse)


def twiddle_table(radix):
    half = radix // 2
    turns = np.outer(np.arange(SUB), np.arange(half + 1)) * (2.0 * np.pi / (radix * SUB))
    return np.concatenate([np.cos(turns), -np.sin(turns)], axis=1).astype(np.float32)


def times(value, factor):
    return None if value is None else value * factor


def plus(left, right):
    if left is None:
        return right
    return left if right is None else left + right


def minus(left, right):
    if right is None:
        return left
    return -right if left is None else left - right


def rotate(value, turn):
    real, imag = value
    cos, sin = math.cos(2 * math.pi * turn), math.sin(2 * math.pi * turn)
    if abs(cos - sin) < 1e-12 and imag is not None:
        return (real + imag) * cos, (imag - real) * cos
    return plus(times(real, cos), times(imag, sin)), minus(times(imag, cos), times(real, sin))


def real_forward(values):
    points = 2 * len(values)
    if points == 2:
        return [(values[0], None), (values[0], None)]
    even, odd = real_forward(values[0::2]), real_forward(values[1::2])
    bins = [None] * (points // 2 + 1)
    bins[0] = (even[0][0] + odd[0][0], None)
    bins[points // 2] = (even[0][0] - odd[0][0], None)
    quarter = points // 4
    for k in range(1, quarter):
        turned = rotate(odd[k], k / points)
        bins[k] = (even[k][0] + turned[0], even[k][1] + turned[1])
        bins[points // 2 - k] = (even[k][0] - turned[0], turned[1] - even[k][1])
    bins[quarter] = (even[quarter][0], -odd[quarter][0])
    return bins


def real_inverse(bins):
    half = len(bins) - 1
    points = 2 * half
    if points == 2:
        return [bins[0][0] + bins[1][0]]
    even, odd = [], []
    for k in range(half // 2 + 1):
        ahead, back = bins[k], bins[half - k]
        if k == 0:
            even.append((ahead[0] + back[0], None))
            odd.append((ahead[0] - back[0], None))
        elif k == half // 2:
            even.append((ahead[0] * 2.0, None))
            odd.append((ahead[1] * -2.0, None))
        else:
            even.append((ahead[0] + back[0], ahead[1] - back[1]))
            difference = (ahead[0] - back[0], ahead[1] + back[1])
            odd.append(rotate(difference, -k / points))
    even, odd = real_inverse(even), real_inverse(odd)
    return [value for pair in zip(even, odd) for value in pair]


def split_dot(table, data):
    high = data.astype(BF16)
    low = (data - high.astype(F32)).astype(BF16)
    return jnp.dot(
        table[...], jnp.concatenate([high, low, high], axis=0), preferred_element_type=F32
    )


def over_pairs(count, pair):
    whole = count // 4 * 4
    lax.fori_loop(0, whole, pair, 0, unroll=4)
    for p in range(whole, count):
        pair(p, 0)


def first_stage(series, spectra, twiddle):
    half = series.shape[0] // SUB
    lanes = series.shape[1]

    def slab(step, carry):
        row = pl.multiple_of(step * 8, 8)
        values = [series[pl.ds(SUB * n + row, 8), :] for n in range(half)]
        factors = twiddle[pl.ds(row, 8), :]
        for k, (real, imag) in enumerate(real_forward(values)):
            if k == 0:
                spectra[0, pl.ds(row, 8), :] = real
                spectra[0, pl.ds(SUB + row, 8), :] = jnp.zeros_like(real)
                continue
            cos = jnp.broadcast_to(factors[:, k : k + 1], (8, lanes))
            sin = jnp.broadcast_to(factors[:, half + 1 + k : half + 2 + k], (8, lanes))
            if imag is None:
                spectra[k, pl.ds(row, 8), :] = real * cos
                spectra[k, pl.ds(SUB + row, 8), :] = real * sin
            else:
                spectra[k, pl.ds(row, 8), :] = real * cos - imag * sin
                spectra[k, pl.ds(SUB + row, 8), :] = real * sin + imag * cos
        return carry

    lax.fori_loop(0, SUB // 8, slab, 0, unroll=2)
    for k in range(half + 1, spectra.shape[0]):
        spectra[k] = jnp.zeros(spectra.shape[1:], F32)


def last_stage(spectra, series, twiddle, signal, skip):
    half = series.shape[0] // SUB
    lanes = series.shape[1]

    def slab(step, carry):
        row = pl.multiple_of(step * 8, 8)
        factors = twiddle[pl.ds(row, 8), :]
        bins = []
        for k in range(half + 1):
            real = spectra[k, pl.ds(row, 8), :]
            if k == 0:
                bins.append((real, None))
                continue
            imag = spectra[k, pl.ds(SUB + row, 8), :]
            cos = jnp.broadcast_to(factors[:, k : k + 1], (8, lanes))
            sin = jnp.broadcast_to(factors[:, half + 1 + k : half + 2 + k], (8, lanes))
            turned = real * cos + imag * sin
            bins.append((turned, None if k == half else imag * cos - real * sin))
        gain = jnp.broadcast_to(skip[...], (8, lanes))
        for n, value in enumerate(real_inverse(bins)):
            rows = pl.ds(SUB * n + row, 8)
            series[rows, :] = value + gain * signal[rows, :]
        return carry

    lax.fori_loop(0, SUB // 8, slab, 0, unroll=2)


def taps_kernel(chips, me_ref, *refs):
    pairs, (swapped, twiddle, forward, spectra_out, series, spectra) = refs[:chips], refs[chips:]
    _, lanes, span = swapped.shape
    mine = pl.ds(pl.multiple_of(me_ref[0] % 2 * lanes, lanes), lanes)
    for q in range(chips):
        for m, piece in ((2 * q, pairs[q][mine, :]), (2 * q + 1, swapped[q])):
            start = pl.multiple_of((me_ref[0] ^ m) * span, span)
            series[pl.ds(start, span), :] = piece.astype(F32).T
    first_stage(series, spectra, twiddle)

    def pair(p, carry):
        data = jnp.concatenate([spectra[2 * p], spectra[2 * p + 1]], axis=1)
        spectra_out[p] = split_dot(forward, data)
        return carry

    over_pairs(spectra_out.shape[0], pair)


def conv_kernel(blocks, me_ref, stay, swapped, *refs):
    others = refs[: blocks // 2 - 1]
    taps_spectra, twiddle, forward, inverse, skip = refs[blocks // 2 - 1 : blocks // 2 + 4]
    out, series, spectra = refs[blocks // 2 + 4 :]
    span, lanes = stay.shape
    pieces = [stay, swapped.at[0]] + [ref.at[core] for ref in others for core in range(2)]
    for m in range(blocks):
        start = pl.multiple_of((me_ref[0] ^ m) * span, span)
        series[pl.ds(start, span), :] = pieces[m][...].astype(F32)
    first_stage(series, spectra, twiddle)

    def pair(p, carry):
        data = jnp.concatenate([spectra[2 * p], spectra[2 * p + 1]], axis=1)
        signal = split_dot(forward, data)
        signal_re, signal_im = signal[:SUB], signal[SUB:]
        taps_re, taps_im = taps_spectra[p, :SUB, :], taps_spectra[p, SUB:, :]
        product = jnp.concatenate(
            [
                signal_re * taps_re - signal_im * taps_im,
                signal_re * taps_im + signal_im * taps_re,
            ],
            axis=0,
        )
        back = split_dot(inverse, product)
        spectra[2 * p] = back[:, :lanes]
        spectra[2 * p + 1] = back[:, lanes:]
        return carry

    over_pairs(taps_spectra.shape[0], pair)
    last_stage(spectra, out, twiddle, series, skip)


def spread_kernel(me_ref, conv, stay, same, swap):
    chips, span, _ = swap.shape
    for m in range(2 * chips):
        start = pl.multiple_of((me_ref[0] ^ m) * span, span)
        piece = conv[pl.ds(start, span), :].astype(BF16)
        if m % 2:
            swap[m // 2] = piece
        elif m:
            same[m // 2 - 1] = piece
        else:
            stay[...] = piece


VMEM = pl.BlockSpec(memory_space=pltpu.VMEM)
SMEM = pl.BlockSpec(memory_space=pltpu.SMEM)
HBM = pl.BlockSpec(memory_space=pltpu.HBM)


def grant(mebibytes):
    return pltpu.CompilerParams(vmem_limit_bytes=mebibytes * 2**20)


def cost(microseconds):
    return pl.CostEstimate(flops=microseconds * 10**9, bytes_accessed=0, transcendentals=0)


GRANT = grant(16)


def taps_spectra_of(me, pairs, swapped, twiddle, forward):
    chips, lanes, span = swapped.shape
    length = 2 * chips * span
    count = (length // SUB + 2) // 2
    return pl.pallas_call(
        partial(taps_kernel, chips),
        out_shape=jax.ShapeDtypeStruct((count, 2 * SUB, 2 * lanes), F32),
        in_specs=[SMEM] + [VMEM] * (chips + 3),
        out_specs=VMEM,
        scratch_shapes=[
            pltpu.VMEM((length, lanes), F32),
            pltpu.VMEM((2 * count, 2 * SUB, lanes), F32),
        ],
        compiler_params=GRANT,
        cost_estimate=cost(8),
        name="taps_spectra",
    )(me, *pairs, swapped, twiddle, forward)


def long_conv(me, stay, swapped, others, taps_spectra, twiddle, forward, inverse, skip):
    span, lanes = stay.shape
    blocks = 2 * len(others) + 2
    pairs = taps_spectra.shape[0]
    return pl.pallas_call(
        partial(conv_kernel, blocks),
        out_shape=jax.ShapeDtypeStruct((blocks * span, lanes), F32),
        in_specs=[SMEM] + [VMEM] * (len(others) + 7),
        out_specs=VMEM,
        scratch_shapes=[
            pltpu.VMEM((blocks * span, lanes), F32),
            pltpu.VMEM((2 * pairs, 2 * SUB, lanes), F32),
        ],
        compiler_params=grant(20),
        cost_estimate=cost(20),
        name="long_conv",
    )(me, stay, swapped, *others, taps_spectra, twiddle, forward, inverse, skip)


def spread(me, conv, blocks):
    rows, lanes = conv.shape
    span, chips = rows // blocks, blocks // 2
    shapes = [(span, lanes), (chips - 1, span, lanes), (chips, span, lanes)]
    return pl.pallas_call(
        spread_kernel,
        out_shape=[jax.ShapeDtypeStruct(shape, BF16) for shape in shapes],
        in_specs=[SMEM, VMEM],
        out_specs=[VMEM] * 3,
        compiler_params=GRANT,
        name="spread",
    )(me, conv)


def shifted_mix(stream, edge, weight):
    row = lax.broadcasted_iota(jnp.int32, stream.shape, 0)
    first = jnp.where(row == 0, edge[1:2], pltpu.roll(stream, 1, 0))
    second = pltpu.roll(stream, 2, 0)
    second = jnp.where(row == 0, edge[0:1], jnp.where(row == 1, edge[1:2], second))
    return weight[0:1] * stream + weight[1:2] * first + weight[2:3] * second


def rims_kernel(query, key, value, out, held, sems):
    span = query.shape[0]
    copies = [
        pltpu.make_async_copy(ref.at[pl.ds(span - 16, 16), :], held.at[s], sems.at[s])
        for s, ref in enumerate((query, key, value))
    ]
    for copy in copies:
        copy.start()
    for s, copy in enumerate(copies):
        copy.wait()
        out[2 * s : 2 * s + 2, :] = held[s, 14:16, :]


def rims(*streams):
    chans = streams[0].shape[1]
    return pl.pallas_call(
        rims_kernel,
        in_specs=[HBM] * 3,
        out_specs=VMEM,
        out_shape=jax.ShapeDtypeStruct((6, chans), BF16),
        scratch_shapes=[pltpu.VMEM((3, 16, chans), BF16), pltpu.SemaphoreType.DMA((3,))],
        compiler_params=grant(56),
        name="rims",
    )(*streams)


def gate_in_kernel(me_ref, key, value, edges, weight, stay, same, swap, held, sems):
    lanes = stay.shape[1]
    chips = swap.shape[0]
    mine = me_ref[0] % 2
    copies = []
    for q in range(chips):
        start = pl.multiple_of(((me_ref[0] // 2) ^ q) * 2 * lanes, 2 * lanes)
        for s, ref in enumerate((key, value)):
            source = ref.at[:, pl.ds(start, 2 * lanes)]
            copies.append(pltpu.make_async_copy(source, held.at[q, s], sems.at[q, s]))
            copies[-1].start()
    for q in range(chips):
        start = ((me_ref[0] // 2) ^ q) * 2 * lanes
        for copy in copies[2 * q : 2 * q + 2]:
            copy.wait()
        for side in range(2):
            inner = pl.ds(pl.multiple_of((mine ^ side) * lanes, lanes), lanes)
            outer = pl.ds(pl.multiple_of(start + (mine ^ side) * lanes, lanes), lanes)
            mixed = [
                shifted_mix(
                    held[q, s, :, inner].astype(F32),
                    edges[2 * s + 2 : 2 * s + 4, outer].astype(F32),
                    weight[:, s + 1, outer],
                )
                for s in range(2)
            ]
            gated = (mixed[0] * mixed[1]).astype(BF16)
            if side:
                swap[q] = gated
            elif q:
                same[q - 1] = gated
            else:
                stay[...] = gated


def gate_in(me, key_rows, value_rows, edges, short_weight, blocks):
    span, chans = key_rows.shape
    lanes = chans // blocks
    chips = blocks // 2
    shapes = [(span, lanes), (chips - 1, span, lanes), (chips, span, lanes)]
    return pl.pallas_call(
        gate_in_kernel,
        in_specs=[SMEM, HBM, HBM, VMEM, VMEM],
        out_specs=[VMEM] * 3,
        out_shape=[jax.ShapeDtypeStruct(shape, BF16) for shape in shapes],
        scratch_shapes=[
            pltpu.VMEM((chips, 2, span, 2 * lanes), BF16),
            pltpu.SemaphoreType.DMA((chips, 2)),
        ],
        compiler_params=grant(56),
        name="gate_in",
    )(me, key_rows, value_rows, edges, short_weight)


def split_taps_kernel(me_ref, taps, *refs):
    outs, sems = refs[:-1], refs[-1]
    rows = outs[0].shape[0]
    copies = []
    for q, out in enumerate(outs):
        window = pl.ds(pl.multiple_of(((me_ref[0] // 2) ^ q) * rows, rows), rows)
        copies.append(pltpu.make_async_copy(taps.at[window, :], out, sems.at[q]))
        copies[-1].start()
    for copy in copies:
        copy.wait()


def split_taps(me, filter_taps, chips):
    chans, span = filter_taps.shape
    return pl.pallas_call(
        split_taps_kernel,
        in_specs=[SMEM, HBM],
        out_specs=[VMEM] * chips,
        out_shape=[jax.ShapeDtypeStruct((chans // chips, span), BF16)] * chips,
        scratch_shapes=[pltpu.SemaphoreType.DMA((chips,))],
        compiler_params=GRANT,
        name="split_taps",
    )(me, filter_taps)


def other_core_kernel(me_ref, *refs):
    pairs, out = refs[:-1], refs[-1]
    rows = out.shape[1]
    for q, pair in enumerate(pairs):
        window = pl.ds(pl.multiple_of((1 - me_ref[0] % 2) * rows, rows), rows)
        out[q] = pair[window, :]


def other_core(me, pairs):
    rows, span = pairs[0].shape
    return pl.pallas_call(
        other_core_kernel,
        in_specs=[SMEM] + [VMEM] * len(pairs),
        out_specs=VMEM,
        out_shape=jax.ShapeDtypeStruct((len(pairs), rows // 2, span), BF16),
        compiler_params=GRANT,
        name="other_core",
    )(me, *pairs)


def pair_kernel(same, swapped, *outs):
    for q, out in enumerate(outs):
        out[0] = same[q]
        out[1] = swapped[q + 1]


def pair_up(same, swapped):
    count, span, lanes = same.shape
    return pl.pallas_call(
        pair_kernel,
        out_shape=[jax.ShapeDtypeStruct((2, span, lanes), BF16)] * count,
        in_specs=[VMEM] * 2,
        out_specs=[VMEM] * count,
        compiler_params=GRANT,
        name="pair_up",
    )(same, swapped)


def mix_query_kernel(query, edges, weight, out):
    out[...] = shifted_mix(query[...].astype(F32), edges[0:2].astype(F32), weight[:, 0, :])


def mix_query(query_rows, edges, short_weight):
    span, chans = query_rows.shape
    lanes = chans // 4
    return pl.pallas_call(
        mix_query_kernel,
        grid=(4,),
        in_specs=[
            pl.BlockSpec((span, lanes), lambda g: (0, g)),
            pl.BlockSpec((6, lanes), lambda g: (0, g)),
            pl.BlockSpec((3, 3, lanes), lambda g: (0, 0, g)),
        ],
        out_specs=pl.BlockSpec((span, lanes), lambda g: (0, g)),
        out_shape=jax.ShapeDtypeStruct((span, chans), F32),
        compiler_params=GRANT,
        name="mix_query",
    )(query_rows, edges, short_weight)


def after(values, others):
    return lax.optimization_barrier((values, others))[0]


HEAD, PASS, ADD = 0, 1, 2
SENT = np.array(
    [
        (HEAD, ADD, ADD, 2, 1),
        (ADD, PASS, ADD, 3, 2),
        (PASS, ADD, PASS, 3, 3),
        (PASS, PASS, PASS, 3, 3),
    ],
    np.int32,
)


def gate_out_kernel(blocks, spot, *refs):
    stay, swapped, *others = refs[: blocks // 2 + 1]
    mixed, far_weight, gated, sent = refs[blocks // 2 + 1 :]
    convs = [stay, swapped.at[0]] + [ref.at[core] for ref in others for core in range(2)]
    lanes = convs[0].shape[1]
    rows = gated.shape[1]
    for m in range(blocks):
        window = pl.ds(pl.multiple_of((spot[0] ^ m) * lanes, lanes), lanes)
        piece = (mixed[:, window] * convs[m][...].astype(F32)).astype(BF16)
        gated[0, :, window] = piece[:rows]
        gated[1, :, window] = piece[rows:]
    first_sent(spot, gated, far_weight, sent)


def first_sent(spot, gated, far_weight, sent):
    @pl.when(spot[1] == 0)
    def _():
        term = jnp.dot(gated[1], far_weight[...], preferred_element_type=F32)
        sent[...] = term.astype(BF16)

    @pl.when(spot[1] != 0)
    def _():
        sent[...] = gated[0]


def gate_out(spot, convs, mixed, far_weight):
    span, chans = mixed.shape
    return pl.pallas_call(
        partial(gate_out_kernel, 2 * len(convs) - 2),
        in_specs=[SMEM] + [VMEM] * (len(convs) + 2),
        out_specs=[VMEM] * 2,
        out_shape=[
            jax.ShapeDtypeStruct((2, span // 2, chans), BF16),
            jax.ShapeDtypeStruct((span // 2, chans), BF16),
        ],
        compiler_params=GRANT,
        name="gate_out",
    )(spot, *convs, mixed, far_weight)


def partner_sent(spot, gated, far_weight):
    return pl.pallas_call(
        first_sent,
        in_specs=[SMEM, VMEM, VMEM],
        out_specs=VMEM,
        out_shape=jax.ShapeDtypeStruct(gated.shape[1:], BF16),
        compiler_params=GRANT,
        cost_estimate=cost(1),
        name="partner_sent",
    )(spot, gated, far_weight)


def step_kernel(step, plan, head, term, got, out):
    mode = plan[step - 1]

    @pl.when(mode == HEAD)
    def _():
        out[...] = head[...]

    @pl.when(mode == PASS)
    def _():
        out[...] = got[...]

    @pl.when(mode == ADD)
    def _():
        out[...] = (term[...].astype(F32) + got[...].astype(F32)).astype(BF16)


def next_step(plan, step, chain, gated, terms, got):
    rows, chans = got.shape
    whole = pl.BlockSpec((rows, chans), lambda g, plan: (0, 0))
    return pl.pallas_call(
        partial(step_kernel, step),
        grid_spec=pltpu.PrefetchScalarGridSpec(
            num_scalar_prefetch=1,
            grid=(1,),
            in_specs=[
                pl.BlockSpec((None, rows, chans), lambda g, plan: (0, 0, 0)),
                pl.BlockSpec(
                    (None, None, rows, chans), lambda g, plan: (chain, step // 3, 0, 0)
                ),
                whole,
            ],
            out_specs=whole,
        ),
        out_shape=jax.ShapeDtypeStruct((rows, chans), BF16),
        compiler_params=GRANT,
        cost_estimate=cost(1),
        name="next_step",
    )(plan, gated, terms, got)


def terms_kernel(plan, mine, partners, weight, out, held, sems):
    count, chans = held.shape[:2]
    copies = []
    for k in range(count):
        columns = pl.ds(pl.multiple_of(plan[3 + k] * chans, chans), chans)
        copies.append(pltpu.make_async_copy(weight.at[:, columns], held.at[k], sems.at[k]))
        copies[-1].start()
    for k, copy in enumerate(copies):
        copy.wait()
        for chain, gated in enumerate((mine, partners)):
            term = jnp.dot(gated[1], held[k], preferred_element_type=F32)
            out[chain, k] = term.astype(BF16)


def sent_terms(plan, mine, partners, out_weight):
    _, rows, chans = mine.shape
    return pl.pallas_call(
        terms_kernel,
        in_specs=[SMEM, VMEM, VMEM, HBM],
        out_specs=VMEM,
        out_shape=jax.ShapeDtypeStruct((2, 2, rows, chans), BF16),
        scratch_shapes=[pltpu.VMEM((2, chans, chans), BF16), pltpu.SemaphoreType.DMA((2,))],
        compiler_params=GRANT,
        cost_estimate=cost(4),
        name="sent_terms",
    )(plan, mine, partners, out_weight)


def pick_weight(out_weight):
    stages, blocks = lax.axis_size("tp"), lax.axis_size("ctx")
    stage, place = lax.axis_index("tp"), lax.axis_index("ctx")
    chans = out_weight.shape[0]
    hops = jnp.where(place % 2 == 0, 1, stages - 1)
    corners = jnp.stack([place // 2, (stage + hops) % stages, place, (stage + 2) % stages])
    return weight_corners(corners.astype(jnp.int32), out_weight, blocks)


def turn_weight(parts):
    stages, blocks = lax.axis_size("tp"), lax.axis_size("ctx")
    found = []
    for part, static in zip(parts, ((1, stages - 1), (2, 2))):
        route = [
            (c * stages + k, c * stages + (k + static[c % 2]) % stages)
            for c in range(blocks)
            for k in range(stages)
        ]
        found.append(lax.ppermute(part, ("ctx", "tp"), route))
    return found


def corners_kernel(corners, weight, *refs):
    outs, sems = refs[:-1], refs[-1]
    copies = []
    for n, out in enumerate(outs):
        rows, chans = out.shape
        row = pl.multiple_of(corners[2 * n] * rows, rows)
        column = pl.multiple_of(corners[2 * n + 1] * chans, chans)
        source = weight.at[pl.ds(row, rows), pl.ds(column, chans)]
        copies.append(pltpu.make_async_copy(source, out, sems.at[n]))
        copies[-1].start()
    for copy in copies:
        copy.wait()


def weight_corners(corners, out_weight, blocks):
    chans = out_weight.shape[0]
    shapes = [(2 * chans // blocks, chans), (chans // blocks, chans)]
    return pl.pallas_call(
        corners_kernel,
        in_specs=[SMEM, HBM],
        out_specs=[VMEM] * 2,
        out_shape=[jax.ShapeDtypeStruct(shape, BF16) for shape in shapes],
        scratch_shapes=[pltpu.SemaphoreType.DMA((2,))],
        compiler_params=grant(56),
        name="weight_corners",
    )(corners, out_weight)


def swap_weight(part):
    devices = range(lax.axis_size("ctx"))
    return lax.ppermute(part, "ctx", [(i, i ^ (4 if i & 1 else 2)) for i in devices])


def swap_other(two):
    devices = range(lax.axis_size("ctx"))
    other = [(i, i ^ (2 if i & 1 else 4)) for i in devices]
    return [lax.ppermute(x, "ctx", other) for x in two]


def add_parts(order, data, parts, hops):
    chans = data.shape[1]
    if hops == 2:
        rows, row, chosen = chans // 8, chans // 4, range(8)
    else:
        rows, row, chosen = chans // 4, 0, range(4) if hops == 1 else range(4, 8)
    picked = []
    for q in chosen:
        index = order[q] if hops == 2 else order[q] // 2
        picked.append(data[:, pl.ds(pl.multiple_of(index * rows, rows), rows)])
    block = jnp.concatenate([parts[q][row : row + rows, :] for q in chosen], axis=0)
    return jnp.dot(jnp.concatenate(picked, axis=1), block, preferred_element_type=F32)


def early_kernel(order, mine, got0, got1, partner0, partner1, weight, *refs):
    parts, (out, own, first, own_weight, sem) = refs[:8], refs[8:]
    turn_count = order[8]
    rows, chans = got0.shape
    columns = pl.ds(pl.multiple_of(order[9] * chans, chans), chans)
    copy = pltpu.make_async_copy(weight.at[:, columns], own_weight, sem)
    copy.start()

    @pl.when(turn_count >= 2)
    def _():
        first[:rows, :] = got0[...]
        first[rows:, :] = partner0[...]

    @pl.when(turn_count < 2)
    def _():
        first[:rows, :] = got1[...]
        first[rows:, :] = partner1[...]

    @pl.when(turn_count >= 1)
    def _():
        out[...] = add_parts(order, first, parts, 1)

    @pl.when(turn_count < 1)
    def _():
        out[...] = jnp.zeros_like(out)

    @pl.when(turn_count == 3)
    def _():
        first[:rows, :] = got1[...]
        first[rows:, :] = partner1[...]
        out[...] += add_parts(order, first, parts, 2)

    copy.wait()
    out[:rows, :] += jnp.dot(mine[0], own_weight[...], preferred_element_type=F32)
    own[...] = jnp.dot(mine[1], own_weight[...], preferred_element_type=F32)


def early_sum(order, mine, arrivals, out_weight, weights):
    _, rows, chans = mine.shape
    whole = lambda shape: pl.BlockSpec(shape, lambda g, order: (0,) * len(shape))
    return pl.pallas_call(
        early_kernel,
        grid_spec=pltpu.PrefetchScalarGridSpec(
            num_scalar_prefetch=1,
            grid=(1,),
            in_specs=[whole(mine.shape)]
            + [whole((rows, chans))] * 4
            + [HBM]
            + [whole(x.shape) for x in weights],
            out_specs=[whole((2 * rows, chans)), whole((rows, chans))],
            scratch_shapes=[
                pltpu.VMEM((2 * rows, chans), BF16),
                pltpu.VMEM((chans, chans), BF16),
                pltpu.SemaphoreType.DMA,
            ],
        ),
        out_shape=[
            jax.ShapeDtypeStruct((2 * rows, chans), F32),
            jax.ShapeDtypeStruct((rows, chans), F32),
        ],
        compiler_params=grant(24),
        cost_estimate=cost(1),
        name="early_sum",
    )(order, mine, *arrivals, out_weight, *weights)


def late_sum(order, early, got2, got3, weights, total):
    behind = order[8]

    @pl.when(behind < 2)
    def _():
        total[...] = early[...]

    @pl.when(behind == 2)
    def _():
        total[...] = early[...] + add_parts(order, got2, weights, 2)

    @pl.when(behind == 3)
    def _():
        total[...] = early[...] + add_parts(order, got3, weights, 3)

    summed = jnp.where(behind == 3, got2[...].astype(F32), got3[...].astype(F32))
    return jnp.where(behind == 0, 0.0, summed)


def partner_kernel(order, early, got2, got3, *refs):
    weights, (out, total) = refs[:8], refs[8:]
    out[1] = late_sum(order, early, got2, got3, weights, total).astype(BF16)
    out[0] = total[...].astype(BF16)


def partner_sum(order, early, arrivals, weights):
    rows, chans = arrivals[0].shape
    whole = lambda shape: pl.BlockSpec(shape, lambda g, order: (0,) * len(shape))
    return pl.pallas_call(
        partner_kernel,
        grid_spec=pltpu.PrefetchScalarGridSpec(
            num_scalar_prefetch=1,
            grid=(1,),
            in_specs=[pl.BlockSpec((rows, chans), lambda g, order: (1, 0))]
            + [whole((rows, chans))] * 2
            + [whole(x.shape) for x in weights],
            out_specs=whole((2, rows, chans)),
            scratch_shapes=[pltpu.VMEM((rows, chans), F32)],
        ),
        out_shape=jax.ShapeDtypeStruct((2, rows, chans), BF16),
        compiler_params=grant(24),
        cost_estimate=cost(2),
        name="partner_sum",
    )(order, early, *arrivals, *weights)


def mine_kernel(order, early, own, got2, got3, *refs):
    weights, (out, total) = refs[:8], refs[8:]
    rows = early.shape[0]
    out[rows:, :] = late_sum(order, early, got2, got3, weights, total) + own[...]
    out[:rows, :] = total[...]


def mine_sum(order, early, own, arrivals, weights):
    rows, chans = arrivals[0].shape
    whole = lambda shape: pl.BlockSpec(shape, lambda g, order: (0,) * len(shape))
    return pl.pallas_call(
        mine_kernel,
        grid_spec=pltpu.PrefetchScalarGridSpec(
            num_scalar_prefetch=1,
            grid=(1,),
            in_specs=[pl.BlockSpec((rows, chans), lambda g, order: (0, 0))]
            + [whole((rows, chans))] * 3
            + [whole(x.shape) for x in weights],
            out_specs=whole((2 * rows, chans)),
            scratch_shapes=[pltpu.VMEM((rows, chans), F32)],
        ),
        out_shape=jax.ShapeDtypeStruct((2 * rows, chans), F32),
        compiler_params=grant(24),
        cost_estimate=cost(3),
        name="mine_sum",
    )(order, early, own, *arrivals, *weights)


def join_kernel(mine, partners, out):
    rows = partners.shape[1]
    for half in range(2):
        part = slice(half * rows, (half + 1) * rows)
        out[part, :] = (mine[part, :] + partners[half].astype(F32)).astype(BF16)


def join_sums(mine, partners):
    return pl.pallas_call(
        join_kernel,
        in_specs=[VMEM] * 2,
        out_specs=VMEM,
        out_shape=jax.ShapeDtypeStruct(mine.shape, BF16),
        compiler_params=GRANT,
        name="join_sums",
    )(mine, partners)


def weight_order():
    place, stage = lax.axis_index("ctx"), lax.axis_index("tp")
    up = place % 2 == 0
    last = lax.axis_size("tp") - 1
    a = jnp.where(up, 2, 4)
    masks = [0 * a, a, 6 - a, 0 * a + 6]
    swapped = [0 * a + 1, (6 - a) ^ 1, a ^ 1, 0 * a + 7]
    parts = [place ^ mask for mask in masks + swapped]
    return jnp.stack(parts + [jnp.where(up, stage, last - stage), stage]).astype(jnp.int32)


def project(spot, plan, order, convs, mixed, out_weight, weight_parts):
    stages, blocks = lax.axis_size("tp"), lax.axis_size("ctx")
    chans = out_weight.shape[0]
    far_weight = lax.dynamic_slice(out_weight, (0, spot[2] * chans), (chans, chans))
    mine, sent = gate_out(spot, convs, mixed, far_weight)
    route = []
    for c in range(blocks):
        for k in range(stages):
            to = k + (1 if c % 2 == 0 else -1)
            if 0 <= to < stages:
                route.append((c * stages + k, c * stages + to))
    onward = lambda x: lax.ppermute(x, ("ctx", "tp"), route)
    core_swap = lambda x: lax.ppermute(x, "ctx", [(i, i ^ 1) for i in range(blocks)])
    partners = core_swap(mine)
    partner_first = partner_sent(spot, partners, far_weight)
    got = [[onward(sent), onward(partner_first)]]
    terms = sent_terms(plan, mine, partners, out_weight)
    weight_part = after(jnp.concatenate(weight_parts), partner_first)
    weight_two = [weight_part, swap_weight(weight_part)]
    far_two = [core_swap(x) for x in weight_two]
    later = after(plan, far_two)
    steps = []
    for step in range(1, stages):
        row = []
        for chain, gated in enumerate((mine, partners)):
            row.append(next_step(later if chain and step == 3 else plan, step, chain, gated, terms, got[-1][chain]))
        steps.append(row)
        got.append([onward(x) for x in row])

    near_two = swap_other(weight_two)
    weights = weight_two + near_two + far_two
    weights += [core_swap(x) for x in after(near_two, steps[2][0])]
    arrivals = [got[0][0], got[1][0], got[0][1], got[1][1]]
    early, own = early_sum(order, mine, arrivals, out_weight, weights)
    theirs = partner_sum(after(order, got[3][0]), early, [got[2][1], got[3][1]], weights)
    ours = mine_sum(order, early, own, [got[2][0], got[3][0]], weights)
    return join_sums(ours, core_swap(theirs))


def fast_per_device(
    query_rows, key_rows, value_rows, short_weight, skip_gain, filter_taps, out_weight
):
    span, chans = query_rows.shape
    blocks, stages = lax.axis_size("ctx"), lax.axis_size("tp")
    lanes = chans // blocks
    length = span * blocks
    radix = 2 * length // SUB
    place, stage = lax.axis_index("ctx"), lax.axis_index("tp")
    me = place.astype(jnp.int32).reshape(1)
    up = place % 2 == 0
    behind = jnp.where(up, stage, stages - 1 - stage)
    far = jnp.where(up, stages - 1, 0)
    spot = jnp.stack([place, behind, far]).astype(jnp.int32)
    plan = lax.dynamic_index_in_dim(jnp.asarray(SENT), behind, keepdims=False)
    plan = jnp.where(up | (jnp.arange(5) < 3), plan, stages - 1 - plan)
    me, spot, plan, order = lax.optimization_barrier((me, spot, plan, weight_order()))
    skip = lax.dynamic_slice(skip_gain, (place * lanes,), (lanes,)).reshape(1, lanes)
    forward, inverse = (jnp.asarray(t) for t in dft_tables(2 * length))
    twiddle = jnp.asarray(twiddle_table(radix))
    devices = range(blocks)
    core_swap = lambda x: lax.ppermute(x, "ctx", [(i, i ^ 1) for i in devices])
    to_chips = lambda xs: [
        lax.ppermute(x, "ctx", [(i, i ^ (2 * q + 2)) for i in devices])
        for q, x in enumerate(xs)
    ]
    edges = passed_along(rims(query_rows, key_rows, value_rows), "ctx", 1)
    pairs = split_taps(after(me, edges), filter_taps, blocks // 2)
    pairs = [pairs[0]] + to_chips(pairs[1:])
    weight_parts = pick_weight(out_weight)
    stay, same, swap = gate_in(after(me, weight_parts), key_rows, value_rows, edges, short_weight, blocks)
    swapped = core_swap(swap)
    packed = pair_up(same, swapped)
    others = to_chips(packed)
    taps_swapped = core_swap(other_core(me, pairs))
    mixed = mix_query(query_rows, edges, short_weight)
    spectra = taps_spectra_of(me, pairs, taps_swapped, twiddle, forward)
    weight_parts = turn_weight(after(weight_parts, taps_swapped))
    conv = long_conv(me, stay, swapped, others, spectra, twiddle, forward, inverse, skip)
    stay, same, swap = spread(after(me, weight_parts), conv, blocks)
    swapped = core_swap(swap)
    convs = [stay, swapped] + to_chips(pair_up(same, swapped))
    return project(spot, plan, order, convs, mixed, out_weight, weight_parts)


def per_device(*arrays):
    span, chans = arrays[0].shape
    blocks = lax.axis_size("ctx")
    suits = blocks == 8 and lax.axis_size("tp") == 4 and span == 512 and chans == 8 * SUB
    return (fast_per_device if suits else general_per_device)(*arrays)


def solution(mesh):
    placed = (
        P("ctx", "tp"),
        P("ctx", "tp"),
        P("ctx", "tp"),
        P(None, None, "tp"),
        P("tp"),
        P("tp", "ctx"),
        P("tp", None),
    )
    return jax.shard_map(
        per_device, mesh=mesh, in_specs=placed, out_specs=P("ctx", "tp"), check_vma=False
    )
```
